32 devices in a mesh: fsdp: 2 (over x), ctx: 4 (over y, core), tp: 4 (over z).
Axes of the slice: x: 2, y: 2, z: 4, core: 2. Of those that a mesh axis runs over, the one named last changes fastest.
Arguments:
- tokens: bfloat16 [2048, 4, 1024], P(('ctx', 'tp'), 'fsdp'), may hold values from -6 to 6
- segment_ids: int32 [4, 2048], P('fsdp', 'ctx'), may hold values from 0 to 5, never falling along the last dimension, each value on 1 to 800 neighbouring positions
- decay_rate: float32 [8], P('tp'), may hold values from 0.0005 to 0.07
- w_query: float32 [1024, 1024], P(('fsdp', 'ctx'), 'tp'), may hold values from -0.1875 to 0.1875
- w_key: float32 [1024, 1024], P(('fsdp', 'ctx'), 'tp'), may hold values from -0.1875 to 0.1875
- w_value: float32 [1024, 1024], P(('fsdp', 'ctx'), 'tp'), may hold values from -0.1875 to 0.1875
- w_gate: float32 [1024, 1024], P(('fsdp', 'ctx'), 'tp'), may hold values from -0.1875 to 0.1875
- w_out: float32 [1024, 1024], P('tp', ('fsdp', 'ctx')), may hold values from -0.375 to 0.375
- glu_left: float32 [1024, 2816], P(('fsdp', 'ctx'), 'tp'), may hold values from -0.1875 to 0.1875
- glu_right: float32 [1024, 2816], P(('fsdp', 'ctx'), 'tp'), may hold values from -0.1875 to 0.1875
- glu_down: float32 [2816, 1024], P('tp', ('fsdp', 'ctx')), may hold values from -0.109375 to 0.109375
- cotangent: bfloat16 [2048, 4, 1024], P(('ctx', 'tp'), 'fsdp'), may hold values from -6 to 6
Outputs:
- output: bfloat16 [2048, 4, 1024], P(('ctx', 'tp'), 'fsdp')
- grad_tokens: float32 [2048, 4, 1024], P(('ctx', 'tp'), 'fsdp')
- grad_query: float32 [1024, 1024], P(('fsdp', 'ctx'), 'tp')
- grad_key: float32 [1024, 1024], P(('fsdp', 'ctx'), 'tp')
- grad_value: float32 [1024, 1024], P(('fsdp', 'ctx'), 'tp')
- grad_gate: float32 [1024, 1024], P(('fsdp', 'ctx'), 'tp')
- grad_out: float32 [1024, 1024], P('tp', ('fsdp', 'ctx'))
- grad_left: float32 [1024, 2816], P(('fsdp', 'ctx'), 'tp')
- grad_right: float32 [1024, 2816], P(('fsdp', 'ctx'), 'tp')
- grad_down: float32 [2816, 1024], P('tp', ('fsdp', 'ctx'))
The draws below stay inside these ranges and needn't reach their ends.
Inputs may be any that keep to these rules, and one draw needn't show every extreme that they name: `segment_ids`: along each sequence the document numbers never fall; every document has 1 to 800 tokens and one has exactly 800.
All inputs are finite; a program needn't handle non-finite values.
Results may differ from the reference program's by a relative error of at most 0.013.
Values may be sent and summed in bfloat16 or wider, within the bound.
A program may use at most 128 MiB of HBM per device.

```python
import math
import jax
import jax.numpy as jnp
import numpy as np
from jax import lax

D = 1024
H = 8
DH = 128
FF = 2816
SEQLEN = 2048
DOCS = 6
MOST_DOC = 800
LEN_DEV = 512
SEQS = 4
N_CTX = 4


def raised(entries, own_key, source, target, shards_of, factor):
    owner, partner = [(jnp.arange(entries.shape[axis_at]) // (entries.shape[axis_at] // shards_of)).reshape([-1 if axis == axis_at else 1 for axis in range(entries.ndim)]) for axis_at in (source, target)]
    chosen = jax.random.permutation(own_key, shards_of)[partner]
    strong = (owner == chosen) | (owner == (partner + shards_of // 2) % shards_of)
    return jnp.where(strong, factor * entries, entries)


def level_of(own_key, shape, shards, smallest, high):
    loudness, own = 1.0, jax.random.fold_in(own_key, 6)
    for dim, parts in shards:
        steps = jnp.exp(jax.random.uniform(jax.random.fold_in(own, dim), (parts,), jnp.float32, smallest / len(shards), high / len(shards)))
        loudness = loudness * jnp.repeat(steps, shape[dim] // parts).reshape([-1 if axis == dim else 1 for axis in range(len(shape))])
    return loudness


def profile(count, total, bound, skew):
    weights = [(1 << 20) // math.isqrt(grade ** skew) + 1 for grade in range(2, count + 1)]
    surplus, holding = total - bound - (count - 1), [1] * (count - 1)
    while surplus > 0:
        movable = [i for i in range(count - 1) if holding[i] < bound]
        pool, budget = sum([weights[i] for i in movable]), surplus
        for i in movable:
            extra = min(bound - holding[i], max(1, budget * weights[i] // pool), surplus)
            holding[i] = holding[i] + extra
            surplus = surplus - extra
    return np.array([bound] + holding)


def ragged_sizes(key, amount, total, bound, lean):
    if amount == 2:
        one = jax.random.randint(key, (), max(1, total - bound), min(bound, total - 1) + 1)
        return jnp.stack([one, total - one])
    tallies = jnp.asarray(profile(amount, total, bound, lean), jnp.int32)
    couples = (amount - 1) // 2
    giver, sink = tallies[1:1 + 2 * couples:2], tallies[2:2 + 2 * couples:2]
    slack = jnp.minimum(giver - 1, bound - sink)
    passed = jax.random.randint(jax.random.fold_in(key, 1), (couples,), 0, 1 << 20) % (slack + 1)
    tallies = tallies.at[1:1 + 2 * couples:2].set(giver - passed).at[2:2 + 2 * couples:2].set(sink + passed)
    return tallies[jax.random.permutation(jax.random.fold_in(key, 2), amount)]


def normal_values(key, dims, spread, reach, cuts=(), held_as=jnp.bfloat16):
    level = level_of(key, dims, cuts, -0.22, 0.18) if cuts else 1.0
    entries = jax.random.normal(key, dims, jnp.float32) * spread * level
    return jnp.minimum(jnp.maximum(entries, -reach), reach).astype(held_as)


def bell_draw_with(own_key, dims, width, limit, cuts, heavy, kind=jnp.bfloat16):
    result = width * jax.random.normal(own_key, dims, jnp.float32)
    if cuts:
        result = result * level_of(own_key, dims, cuts, -0.22, 0.18)
    return jnp.clip(raised(result, jax.random.fold_in(own_key, 3), *heavy), -limit, limit).astype(kind)


def setup_inputs(seed: int = 0) -> dict:
    streams_of = jax.random.split(jax.random.key(seed), 13)
    return {
        "tokens": bell_draw_with(streams_of[0], (SEQLEN, SEQS, D), 1.0, 6.0, ((0, 16), (1, 2)), (1, 2, 2, 2.0)),
        "segment_ids": jax.vmap(lambda own: jnp.searchsorted(jnp.cumsum(ragged_sizes(own, DOCS, SEQLEN, MOST_DOC, 0)), jnp.arange(SEQLEN), side="right"))(jax.random.split(streams_of[1], SEQS)).reshape((SEQS, SEQLEN)).astype(jnp.int32),
        "decay_rate": jnp.clip(jnp.exp(math.log(0.07) - 4.9416424 * jax.random.uniform(streams_of[2], (H,), jnp.float32) ** level_of(streams_of[2], (H,), ((0, 4),), -0.2, 0.2)), 0.0005, 0.07),
        "w_query": normal_values(streams_of[3], (D, D), D ** -0.5, 0.1875, ((0, 8), (1, 4)), jnp.float32),
        "w_key": normal_values(streams_of[4], (D, D), D ** -0.5, 0.1875, ((0, 8), (1, 4)), jnp.float32),
        "w_value": normal_values(streams_of[5], (D, D), D ** -0.5, 0.1875, ((0, 8), (1, 4)), jnp.float32),
        "w_gate": normal_values(streams_of[6], (D, D), D ** -0.5, 0.1875, ((0, 8), (1, 4)), jnp.float32),
        "w_out": normal_values(streams_of[7], (D, D), (D // 4) ** -0.5, 0.375, ((0, 4), (1, 8)), jnp.float32),
        "glu_left": normal_values(streams_of[8], (D, FF), D ** -0.5, 0.1875, ((0, 8), (1, 4)), jnp.float32),
        "glu_right": normal_values(streams_of[9], (D, FF), D ** -0.5, 0.1875, ((0, 8), (1, 4)), jnp.float32),
        "glu_down": normal_values(streams_of[10], (FF, D), FF ** -0.5, 0.109375, ((0, 4), (1, 8)), jnp.float32),
        "cotangent": bell_draw_with(streams_of[11], (SEQLEN, SEQS, D), 1.0, 6.0, ((0, 16), (1, 2)), (1, 2, 2, 2.0)),
    }


EPSILON = 1e-06
HEAD_FLOOR = 1.0
HIGHEST = lax.Precision.HIGHEST

@jax.custom_vjp
def low(v):
    return lax.optimization_barrier(v.astype(jnp.bfloat16)).astype(jnp.float32)

@jax.custom_vjp
def low_back(v):
    return v

def low_keep(v):
    return (low(v), None)

def low_pass(kept, grad):
    return (grad,)

def back_keep(v):
    return (v, None)

def back_low(kept, grad):
    return (low(grad),)
low.defvjp(low_keep, low_pass)
low_back.defvjp(back_keep, back_low)

def normalize(values, floor_value=EPSILON):
    return values * lax.rsqrt(lax.optimization_barrier(jnp.mean(values * values, axis=-1, keepdims=True)) + floor_value)

def matmul(left_in, right_in):
    return jnp.dot(left_in, right_in, precision=HIGHEST, preferred_element_type=jnp.float32)

def by_block(array_in):
    return array_in.reshape((N_CTX, LEN_DEV) + array_in.shape[1:])

def lightning(queries, keys, values, seg_row, decay_rate):
    seg_row = seg_row.astype(jnp.int32)
    position = jnp.arange(LEN_DEV).astype(jnp.float32)
    distance = position[:, None] - position[None, :]

    def block_step(carry, block_item):
        state, prior_last = carry
        block_query, block_key, block_value, block_seg = block_item
        scores = low_back(jnp.einsum('thd,shd->hts', block_query, block_key, precision=HIGHEST))
        same_doc = (block_seg[:, None] == block_seg[None, :]) & (distance >= 0.0)
        decay_grid = jnp.where(same_doc[None], jnp.exp(-decay_rate[:, None, None] * jnp.maximum(distance, 0.0)[None]), 0.0)
        weights = low(scores * decay_grid)
        inflow = jnp.where((block_seg == prior_last)[:, None], jnp.exp(-(position + 1.0)[:, None] * decay_rate[None, :]), 0.0)
        state_low = low(state)
        intra = jnp.einsum('hts,shd->thd', weights, block_value, precision=HIGHEST)
        inter = jnp.einsum('thd,hde->the', block_query, state_low, precision=HIGHEST) * inflow[:, :, None]
        attended = low_back(intra + inter)
        end_weight = jnp.where((block_seg == block_seg[-1])[:, None], jnp.exp(-(LEN_DEV - 1.0 - position)[:, None] * decay_rate[None, :]), 0.0)
        keys_end = low(block_key * end_weight[:, :, None])
        update = jnp.einsum('shd,she->hde', keys_end, block_value, precision=HIGHEST)
        carried = jnp.where((block_seg[0] == block_seg[-1]) & (block_seg[0] == prior_last), jnp.exp(-LEN_DEV * decay_rate), 0.0)
        new_state = (carried[:, None, None] * state + update).astype(jnp.float32)
        return ((new_state, block_seg[-1].astype(jnp.int32)), attended)
    initial = (jnp.zeros((H, DH, DH), jnp.float32), jnp.array(-1, jnp.int32))
    _, attended = lax.scan(jax.checkpoint(block_step), initial, (by_block(queries), by_block(keys), by_block(values), by_block(seg_row)))
    return attended.reshape(SEQLEN, H, DH)

def forward(tokens_seq, seg_row, decay_rate, w_query, w_key, w_value, w_gate, w_out, glu_left, glu_right, glu_down):
    normed = low(normalize(tokens_seq))
    proj_query = low_back(matmul(normed, low(w_query)))
    proj_key = low_back(matmul(normed, low(w_key)))
    proj_value = low_back(matmul(normed, low(w_value)))
    proj_gate = low_back(matmul(normed, low(w_gate)))
    head_shape = (SEQLEN, H, DH)
    queries = low(jax.nn.silu(proj_query)).reshape(head_shape)
    keys = low(jax.nn.silu(proj_key)).reshape(head_shape)
    values = low(proj_value).reshape(head_shape)
    attended = lightning(queries, keys, values, seg_row, decay_rate)
    attended_norm = normalize(attended, HEAD_FLOOR).reshape(SEQLEN, D)
    mixed_heads = low(attended_norm * jax.nn.sigmoid(proj_gate))
    residual = tokens_seq + low_back(matmul(mixed_heads, low(w_out)))
    second = low(normalize(residual))
    left_proj = low_back(matmul(second, low(glu_left)))
    right_proj = low_back(matmul(second, low(glu_right)))
    hidden = low(left_proj * right_proj)
    return residual + matmul(hidden, low(glu_down))

def reference(tokens, segment_ids, decay_rate, w_query, w_key, w_value, w_gate, w_out, glu_left, glu_right, glu_down, cotangent):
    masters = tuple((master.astype(jnp.float32) for master in (w_query, w_key, w_value, w_gate, w_out, glu_left, glu_right, glu_down)))
    rates = decay_rate.astype(jnp.float32)

    def per_sequence(totals, sequence_item):
        tokens_seq, seg_row, upstream = sequence_item

        def layer_call(inputs, wq_in, wk_in, wv_in, wg_in, wo_in, wl_in, wr_in, wd_in):
            return forward(inputs, seg_row, rates, wq_in, wk_in, wv_in, wg_in, wo_in, wl_in, wr_in, wd_in)
        output, pullback = jax.vjp(layer_call, tokens_seq.astype(jnp.float32), masters[0], masters[1], masters[2], masters[3], masters[4], masters[5], masters[6], masters[7])
        gradients = pullback(upstream.astype(jnp.float32).astype(output.dtype))
        totals = tuple(((accum + gradient.astype(jnp.float32)).astype(jnp.float32) for accum, gradient in zip(totals, gradients[1:])))
        return (totals, (output.astype(jnp.bfloat16), gradients[0].astype(jnp.float32)))
    zero_grads = tuple((jnp.zeros(master.shape, jnp.float32) for master in masters))
    totals, (outputs, grad_tokens) = lax.scan(per_sequence, zero_grads, (jnp.swapaxes(tokens, 0, 1), segment_ids.astype(jnp.int32), jnp.swapaxes(cotangent, 0, 1)))
    return (jnp.swapaxes(outputs, 0, 1), jnp.swapaxes(grad_tokens, 0, 1), totals[0], totals[1], totals[2], totals[3], totals[4], totals[5], totals[6], totals[7])
```

```python
import functools

import jax
import jax.numpy as jnp
from jax import lax
from jax.experimental import pallas as pl
from jax.experimental.pallas import tpu as pltpu
from jax.sharding import PartitionSpec as P

DH = 128
CH = 256
EPSILON = 1e-06
HEAD_FLOOR = 1.0
BF = jnp.bfloat16
F32 = jnp.float32
MESH = pl.DeviceIdType.MESH
MIB = 1 << 20


def dg(a, b, ca, cb):
    return lax.dot_general(a, b, (((ca,), (cb,)), ((), ())), preferred_element_type=F32)


def rows128(i):
    return pl.ds(pl.multiple_of(i * 128, 128), 128)


def inverse_norm(v, floor_value):
    return lax.rsqrt(jnp.mean(v * v, axis=-1, keepdims=True) + floor_value)


def norm_slope(v, d, floor_value):
    inv = inverse_norm(v, floor_value)
    inner = jnp.mean(d * v, axis=-1, keepdims=True)
    return inv * (d - v * (inner * inv * inv))


class Place:
    def __init__(self):
        x, k, z = lax.axis_index("fsdp"), lax.axis_index("ctx"), lax.axis_index("tp")
        self.x, self.k, self.z = x, k, z
        self.y, self.c = k // 2, k % 2
        self.t, self.zh = z % 2, z // 2
        self.r = x * 4 + k
        self.peer = {
            "X": (1 - x, k, z),
            "Y": (x, (k + 2) % 4, z),
            "C": (x, k + 1 - 2 * self.c, z),
            "P": (x, k, z + 1 - 2 * self.t),
            "Q": (x, k, (z + 2) % 4),
        }

    def flip(self, r, axis):
        if axis == "X":
            return (r + 4) % 8
        if axis == "Y":
            return r + 2 - 4 * ((r // 2) % 2)
        return r + 1 - 2 * (r % 2)

    def greet(self):
        bar = pltpu.get_barrier_semaphore()
        for peer in self.peer.values():
            pl.semaphore_signal(bar, inc=1, device_id=peer, device_id_type=MESH)

    def meet(self):
        pl.semaphore_wait(pltpu.get_barrier_semaphore(), len(self.peer))


class Links:
    def __init__(self, place, send, recv, local):
        self.place, self.send, self.recv, self.local = place, send, recv, local
        self.n = self.m = 0
        self.sent, self.kept = [], []

    def remote(self, src, dst, peer):
        cp = pltpu.make_async_remote_copy(
            src_ref=src,
            dst_ref=dst,
            send_sem=self.send.at[self.n],
            recv_sem=self.recv.at[self.n],
            device_id=self.place.peer[peer],
            device_id_type=MESH,
        )
        self.n += 1
        return cp

    def go(self, src, dst, peer):
        cp = self.remote(src, dst, peer)
        cp.start()
        self.sent.append(cp)
        return cp

    def keep(self, src, dst):
        cp = pltpu.make_async_copy(src, dst, self.local.at[self.m])
        self.m += 1
        cp.start()
        self.kept.append(cp)
        return cp

    def fetch(self, src, dst):
        cp = pltpu.make_async_copy(src, dst, self.local.at[self.m])
        self.m += 1
        cp.start()
        return cp

    def drain(self):
        for cp in self.sent:
            cp.wait_send()
        for cp in self.kept:
            cp.wait()


class Gather:
    def __init__(self, links, order, view, own=None):
        self.links, self.view = links, view
        pc = links.place
        self.pc, self.own = pc, own
        self.first, self.second = ("X", "Y") if order == "A" else ("Y", "X")
        self.rf = pc.flip(pc.r, self.first)
        self.rs = pc.flip(pc.r, self.second)
        self.rfs = pc.flip(self.rf, self.second)
        self.cps = [{}, {}]

    def put(self, slot, name, r, peer, src=None):
        b = self.pc.zh if slot == 0 else 1 - self.pc.zh
        src = self.view(b, r) if src is None else src
        self.cps[slot][name] = self.links.go(src, self.view(b, r), peer)

    def launch(self, slot, src=None):
        r = self.pc.r
        self.put(slot, "f", r, self.first, src)
        self.put(slot, "sa", r, self.second, src)
        self.put(slot, "c0", r, "C", src)

    def start(self):
        self.put(0, "z", self.pc.r, "Q", self.own)
        self.launch(0, self.own)

    def other(self):
        self.cps[0]["z"].wait_recv()
        self.launch(1)

    def step1(self, slot):
        self.cps[slot]["f"].wait_recv()
        self.put(slot, "sb", self.rf, self.second)
        self.put(slot, "c1", self.rf, "C")

    def step2(self, slot):
        self.cps[slot]["sa"].wait_recv()
        self.put(slot, "c2", self.rs, "C")
        self.cps[slot]["sb"].wait_recv()
        self.put(slot, "c3", self.rfs, "C")

    def step3(self, slot):
        for name in ("c0", "c1", "c2", "c3"):
            self.cps[slot][name].wait_recv()


def last_id(ids, kk, half, s):
    at = 255 + 256 * half
    return ids[kk, s : s + 1, at : at + 1]


def prior_id(pc, ids, s):
    before = jnp.where(pc.zh == 1, last_id(ids, pc.k, 0, s), last_id(ids, (pc.k + 3) % 4, 1, s))
    return jnp.where((pc.zh == 1) | (pc.k > 0), before, -1.0)


def same(a, b):
    return jnp.where(a == b, 1.0, 0.0)


def fill_decay(rate, grid, wend, gin):
    ti = lax.broadcasted_iota(jnp.int32, (CH, CH), 0).astype(F32)
    si = lax.broadcasted_iota(jnp.int32, (CH, CH), 1).astype(F32)
    dist = ti - si
    pos = lax.broadcasted_iota(jnp.int32, (CH, DH), 0).astype(F32)

    def head(h, _):
        lane = rate[h, 0:1, :]
        both = jnp.concatenate([lane, lane], axis=1)
        grid[h] = jnp.where(dist >= 0.0, jnp.exp(-both * jnp.maximum(dist, 0.0)), 0.0)
        wend[h] = jnp.exp(-lane * (CH - 1.0 - pos))
        gin[h] = jnp.exp(-lane * (pos + 1.0))
        return 0

    lax.fori_loop(0, 4, head, 0)


def fill_masks(pc, ids, mask, endf, inf):
    for s in range(2):
        row = ids[pc.k, s : s + 1, pl.ds(pl.multiple_of(pc.zh * CH, CH), CH)]
        along = jnp.broadcast_to(row, (CH, CH))
        down = along.T
        mask[s] = same(along, down)
        col = down[:, :DH]
        endf[s] = same(col, jnp.broadcast_to(row[:, CH - 1 : CH], (CH, DH)))
        inf[s] = same(col, jnp.broadcast_to(prior_id(pc, ids, s), (CH, DH)))


def attn_forward(
    rate_in, tok, cot, seg, wq, wk, wv, wg, wo_in, gl, gr, gd,
    n1_o, ct_o, n2_o, x1_o, proj_o, qkv_o, p_o, att_o, mix_o, sb_o, w_o, wo_o,
    gl_o, gr_o, gd_o, ids_o, rate_o,
    n1, ct, n2, x1, proj, qkv, pm, att, mix, sb, wb, wo, glb, grb, gdb,
    ids, rate, grid, wend, gin, mask, endf, inf, uf, us, ur, ts, tr, vs, vr, pf,
    br_s, br_r, send, recv, local,
):
    pc = Place()
    pc.greet()
    ln = Links(pc, send, recv, local)
    own, r = pc.zh, pc.r

    for i, w in enumerate((wk, wv, wq, wg)):
        wb[i, own, rows128(r), :] = w[...].astype(BF)
    ids[pc.k] = jnp.zeros((8, 512), F32)
    ids[pc.k, 0:2, :] = seg[...].astype(F32)
    for hh in range(2):
        rate[own * 2 + hh] = jnp.full((8, DH), rate_in[hh], F32)
    for s in range(2):
        xf = tok[s].astype(F32)
        n1[pl.ds(pl.multiple_of(s * CH + pc.t * 128, 128), 128), :] = (
            xf * inverse_norm(xf, EPSILON)
        ).astype(BF)
        ct[pl.ds(pl.multiple_of(s * CH + pc.t * 128, 128), 128), :] = cot[s]
    pc.meet()

    def mine(s):
        return pl.ds(pl.multiple_of(s * CH + pc.t * 128, 128), 128)

    def theirs(s):
        return pl.ds(pl.multiple_of(s * CH + (1 - pc.t) * 128, 128), 128)

    def wview(i):
        return lambda b, rr: wb.at[i, b, rows128(rr), :]

    qkvg = [Gather(ln, "AB"[i % 2], wview(i)) for i in range(4)]
    for g in qkvg:
        g.start()
    rate_cp = ln.go(rate.at[pl.ds(own * 2, 2)], rate.at[pl.ds(own * 2, 2)], "Q")
    ids_y = ln.go(ids.at[pc.k], ids.at[pc.k], "Y")
    ids_c = ln.go(ids.at[pc.k], ids.at[pc.k], "C")
    n1_cp = [ln.go(n1.at[mine(s)], n1.at[mine(s)], "P") for s in range(2)]

    wo[pl.ds(pl.multiple_of(own * 256, 256), 256), rows128(r)] = wo_in[...].astype(BF)
    glb[...] = gl[...].astype(BF)
    grb[...] = gr[...].astype(BF)
    gdb[...] = gd[...].astype(BF)

    kf = (pc.k + 2) % 4
    ids_y.wait_recv()
    ids_f = ln.go(ids.at[kf], ids.at[kf], "C")
    rate_cp.wait_recv()
    fill_decay(rate, grid, wend, gin)

    for g in qkvg:
        g.step1(0)
    for g in qkvg:
        g.other()
    ids_c.wait_recv()
    ids_f.wait_recv()
    fill_masks(pc, ids, mask, endf, inf)
    for g in qkvg:
        g.step2(0)
    for g in qkvg:
        g.step1(1)
    for g in qkvg:
        g.step3(0)
    for g in qkvg:
        g.step2(1)

    gather_o = Gather(ln, "A", lambda b, rr: wo.at[pl.ds(pl.multiple_of(b * 256, 256), 256), rows128(rr)])
    gather_l = Gather(ln, "A", lambda b, rr: gl_o.at[b, rows128(rr), :], glb)
    gather_r = Gather(ln, "B", lambda b, rr: gr_o.at[b, rows128(rr), :], grb)
    gather_d = Gather(ln, "A", lambda b, rr: gd_o.at[b, :, rows128(rr)], gdb)
    later = [gather_o, gather_l, gather_r, gather_d]
    for g in later:
        g.start()
    ln.keep(glb, gl_o.at[own, rows128(r), :])
    ln.keep(grb, gr_o.at[own, rows128(r), :])
    ln.keep(gdb, gd_o.at[own, :, rows128(r)])
    ct_cp = [ln.go(ct.at[mine(s)], ct.at[mine(s)], "P") for s in range(2)]
    for cp in n1_cp:
        cp.wait_recv()

    def project(i):
        def block(b, _):
            p = dg(n1[...], wb[i, b], 1, 0)
            for hh in range(2):
                h = b * 2 + hh
                part = p[:, hh * DH : (hh + 1) * DH]
                if i == 1:
                    qkv[1, h] = part.astype(BF)
                elif i == 3:
                    proj[2, h] = part
                else:
                    proj[i // 2, h] = part
                    qkv[i, h] = (part * jax.nn.sigmoid(part)).astype(BF)
            return 0

        lax.fori_loop(0, 2, block, 0)

    for i in range(4):
        qkvg[i].step3(1)
        project(i)
        if i == 1:
            for s in range(2):
                rs_ = pl.ds(s * CH, CH)

                def state(h, _):
                    kw = (qkv[0, h, rs_, :].astype(F32) * (wend[h] * endf[s])).astype(BF)
                    u = dg(kw, qkv[1, h, rs_, :], 0, 0)
                    uf[s, h] = u
                    us[s, h] = u.astype(BF)
                    return 0

                lax.fori_loop(0, 4, state, 0)
            u_cp = [ln.go(us.at[s], ur.at[s], "Q") for s in range(2)]
    for i in range(4):
        ln.keep(wb.at[i], w_o.at[i])
    ln.keep(n1, n1_o)
    ln.keep(proj, proj_o)
    ln.keep(qkv, qkv_o)
    ln.keep(ids, ids_o)
    ln.keep(rate, rate_o)
    for g in later:
        g.step1(0)

    for s in range(2):
        rs_ = pl.ds(s * CH, CH)

        def inside(h, _):
            sc = dg(qkv[2, h, rs_, :], qkv[0, h, rs_, :], 1, 1)
            p = (sc * grid[h] * mask[s]).astype(BF)
            pm[s, h] = p
            att[h, rs_, :] = dg(p, qkv[1, h, rs_, :], 1, 0)
            return 0

        lax.fori_loop(0, 4, inside, 0)
    ln.keep(pm, p_o)
    for g in later:
        g.other()

    t_cp, v_cp = [], []
    for s in range(2):
        u_cp[s].wait_recv()
        fl = same(last_id(ids, pc.k, 0, s), last_id(ids, pc.k, 1, s))

        def pair(h, _):
            lane = jnp.exp(-CH * rate[h, 0:1, :]) * fl
            got = ur[s, h].astype(F32)
            wo_ = jnp.where(pc.zh == 1, jnp.ones_like(lane), lane)
            wr_ = jnp.where(pc.zh == 1, lane, jnp.ones_like(lane))
            tot = wo_ * uf[s, h] + wr_ * got
            pf[s, h] = jnp.where(pc.zh == 1, got, jnp.zeros_like(got))
            uf[s, h] = tot
            ts[s, h] = tot.astype(BF)
            return 0

        lax.fori_loop(0, 4, pair, 0)
        t_cp.append(ln.go(ts.at[s], tr.at[s], "C"))
    for g in later:
        g.step2(0)
    for s in range(2):
        t_cp[s].wait_recv()
        prior = prior_id(pc, ids, s)
        low = last_id(ids, pc.y * 2, 1, s)
        fl = same(low, last_id(ids, pc.y * 2 + 1, 1, s))
        fp = same(low, prior) * jnp.where(pc.c == 1, 1.0, 0.0)

        def quad(h, _):
            one = rate[h, 0:1, :]
            lane = jnp.exp(-2.0 * CH * one) * fl
            got = tr[s, h].astype(F32)
            wo_ = jnp.where(pc.c == 1, jnp.ones_like(lane), lane)
            wr_ = jnp.where(pc.c == 1, lane, jnp.ones_like(lane))
            vs[s, h] = (wo_ * uf[s, h] + wr_ * got).astype(BF)
            pf[s, h] = pf[s, h] + (jnp.exp(-(CH * 1.0) * pc.zh.astype(F32) * one) * fp) * got
            return 0

        lax.fori_loop(0, 4, quad, 0)
        v_cp.append(ln.go(vs.at[s], vr.at[s], "Y"))
    for g in later:
        g.step1(1)
    for s in range(2):
        v_cp[s].wait_recv()
        fp = same(last_id(ids, 1, 1, s), prior_id(pc, ids, s)) * jnp.where(pc.y == 1, 1.0, 0.0)
        far = (2 * pc.c + pc.zh).astype(F32) * CH
        rs_ = pl.ds(s * CH, CH)

        def enter(h, _):
            got = vr[s, h].astype(F32)
            st = pf[s, h] + (jnp.exp(-far * rate[h, 0:1, :]) * fp) * got
            low_st = st.astype(BF)
            sb[s, h] = low_st
            o = att[h, rs_, :] + (gin[h] * inf[s]) * dg(qkv[2, h, rs_, :], low_st, 1, 0)
            att[h, rs_, :] = o
            on = o * inverse_norm(o, HEAD_FLOOR)
            mix[rs_, rows128(h)] = (on * jax.nn.sigmoid(proj[2, h, rs_, :])).astype(BF)
            return 0

        lax.fori_loop(0, 4, enter, 0)
        if s == 0:
            gather_o.step3(0)
            gather_o.step2(1)
            gather_o.step3(1)
            b_cp = []
        br_s[s] = dg(mix[theirs(s), :], wo[...], 1, 0).astype(BF)
        b_cp.append(ln.go(br_s.at[s], br_r.at[s], "P"))
        x1[s] = tok[s].astype(F32) + dg(mix[mine(s), :], wo[...], 1, 0)
    ln.keep(att, att_o)
    ln.keep(mix, mix_o)
    ln.keep(sb, sb_o)
    ln.keep(wo, wo_o)
    n2_cp = []
    for s in range(2):
        b_cp[s].wait_recv()
        v = x1[s] + br_r[s].astype(F32)
        x1[s] = v
        n2[mine(s), :] = (v * inverse_norm(v, EPSILON)).astype(BF)
        n2_cp.append(ln.go(n2.at[mine(s)], n2.at[mine(s)], "P"))
    ln.keep(x1, x1_o)
    for g in later[1:]:
        g.step2(1)
    for g in later[1:]:
        g.step3(0)
        g.step3(1)
    for cp in ct_cp:
        cp.wait_recv()
    ln.keep(ct, ct_o)
    for cp in n2_cp:
        cp.wait_recv()
    ln.keep(n2, n2_o)
    ln.drain()


def call_forward(rate, tok, cot, seg, ws, wo, gl, gr, gd):
    sd = jax.ShapeDtypeStruct
    ff = gl.shape[1]
    vm = pltpu.VMEM
    outs = [
        sd((512, 1024), BF),
        sd((512, 1024), BF),
        sd((512, 1024), BF),
        sd((2, 128, 1024), F32),
        sd((3, 4, 512, DH), F32),
        sd((3, 4, 512, DH), BF),
        sd((2, 4, CH, CH), BF),
        sd((4, 512, DH), F32),
        sd((512, 512), BF),
        sd((2, 4, DH, DH), BF),
        sd((4, 2, 1024, 256), BF),
        sd((512, 1024), BF),
        sd((2, 1024, ff), BF),
        sd((2, 1024, ff), BF),
        sd((2, ff, 1024), BF),
        sd((4, 8, 512), F32),
        sd((4, 8, DH), F32),
    ]
    scratch = [
        vm((512, 1024), BF), vm((512, 1024), BF), vm((512, 1024), BF), vm((2, 128, 1024), F32),
        vm((3, 4, 512, DH), F32), vm((3, 4, 512, DH), BF), vm((2, 4, CH, CH), BF),
        vm((4, 512, DH), F32), vm((512, 512), BF), vm((2, 4, DH, DH), BF),
        vm((4, 2, 1024, 256), BF), vm((512, 1024), BF),
        vm((128, ff), BF), vm((128, ff), BF), vm((ff, 128), BF),
        vm((4, 8, 512), F32), vm((4, 8, DH), F32),
        vm((4, CH, CH), F32), vm((4, CH, DH), F32), vm((4, CH, DH), F32),
        vm((2, CH, CH), F32), vm((2, CH, DH), F32), vm((2, CH, DH), F32),
        vm((2, 4, DH, DH), F32), vm((2, 4, DH, DH), BF), vm((2, 4, DH, DH), BF),
        vm((2, 4, DH, DH), BF), vm((2, 4, DH, DH), BF), vm((2, 4, DH, DH), BF), vm((2, 4, DH, DH), BF),
        vm((2, 4, DH, DH), F32),
        vm((2, 128, 1024), BF), vm((2, 128, 1024), BF),
        pltpu.SemaphoreType.DMA((144,)), pltpu.SemaphoreType.DMA((144,)), pltpu.SemaphoreType.DMA((24,)),
    ]
    vin = pl.BlockSpec(memory_space=pltpu.VMEM)
    return pl.pallas_call(
        attn_forward,
        out_shape=outs,
        in_specs=[pl.BlockSpec(memory_space=pltpu.SMEM)] + [vin] * 11,
        out_specs=[pl.BlockSpec(memory_space=pl.ANY)] * len(outs),
        scratch_shapes=scratch,
        compiler_params=pltpu.CompilerParams(
            collective_id=0, has_side_effects=True, vmem_limit_bytes=60 * MIB
        ),
        name="attention_forward",
    )(rate, tok, cot, seg, *ws, wo, gl, gr, gd)


class Scatter:
    def __init__(self, links, order, kind, bufs):
        self.links, self.kind = links, kind
        pc = links.place
        self.pc = pc
        self.acc, self.sc, self.rc, self.sf, self.rf, self.ss, self.rs, self.sz, self.rz, self.tile = bufs
        if order == "A":
            self.first, self.second, self.fv, self.sv = "X", "Y", pc.x, pc.y
            self.at = lambda f, m: 2 * f + m
        else:
            self.first, self.second, self.fv, self.sv = "Y", "X", pc.y, pc.x
            self.at = lambda f, m: 2 * m + f
        self.c_cp, self.f_cp, self.s_cp = {}, {}, {}

    def part(self, half):
        return self.tile[rows128(half), :] if self.kind == "rows" else self.tile[:, rows128(half)]

    def core_stage(self, b, product):
        def pair(i, _):
            self.tile[...] = product(b, i)
            self.sc[b, i] = self.part(1 - self.pc.c).astype(BF)
            self.acc[b, i] = self.part(self.pc.c)
            return 0

        lax.fori_loop(0, 4, pair, 0)
        self.c_cp[b] = self.links.go(self.sc.at[b], self.rc.at[b], "C")

    def first_stage(self, b):
        self.c_cp[b].wait_recv()
        for m in range(2):
            away, here = self.at(1 - self.fv, m), self.at(self.fv, m)
            self.sf[b, m] = (self.acc[b, away] + self.rc[b, away].astype(F32)).astype(BF)
        self.f_cp[b] = self.links.go(self.sf.at[b], self.rf.at[b], self.first)
        for m in range(2):
            here = self.at(self.fv, m)
            self.acc[b, here] = self.acc[b, here] + self.rc[b, here].astype(F32)

    def second_stage(self, b):
        self.f_cp[b].wait_recv()
        away, here = self.at(self.fv, 1 - self.sv), self.at(self.fv, self.sv)
        self.ss[b] = (self.acc[b, away] + self.rf[b, 1 - self.sv].astype(F32)).astype(BF)
        self.s_cp[b] = self.links.go(self.ss.at[b], self.rs.at[b], self.second)
        self.acc[b, here] = self.acc[b, here] + self.rf[b, self.sv].astype(F32)

    def plane_stage(self):
        here = self.at(self.fv, self.sv)
        away = 1 - self.pc.zh
        for b in range(2):
            self.s_cp[b].wait_recv()
        self.sz[...] = (self.acc[away, here] + self.rs[away].astype(F32)).astype(BF)
        self.z_cp = self.links.go(self.sz, self.rz, "Q")

    def total(self):
        here = self.at(self.fv, self.sv)
        zh = self.pc.zh
        self.z_cp.wait_recv()
        return self.acc[zh, here] + self.rs[zh].astype(F32) + self.rz[...].astype(F32)


def scatter_bufs(slab, tile):
    vm = pltpu.VMEM
    return [
        vm((2, 4) + slab, F32), vm((2, 4) + slab, BF), vm((2, 4) + slab, BF),
        vm((2, 2) + slab, BF), vm((2, 2) + slab, BF), vm((2,) + slab, BF), vm((2,) + slab, BF),
        vm(slab, BF), vm(slab, BF), vm(tile, F32),
    ]


def cols256(i):
    return pl.ds(pl.multiple_of(i * 256, 256), 256)


def glu(
    n2_i, ct_i, x1_i, gl_i, gr_i, gd_i,
    dr_o, dx1_o, fs_o, fo_o, dpr_o, gdown_o, gleft_o,
    n2, ct, x1, gl, gr, gd, hid, dpl, dpr, tmp, dsend, drecv, dx1, dr, fs, fo, gdown, gleft,
    *rest,
):
    down_b, left_b = rest[:10], rest[10:20]
    send, recv, local = rest[20:]
    pc = Place()
    pc.greet()
    ln = Links(pc, send, recv, local)
    got = {}
    got["n2"] = ln.fetch(n2_i, n2)
    got["gl"] = ln.fetch(gl_i, gl)
    got["gr"] = ln.fetch(gr_i, gr)
    got["ct"] = ln.fetch(ct_i, ct)
    got["gd"] = ln.fetch(gd_i, gd)
    got["x1"] = ln.fetch(x1_i, x1)
    pc.meet()

    def mine(s):
        return pl.ds(pl.multiple_of(s * CH + pc.t * 128, 128), 128)

    for name in ("n2", "gl", "gr", "ct", "gd"):
        got[name].wait()
    d_cp = []
    for s in range(2):
        rs_ = pl.ds(s * CH, CH)

        def block(b, _):
            a = dg(n2[rs_, :], gl[b], 1, 0)
            c = dg(n2[rs_, :], gr[b], 1, 0)
            hid[b, rs_, :] = (a * c).astype(BF)
            dh = dg(ct[rs_, :], gd[b], 1, 1)
            dpl[b, rs_, :] = (dh * c).astype(BF)
            dpr[b, rs_, :] = (dh * a).astype(BF)
            return 0

        lax.fori_loop(0, 2, block, 0)
        tmp[...] = (
            dg(dpl[0, rs_, :], gl[0], 1, 1) + dg(dpr[0, rs_, :], gr[0], 1, 1)
            + dg(dpl[1, rs_, :], gl[1], 1, 1) + dg(dpr[1, rs_, :], gr[1], 1, 1)
        )
        dsend[s] = tmp[rows128(1 - pc.t), :].astype(BF)
        d_cp.append(ln.go(dsend.at[s], drecv.at[s], "P"))
        dx1[s] = tmp[rows128(pc.t), :]

    down = Scatter(ln, "A", "cols", down_b)
    left = Scatter(ln, "B", "rows", left_b)
    for b in range(2):
        down.core_stage(b, lambda b, i: dg(hid[b], ct[:, cols256(i)], 0, 0))
    got["x1"].wait()
    r_cp = []

    def turn(s):
        d_cp[s].wait_recv()
        v = x1[s]
        dn = dx1[s] + drecv[s].astype(F32)
        g = ct[mine(s), :].astype(F32) + norm_slope(v, dn, EPSILON)
        dx1[s] = g
        dr[mine(s), :] = g.astype(BF)
        r_cp.append(ln.go(dr.at[mine(s)], dr.at[mine(s)], "P"))

    turn(0)
    for b in range(2):
        down.first_stage(b)
    for b in range(2):
        left.core_stage(b, lambda b, i: dg(n2[:, cols256(i)], dpl[b], 0, 0))
    turn(1)
    ln.keep(dx1, dx1_o)
    ln.keep(dpr, dpr_o)
    for s in range(2):
        rs_ = pl.ds(s * CH, CH)
        tmp[...] = dg(hid[0, rs_, :], gd[0], 1, 0) + dg(hid[1, rs_, :], gd[1], 1, 0)
        fs[s] = tmp[rows128(1 - pc.t), :].astype(BF)
        fo[s] = x1[s] + tmp[rows128(pc.t), :]
    ln.keep(fs, fs_o)
    ln.keep(fo, fo_o)
    for b in range(2):
        down.second_stage(b)
    for b in range(2):
        left.first_stage(b)
    down.plane_stage()
    for b in range(2):
        left.second_stage(b)
    left.plane_stage()
    for cp in r_cp:
        cp.wait_recv()
    ln.keep(dr, dr_o)
    gdown[...] = down.total()
    ln.keep(gdown, gdown_o)
    gleft[...] = left.total()
    ln.keep(gleft, gleft_o)
    ln.drain()


def call_glu(n2, ct, x1, gl, gr, gd):
    sd, vm = jax.ShapeDtypeStruct, pltpu.VMEM
    ff = gl.shape[2]
    outs = [
        sd((512, 1024), BF), sd((2, 128, 1024), F32), sd((2, 128, 1024), BF),
        sd((2, 128, 1024), F32), sd((2, 512, ff), BF), sd((ff, 128), F32), sd((128, ff), F32),
    ]
    scratch = [
        vm((512, 1024), BF), vm((512, 1024), BF), vm((2, 128, 1024), F32),
        vm((2, 1024, ff), BF), vm((2, 1024, ff), BF), vm((2, ff, 1024), BF),
        vm((2, 512, ff), BF), vm((2, 512, ff), BF), vm((2, 512, ff), BF),
        vm((CH, 1024), F32), vm((2, 128, 1024), BF), vm((2, 128, 1024), BF),
        vm((2, 128, 1024), F32), vm((512, 1024), BF), vm((2, 128, 1024), BF),
        vm((2, 128, 1024), F32), vm((ff, 128), F32), vm((128, ff), F32),
        *scatter_bufs((ff, 128), (ff, 256)), *scatter_bufs((128, ff), (256, ff)),
        pltpu.SemaphoreType.DMA((24,)), pltpu.SemaphoreType.DMA((24,)), pltpu.SemaphoreType.DMA((24,)),
    ]
    return pl.pallas_call(
        glu,
        out_shape=outs,
        in_specs=[pl.BlockSpec(memory_space=pl.ANY)] * 6,
        out_specs=[pl.BlockSpec(memory_space=pl.ANY)] * len(outs),
        scratch_shapes=scratch,
        compiler_params=pltpu.CompilerParams(
            collective_id=1, has_side_effects=True, vmem_limit_bytes=62 * MIB
        ),
        name="glu",
    )(n2, ct, x1, gl, gr, gd)


def silu_slope(v):
    g = jax.nn.sigmoid(v)
    return g * (1.0 + v * (1.0 - g))


N_BACK_IN = 18


def attn_backward(*refs):
    ins, refs = refs[:N_BACK_IN], refs[N_BACK_IN:]
    outs, refs = refs[:8], refs[8:]
    bufs, refs = refs[:N_BACK_IN], refs[N_BACK_IN:]
    out_o, gtok_o, gq_o, gk_o, gv_o, gg_o, go_o, gr_o = outs
    (dr, dx1, n1, n2, dpr, mix, wo, wb, proj, qkv, pm, att, sb, ids, rate, fs, fo, x) = bufs
    (
        grid, wend, gin, mask, endf, inf, dm, dob, dp, dki, dvi, vf, vs, vr, ts, tr, ws, wr, rf, du,
        tmp, nsend, nrecv, frecv, outb, gtok, gw, gout, gright,
    ) = refs[:29]
    refs = refs[29:]
    sc_bufs = [refs[10 * i : 10 * i + 10] for i in range(6)]
    send, recv, local = refs[60:]
    pc = Place()
    pc.greet()
    ln = Links(pc, send, recv, local)
    got = [ln.fetch(a, b) for a, b in zip(ins, bufs)]
    pc.meet()
    for cp in got:
        cp.wait()
    f_cp = ln.go(fs, frecv, "P")
    fill_decay(rate, grid, wend, gin)
    fill_masks(pc, ids, mask, endf, inf)

    def mine(s):
        return pl.ds(pl.multiple_of(s * CH + pc.t * 128, 128), 128)

    def through(b, _):
        dm[:, cols256(b)] = dg(dr[...], wo[cols256(b), :], 1, 1)
        return 0

    lax.fori_loop(0, 2, through, 0)
    v_cp = []
    for s in range(2):
        rs_ = pl.ds(s * CH, CH)

        def outer(h, _):
            d, o = dm[rs_, rows128(h)], att[h, rs_, :]
            g = jax.nn.sigmoid(proj[2, h, rs_, :])
            inv = inverse_norm(o, HEAD_FLOOR)
            dp[3, rs_, rows128(h)] = (d * (o * inv) * g * (1.0 - g)).astype(BF)
            e = d * g
            inner = jnp.mean(e * o, axis=-1, keepdims=True)
            do = (inv * (e - o * (inner * inv * inv))).astype(BF)
            dob[h, rs_, :] = do
            gq = (qkv[2, h, rs_, :].astype(F32) * (gin[h] * inf[s])).astype(BF)
            v = dg(gq, do, 0, 0)
            vf[s, h] = v
            vs[s, h] = v.astype(BF)
            return 0

        lax.fori_loop(0, 4, outer, 0)
        v_cp.append(ln.go(vs.at[s], vr.at[s], "Q"))

    right = Scatter(ln, "A", "rows", sc_bufs[0])
    s_out = Scatter(ln, "B", "cols", sc_bufs[1])
    s_w = [Scatter(ln, "AB"[i % 2], "rows", sc_bufs[2 + i]) for i in range(4)]

    def product(i):
        return lambda b, j: dg(n1[:, cols256(j)], dp[i, :, cols256(b)], 0, 0)

    for b in range(2):
        right.core_stage(b, lambda b, i: dg(n2[:, cols256(i)], dpr[b], 0, 0))
    for b in range(2):
        right.first_stage(b)

    for s in range(2):
        rs_ = pl.ds(s * CH, CH)

        def inside(h, _):
            do, q, k = dob[h, rs_, :], qkv[2, h, rs_, :], qkv[0, h, rs_, :]
            dsc = (dg(do, qkv[1, h, rs_, :], 1, 1) * grid[h] * mask[s]).astype(BF)
            dq = dg(dsc, k, 1, 0) + (gin[h] * inf[s]) * dg(do, sb[s, h], 1, 1)
            dp[2, rs_, rows128(h)] = (dq * silu_slope(proj[1, h, rs_, :])).astype(BF)
            dki[h, rs_, :] = dg(dsc, q, 0, 0)
            dvi[h, rs_, :] = dg(pm[s, h], do, 0, 0)
            return 0

        lax.fori_loop(0, 4, inside, 0)

    for b in range(2):
        s_out.core_stage(b, lambda b, i: dg(mix[:, cols256(b)], dr[:, cols256(i)], 0, 0))
    for i in (3, 2):
        for b in range(2):
            s_w[i].core_stage(b, product(i))
    for b in range(2):
        right.second_stage(b)
        s_out.first_stage(b)

    t_cp, w_cp = [], []
    for s in range(2):
        v_cp[s].wait_recv()
        before = jnp.where(pc.k > 0, last_id(ids, (pc.k + 3) % 4, 1, s), -1.0)
        fb = same(before, last_id(ids, pc.k, 0, s))

        def pair(h, _):
            lane = jnp.exp(-CH * rate[h, 0:1, :]) * fb
            g = vr[s, h].astype(F32)
            wo_ = jnp.where(pc.zh == 0, jnp.ones_like(lane), lane)
            wr_ = jnp.where(pc.zh == 0, lane, jnp.ones_like(lane))
            tot = wo_ * vf[s, h] + wr_ * g
            rf[s, h] = jnp.where(pc.zh == 0, g, jnp.zeros_like(g))
            vf[s, h] = tot
            ts[s, h] = tot.astype(BF)
            return 0

        lax.fori_loop(0, 4, pair, 0)
        t_cp.append(ln.go(ts.at[s], tr.at[s], "C"))
    for i in (3, 2):
        for b in range(2):
            s_w[i].first_stage(b)
    for s in range(2):
        t_cp[s].wait_recv()
        low = last_id(ids, pc.y * 2, 1, s)
        before = jnp.where(pc.y > 0, last_id(ids, (pc.y * 2 + 3) % 4, 1, s), -1.0)
        fb = same(before, low)
        here = jnp.where(pc.zh == 1, last_id(ids, pc.k, 1, s), last_id(ids, pc.k, 0, s))
        fp = same(here, low) * jnp.where(pc.c == 0, 1.0, 0.0)
        far = (1 - pc.zh).astype(F32) * CH

        def quad(h, _):
            one = rate[h, 0:1, :]
            lane = jnp.exp(-2.0 * CH * one) * fb
            g = tr[s, h].astype(F32)
            wo_ = jnp.where(pc.c == 0, jnp.ones_like(lane), lane)
            wr_ = jnp.where(pc.c == 0, lane, jnp.ones_like(lane))
            ws[s, h] = (wo_ * vf[s, h] + wr_ * g).astype(BF)
            rf[s, h] = rf[s, h] + (jnp.exp(-far * one) * fp) * g
            return 0

        lax.fori_loop(0, 4, quad, 0)
        w_cp.append(ln.go(ws.at[s], wr.at[s], "Y"))
    for b in range(2):
        s_out.second_stage(b)
    n_cp = []
    for s in range(2):
        w_cp[s].wait_recv()
        here = jnp.where(pc.zh == 1, last_id(ids, pc.k, 1, s), last_id(ids, pc.k, 0, s))
        fp = same(here, last_id(ids, 1, 1, s)) * jnp.where(pc.y == 0, 1.0, 0.0)
        far = (2 * (1 - pc.c) + (1 - pc.zh)).astype(F32) * CH
        rs_ = pl.ds(s * CH, CH)

        def close(h, _):
            d = (rf[s, h] + (jnp.exp(-far * rate[h, 0:1, :]) * fp) * wr[s, h].astype(F32)).astype(BF)
            k, v = qkv[0, h, rs_, :], qkv[1, h, rs_, :]
            w = wend[h] * endf[s]
            kw = (k.astype(F32) * w).astype(BF)
            dp[1, rs_, rows128(h)] = (dvi[h, rs_, :] + dg(kw, d, 1, 0)).astype(BF)
            dk = dki[h, rs_, :] + w * dg(v, d, 1, 1)
            dp[0, rs_, rows128(h)] = (dk * silu_slope(proj[0, h, rs_, :])).astype(BF)
            return 0

        lax.fori_loop(0, 4, close, 0)
        acc = None
        for i in range(4):
            for b in range(2):
                p = dg(dp[i, rs_, b * 256 : (b + 1) * 256], wb[i, b], 1, 1)
                acc = p if acc is None else acc + p
        tmp[...] = acc
        nsend[s] = tmp[rows128(1 - pc.t), :].astype(BF)
        n_cp.append(ln.go(nsend.at[s], nrecv.at[s], "P"))
        gtok[s] = tmp[rows128(pc.t), :]
    for i in (0, 1):
        for b in range(2):
            s_w[i].core_stage(b, product(i))
    for i in (3, 2):
        for b in range(2):
            s_w[i].second_stage(b)
    right.plane_stage()
    s_out.plane_stage()
    for i in (0, 1):
        for b in range(2):
            s_w[i].first_stage(b)
    for i in (3, 2):
        s_w[i].plane_stage()
    f_cp.wait_recv()
    outb[...] = (fo[...] + frecv[...].astype(F32)).astype(BF)
    ln.keep(outb, out_o)
    for s in range(2):
        n_cp[s].wait_recv()
        dn = gtok[s] + nrecv[s].astype(F32)
        gtok[s] = dx1[s] + norm_slope(x[s].astype(F32), dn, EPSILON)
    ln.keep(gtok, gtok_o)
    for i in (0, 1):
        for b in range(2):
            s_w[i].second_stage(b)
    gright[...] = right.total()
    ln.keep(gright, gr_o)
    for i in (0, 1):
        s_w[i].plane_stage()
    gout[...] = s_out.total()
    ln.keep(gout, go_o)
    for i, o in ((3, gg_o), (2, gq_o), (0, gk_o), (1, gv_o)):
        gw[i] = s_w[i].total()
        ln.keep(gw.at[i], o)
    ln.drain()


def call_backward(*args):
    sd, vm = jax.ShapeDtypeStruct, pltpu.VMEM
    ff = args[4].shape[2]
    outs = [
        sd((2, 128, 1024), BF), sd((2, 128, 1024), F32),
        sd((128, 256), F32), sd((128, 256), F32), sd((128, 256), F32), sd((128, 256), F32),
        sd((256, 128), F32), sd((128, ff), F32),
    ]
    st = (2, 4, DH, DH)
    scratch = [vm(a.shape, a.dtype) for a in args] + [
        vm((4, CH, CH), F32), vm((4, CH, DH), F32), vm((4, CH, DH), F32),
        vm((2, CH, CH), F32), vm((2, CH, DH), F32), vm((2, CH, DH), F32),
        vm((512, 512), F32), vm((4, 512, DH), BF), vm((4, 512, 512), BF),
        vm((4, 512, DH), F32), vm((4, 512, DH), F32),
        vm(st, F32), vm(st, BF), vm(st, BF), vm(st, BF), vm(st, BF), vm(st, BF), vm(st, BF),
        vm(st, F32), vm((8, 128), BF),
        vm((CH, 1024), F32), vm((2, 128, 1024), BF), vm((2, 128, 1024), BF), vm((2, 128, 1024), BF),
        vm((2, 128, 1024), BF), vm((2, 128, 1024), F32), vm((4, 128, 256), F32),
        vm((256, 128), F32), vm((128, ff), F32),
        *scatter_bufs((128, ff), (256, ff)), *scatter_bufs((256, 128), (256, 256)),
        *scatter_bufs((128, 256), (256, 256)), *scatter_bufs((128, 256), (256, 256)),
        *scatter_bufs((128, 256), (256, 256)), *scatter_bufs((128, 256), (256, 256)),
        pltpu.SemaphoreType.DMA((64,)), pltpu.SemaphoreType.DMA((64,)), pltpu.SemaphoreType.DMA((40,)),
    ]
    return pl.pallas_call(
        attn_backward,
        out_shape=outs,
        in_specs=[pl.BlockSpec(memory_space=pl.ANY)] * len(args),
        out_specs=[pl.BlockSpec(memory_space=pl.ANY)] * len(outs),
        scratch_shapes=scratch,
        compiler_params=pltpu.CompilerParams(
            collective_id=2, has_side_effects=True, vmem_limit_bytes=63 * MIB
        ),
        name="attention_backward",
    )(*args)


def entering(x, axis, join, neutral):
    place = lax.axis_index(axis)
    gathered = jax.tree.map(
        lambda a, kind: lax.all_gather(a.astype(kind), axis),
        x,
        (jnp.bfloat16, jnp.bfloat16, jnp.bfloat16, jnp.bfloat16),
    )
    state = jax.tree.map(lambda a, e: jnp.zeros_like(a) + jnp.asarray(e, a.dtype), x, neutral)

    def one(lap, state):
        return join(
            state,
            jax.tree.map(
                lambda a, own: lax.dynamic_index_in_dim(a, lap, 0, False).astype(own.dtype),
                gathered,
                x,
            ),
        )

    return lax.fori_loop(0, place, one, state)


def entering_2(x, axis, join, neutral):
    count = lax.axis_size(axis)
    place = lax.axis_index(axis)
    ahead = count - 1 - place
    gathered = jax.tree.map(
        lambda a, kind: lax.all_gather(a.astype(kind), axis), x, (jnp.bfloat16, jnp.bfloat16)
    )
    state = jax.tree.map(lambda a, e: jnp.zeros_like(a) + jnp.asarray(e, a.dtype), x, neutral)

    def one(lap, state):
        source = count - 1 - lap
        return join(
            state,
            jax.tree.map(
                lambda a, own: lax.dynamic_index_in_dim(a, source, 0, False).astype(own.dtype),
                gathered,
                x,
            ),
        )

    return lax.fori_loop(0, ahead, one, state)


def normalize(values, floor_value=EPSILON):
    return values * lax.rsqrt(jnp.mean(values * values, axis=-1, keepdims=True) + floor_value)


def norm_backward(values, upstream, floor_value=EPSILON):
    inverse = lax.rsqrt(jnp.mean(values * values, axis=-1, keepdims=True) + floor_value)
    inner_mean = jnp.mean(upstream * values, axis=-1, keepdims=True)
    return inverse * (upstream - values * inner_mean * inverse * inverse)


def silu_grad(values):
    sigmoid_value = jax.nn.sigmoid(values)
    return sigmoid_value * (1.0 + values * (1.0 - sigmoid_value))


def chain_forward(earlier, later):
    early_first, early_last, early_decay, early_state = earlier
    late_first, late_last, late_decay, late_state = later
    linked = (late_first == early_last) | (early_last < 0.0) | (late_first < 0.0)
    carried = jnp.where(linked[:, None], late_decay, 0.0)
    first_seg = jnp.where(early_first < 0.0, late_first, early_first)
    last_seg = jnp.where(late_last < 0.0, early_last, late_last)
    return (
        first_seg,
        last_seg,
        early_decay * carried,
        late_state + carried[:, :, None, None] * early_state,
    )


def chain_backward(earlier, later):
    return (earlier[0] * later[0], later[1] + later[0][:, :, None, None] * earlier[1])


def shards(
    tokens,
    segment_ids,
    decay_rate,
    w_query,
    w_key,
    w_value,
    w_gate,
    w_out,
    glu_left,
    glu_right,
    glu_down,
    cotangent,
):
    shard_len, seq_count, model_width = tokens.shape
    tok_float = tokens.astype(jnp.float32)
    normed_part = normalize(tok_float).astype(jnp.bfloat16)
    gathered = (
        lax.all_gather(w_query.astype(jnp.bfloat16), ("fsdp", "ctx"), axis=0, tiled=True),
        lax.all_gather(w_key.astype(jnp.bfloat16), ("fsdp", "ctx"), axis=0, tiled=True),
        lax.all_gather(w_value.astype(jnp.bfloat16), ("fsdp", "ctx"), axis=0, tiled=True),
        lax.all_gather(w_gate.astype(jnp.bfloat16), ("fsdp", "ctx"), axis=0, tiled=True),
        lax.all_gather(w_out.astype(jnp.bfloat16), ("fsdp", "ctx"), axis=1, tiled=True),
        lax.all_gather(glu_left.astype(jnp.bfloat16), ("fsdp", "ctx"), axis=0, tiled=True),
        lax.all_gather(glu_right.astype(jnp.bfloat16), ("fsdp", "ctx"), axis=0, tiled=True),
        lax.all_gather(glu_down.astype(jnp.bfloat16), ("fsdp", "ctx"), axis=1, tiled=True),
    )
    full_query, full_key, full_value, full_gate, full_out, full_left, full_right, full_down = (
        gathered
    )
    normed = lax.all_gather(normed_part, "tp", axis=0, tiled=True)
    block_len = normed.shape[0]
    total_rows = block_len * seq_count
    normed_flat = normed.reshape(total_rows, model_width)
    local_width = full_query.shape[1]
    head_count = local_width // DH
    head_shape = (block_len, seq_count, head_count, DH)
    proj_query = jnp.dot(normed_flat, full_query, preferred_element_type=jnp.float32)
    proj_key = jnp.dot(normed_flat, full_key, preferred_element_type=jnp.float32)
    proj_value = jnp.dot(normed_flat, full_value, preferred_element_type=jnp.float32)
    proj_gate = jnp.dot(normed_flat, full_gate, preferred_element_type=jnp.float32)
    queries = jax.nn.silu(proj_query).astype(jnp.bfloat16).reshape(head_shape)
    keys_low = jax.nn.silu(proj_key).astype(jnp.bfloat16).reshape(head_shape)
    values_low = proj_value.astype(jnp.bfloat16).reshape(head_shape)
    seg_pos = segment_ids.T
    seg_float = seg_pos.astype(jnp.float32)
    position = jnp.arange(block_len).astype(jnp.float32)
    distance = position[:, None] - position[None, :]
    same_doc = (segment_ids[:, :, None] == segment_ids[:, None, :]) & (distance >= 0.0)[None]
    decay_grid = jnp.where(
        same_doc[:, None],
        jnp.exp(-decay_rate[None, :, None, None] * jnp.maximum(distance, 0.0)[None, None]),
        0.0,
    )
    end_weight = jnp.where(
        (seg_pos == seg_pos[-1:])[:, :, None],
        jnp.exp(-(block_len - 1.0 - position)[:, None, None] * decay_rate[None, None, :]),
        0.0,
    )
    keys_end = (keys_low.astype(jnp.float32) * end_weight[..., None]).astype(jnp.bfloat16)
    update = jnp.einsum("tbhd,tbhe->bhde", keys_end, values_low, preferred_element_type=jnp.float32)
    first_seg = seg_float[0]
    last_seg = seg_float[-1]
    span_decay = jnp.where(
        (first_seg == last_seg)[:, None], jnp.exp(-block_len * decay_rate)[None, :], 0.0
    )
    identity = (
        -jnp.ones((seq_count,), jnp.float32),
        -jnp.ones((seq_count,), jnp.float32),
        jnp.ones((seq_count, head_count), jnp.float32),
        jnp.zeros((seq_count, head_count, DH, DH), jnp.float32),
    )
    scanned = entering((first_seg, last_seg, span_decay, update), "ctx", chain_forward, identity)
    prior_last = scanned[1]
    state_low = scanned[3].astype(jnp.bfloat16)
    inflow = jnp.where(
        (seg_pos == prior_last[None, :])[:, :, None],
        jnp.exp(-(position + 1.0)[:, None, None] * decay_rate[None, None, :]),
        0.0,
    )
    scores = jnp.einsum("tbhd,sbhd->bhts", queries, keys_low, preferred_element_type=jnp.float32)
    weights_low = (scores * decay_grid).astype(jnp.bfloat16)
    intra = jnp.einsum(
        "bhts,sbhd->tbhd", weights_low, values_low, preferred_element_type=jnp.float32
    )
    inter = (
        jnp.einsum("tbhd,bhde->tbhe", queries, state_low, preferred_element_type=jnp.float32)
        * inflow[..., None]
    )
    attended = intra + inter
    attended_norm = normalize(attended, HEAD_FLOOR)
    gate_value = jax.nn.sigmoid(proj_gate).reshape(head_shape)
    mixed_heads = (
        (attended_norm * gate_value).astype(jnp.bfloat16).reshape(block_len, seq_count, local_width)
    )
    row_count = shard_len * lax.axis_size("tp")
    piece_rows = mixed_heads.reshape(row_count * seq_count, local_width)
    branch = lax.psum_scatter(
        jnp.dot(piece_rows, full_out, preferred_element_type=jnp.float32).reshape(
            row_count, seq_count, model_width
        ),
        "tp",
        scatter_dimension=0,
        tiled=True,
    )
    residual = tok_float + branch
    second_part = normalize(residual).astype(jnp.bfloat16)
    second = lax.all_gather(second_part, "tp", axis=0, tiled=True)
    second_flat = second.reshape(total_rows, model_width)
    left_proj = jnp.dot(second_flat, full_left, preferred_element_type=jnp.float32)
    right_proj = jnp.dot(second_flat, full_right, preferred_element_type=jnp.float32)
    hidden = (left_proj * right_proj).astype(jnp.bfloat16)
    ffn_width = hidden.shape[1]
    hidden_blocks = hidden.reshape(block_len, seq_count, ffn_width)
    row_count = shard_len * lax.axis_size("tp")
    piece_rows = hidden_blocks.reshape(row_count * seq_count, ffn_width)
    ffn_branch = lax.psum_scatter(
        jnp.dot(piece_rows, full_down, preferred_element_type=jnp.float32)
        .reshape(row_count, seq_count, model_width)
        .astype(jnp.bfloat16),
        "tp",
        scatter_dimension=0,
        tiled=True,
    ).astype(jnp.float32)
    output = (residual + ffn_branch).astype(jnp.bfloat16)
    upstream = lax.all_gather(cotangent, "tp", axis=0, tiled=True).reshape(total_rows, model_width)
    grad_down = jnp.dot(hidden.T, upstream, preferred_element_type=jnp.float32)
    grad_hidden = jnp.dot(upstream, full_down.T, preferred_element_type=jnp.float32)
    grad_left_proj = (grad_hidden * right_proj).astype(jnp.bfloat16)
    grad_right_proj = (grad_hidden * left_proj).astype(jnp.bfloat16)
    grad_left = jnp.dot(second_flat.T, grad_left_proj, preferred_element_type=jnp.float32)
    grad_right = jnp.dot(second_flat.T, grad_right_proj, preferred_element_type=jnp.float32)
    left_blocks = grad_left_proj.reshape(block_len, seq_count, ffn_width)
    right_blocks = grad_right_proj.reshape(block_len, seq_count, ffn_width)
    row_count = shard_len * lax.axis_size("tp")
    left_rows = left_blocks.reshape(row_count * seq_count, ffn_width)
    right_rows = right_blocks.reshape(row_count * seq_count, ffn_width)
    summed = jnp.dot(left_rows, full_left.T, preferred_element_type=jnp.float32) + jnp.dot(
        right_rows, full_right.T, preferred_element_type=jnp.float32
    )
    grad_second = lax.psum_scatter(
        summed.reshape(row_count, seq_count, model_width), "tp", scatter_dimension=0, tiled=True
    )
    grad_residual = cotangent.astype(jnp.float32) + norm_backward(residual, grad_second)
    branch_low = grad_residual.astype(jnp.bfloat16)
    grad_branch = lax.all_gather(branch_low, "tp", axis=0, tiled=True).reshape(
        total_rows, model_width
    )
    grad_wout = jnp.dot(
        mixed_heads.reshape(total_rows, local_width).T,
        grad_branch,
        preferred_element_type=jnp.float32,
    )
    grad_mixed = jnp.dot(grad_branch, full_out.T, preferred_element_type=jnp.float32).reshape(
        head_shape
    )
    grad_gate_proj = (
        (grad_mixed * attended_norm * gate_value * (1.0 - gate_value))
        .astype(jnp.bfloat16)
        .reshape(total_rows, local_width)
    )
    grad_attended = norm_backward(attended, grad_mixed * gate_value, HEAD_FLOOR).astype(
        jnp.bfloat16
    )
    grad_weights = jnp.einsum(
        "tbhd,sbhd->bhts", grad_attended, values_low, preferred_element_type=jnp.float32
    )
    grad_scores = (grad_weights * decay_grid).astype(jnp.bfloat16)
    grad_queries = jnp.einsum(
        "bhts,sbhd->tbhd", grad_scores, keys_low, preferred_element_type=jnp.float32
    )
    grad_queries = (
        grad_queries
        + jnp.einsum(
            "tbhe,bhde->tbhd", grad_attended, state_low, preferred_element_type=jnp.float32
        )
        * inflow[..., None]
    )
    grad_keys = jnp.einsum(
        "bhts,tbhd->sbhd", grad_scores, queries, preferred_element_type=jnp.float32
    )
    grad_values = jnp.einsum(
        "bhts,tbhd->sbhd", weights_low, grad_attended, preferred_element_type=jnp.float32
    )
    weighted_queries = queries.astype(jnp.float32) * inflow[..., None]
    grad_prior_local = jnp.einsum(
        "tbhd,tbhe->bhde", weighted_queries, grad_attended.astype(jnp.float32), precision=lax.Precision.HIGHEST
    )
    link_decay = jnp.where((first_seg == prior_last)[:, None], span_decay, 0.0)
    back_identity = (
        jnp.ones((seq_count, head_count), jnp.float32),
        jnp.zeros((seq_count, head_count, DH, DH), jnp.float32),
    )
    grad_update = entering_2((link_decay, grad_prior_local), "ctx", chain_backward, back_identity)[
        1
    ]
    grad_values = grad_values + jnp.einsum(
        "tbhd,bhde->tbhe", keys_end.astype(jnp.float32), grad_update, precision=lax.Precision.HIGHEST
    )
    grad_keys = (
        grad_keys
        + jnp.einsum(
            "tbhe,bhde->tbhd", values_low.astype(jnp.float32), grad_update, precision=lax.Precision.HIGHEST
        )
        * end_weight[..., None]
    )
    grad_query_proj = (
        (grad_queries * silu_grad(proj_query).reshape(head_shape))
        .astype(jnp.bfloat16)
        .reshape(total_rows, local_width)
    )
    grad_key_proj = (
        (grad_keys * silu_grad(proj_key).reshape(head_shape))
        .astype(jnp.bfloat16)
        .reshape(total_rows, local_width)
    )
    grad_value_proj = grad_values.astype(jnp.bfloat16).reshape(total_rows, local_width)
    grad_wquery = jnp.dot(normed_flat.T, grad_query_proj, preferred_element_type=jnp.float32)
    grad_wkey = jnp.dot(normed_flat.T, grad_key_proj, preferred_element_type=jnp.float32)
    grad_wvalue = jnp.dot(normed_flat.T, grad_value_proj, preferred_element_type=jnp.float32)
    grad_wgate = jnp.dot(normed_flat.T, grad_gate_proj, preferred_element_type=jnp.float32)
    query_blocks = grad_query_proj.reshape(block_len, seq_count, local_width)
    key_blocks = grad_key_proj.reshape(block_len, seq_count, local_width)
    value_blocks = grad_value_proj.reshape(block_len, seq_count, local_width)
    gate_blocks = grad_gate_proj.reshape(block_len, seq_count, local_width)
    row_count = shard_len * lax.axis_size("tp")
    summed = jnp.zeros((row_count * seq_count, model_width), jnp.float32)
    for grad_blocks, weight_full in (
        (query_blocks, full_query),
        (key_blocks, full_key),
        (value_blocks, full_value),
        (gate_blocks, full_gate),
    ):
        piece_rows = grad_blocks.reshape(row_count * seq_count, local_width)
        summed = summed + jnp.dot(piece_rows, weight_full.T, preferred_element_type=jnp.float32)
    grad_normed = lax.psum_scatter(
        summed.reshape(row_count, seq_count, model_width).astype(jnp.bfloat16),
        "tp",
        scatter_dimension=0,
        tiled=True,
    ).astype(jnp.float32)
    grad_tokens = grad_residual + norm_backward(tok_float, grad_normed)
    every_grad = (
        lax.psum_scatter(grad_wquery, ("fsdp", "ctx"), scatter_dimension=0, tiled=True),
        lax.psum_scatter(grad_wkey, ("fsdp", "ctx"), scatter_dimension=0, tiled=True),
        lax.psum_scatter(grad_wvalue, ("fsdp", "ctx"), scatter_dimension=0, tiled=True),
        lax.psum_scatter(grad_wgate, ("fsdp", "ctx"), scatter_dimension=0, tiled=True),
        lax.psum_scatter(grad_wout, ("fsdp", "ctx"), scatter_dimension=1, tiled=True),
        lax.psum_scatter(grad_left, ("fsdp", "ctx"), scatter_dimension=0, tiled=True),
        lax.psum_scatter(grad_right, ("fsdp", "ctx"), scatter_dimension=0, tiled=True),
        lax.psum_scatter(grad_down, ("fsdp", "ctx"), scatter_dimension=1, tiled=True),
    )
    return (
        output,
        grad_tokens,
        every_grad[0],
        every_grad[1],
        every_grad[2],
        every_grad[3],
        every_grad[4],
        every_grad[5],
        every_grad[6],
        every_grad[7],
    )


def paired(
    tokens, segment_ids, decay_rate, w_query, w_key, w_value, w_gate, w_out,
    glu_left, glu_right, glu_down, cotangent,
):
    tok, cot = tokens.transpose(1, 0, 2), cotangent.transpose(1, 0, 2)
    (
        n1, ct, n2, x1, proj, qkv, pm, att, mix, sb, wb, wo, gl, gr, gd, ids, rate,
    ) = call_forward(
        decay_rate, tok, cot, segment_ids, (w_query, w_key, w_value, w_gate), w_out,
        glu_left, glu_right, glu_down,
    )
    dr, dx1, fs, fo, dpr, g_down, g_left = call_glu(n2, ct, x1, gl, gr, gd)
    out, g_tok, g_q, g_k, g_v, g_g, g_o, g_right = call_backward(
        dr, dx1, n1, n2, dpr, mix, wo, wb, proj, qkv, pm, att, sb, ids, rate, fs, fo, tok
    )
    return (
        out.transpose(1, 0, 2), g_tok.transpose(1, 0, 2),
        g_q, g_k, g_v, g_g, g_o, g_left, g_right, g_down,
    )


def solution(mesh):
    in_specs = (
        P(("ctx", "tp"), "fsdp", None),
        P("fsdp", "ctx"),
        P("tp"),
        P(("fsdp", "ctx"), "tp"),
        P(("fsdp", "ctx"), "tp"),
        P(("fsdp", "ctx"), "tp"),
        P(("fsdp", "ctx"), "tp"),
        P("tp", ("fsdp", "ctx")),
        P(("fsdp", "ctx"), "tp"),
        P(("fsdp", "ctx"), "tp"),
        P("tp", ("fsdp", "ctx")),
        P(("ctx", "tp"), "fsdp", None),
    )
    out_specs = (
        P(("ctx", "tp"), "fsdp", None),
        P(("ctx", "tp"), "fsdp", None),
        P(("fsdp", "ctx"), "tp"),
        P(("fsdp", "ctx"), "tp"),
        P(("fsdp", "ctx"), "tp"),
        P(("fsdp", "ctx"), "tp"),
        P("tp", ("fsdp", "ctx")),
        P(("fsdp", "ctx"), "tp"),
        P(("fsdp", "ctx"), "tp"),
        P("tp", ("fsdp", "ctx")),
    )
    sizes = tuple(mesh.shape[a] for a in ("fsdp", "ctx", "tp"))
    body = paired if sizes == (2, 4, 4) else shards
    return jax.shard_map(body, mesh=mesh, in_specs=in_specs, out_specs=out_specs, check_vma=False)
```

```python
import functools

import jax
import jax.numpy as jnp
from jax import lax
from jax.experimental import pallas as pl
from jax.experimental.pallas import tpu as pltpu
from jax.sharding import PartitionSpec as P

DH = 128
CH = 256
EPSILON = 1e-06
HEAD_FLOOR = 1.0
BF = jnp.bfloat16
F32 = jnp.float32
MESH = pl.DeviceIdType.MESH
MIB = 1 << 20


def dg(a, b, ca, cb):
    return lax.dot_general(a, b, (((ca,), (cb,)), ((), ())), preferred_element_type=F32)


def rows128(i):
    return pl.ds(pl.multiple_of(i * 128, 128), 128)


def cols256(i):
    return pl.ds(pl.multiple_of(i * 256, 256), 256)


def inverse_norm(v, floor_value):
    return lax.rsqrt(jnp.mean(v * v, axis=-1, keepdims=True) + floor_value)


def norm_slope(v, d, floor_value):
    inv = inverse_norm(v, floor_value)
    inner = jnp.mean(d * v, axis=-1, keepdims=True)
    return inv * (d - v * (inner * inv * inv))


class Place:
    def __init__(self):
        x, k, z = lax.axis_index("fsdp"), lax.axis_index("ctx"), lax.axis_index("tp")
        self.x, self.k, self.z = x, k, z
        self.y, self.c = k // 2, k % 2
        self.t, self.zh = z % 2, z // 2
        self.r = x * 4 + k
        self.peer = {
            "X": (1 - x, k, z),
            "Y": (x, (k + 2) % 4, z),
            "C": (x, k + 1 - 2 * self.c, z),
            "P": (x, k, z + 1 - 2 * self.t),
            "Q": (x, k, (z + 2) % 4),
        }

    def flip(self, r, axis):
        if axis == "X":
            return (r + 4) % 8
        if axis == "Y":
            return r + 2 - 4 * ((r // 2) % 2)
        return r + 1 - 2 * (r % 2)

    def greet(self):
        bar = pltpu.get_barrier_semaphore()
        for peer in self.peer.values():
            pl.semaphore_signal(bar, inc=1, device_id=peer, device_id_type=MESH)

    def meet(self):
        pl.semaphore_wait(pltpu.get_barrier_semaphore(), len(self.peer))


class Links:
    def __init__(self, place, send, recv, local):
        self.place, self.send, self.recv, self.local = place, send, recv, local
        self.n = self.m = 0
        self.sent, self.kept = [], []

    def remote(self, src, dst, peer):
        cp = pltpu.make_async_remote_copy(
            src_ref=src,
            dst_ref=dst,
            send_sem=self.send.at[self.n],
            recv_sem=self.recv.at[self.n],
            device_id=self.place.peer[peer],
            device_id_type=MESH,
        )
        self.n += 1
        return cp

    def go(self, src, dst, peer):
        cp = self.remote(src, dst, peer)
        cp.start()
        self.sent.append(cp)
        return cp

    def keep(self, src, dst):
        cp = pltpu.make_async_copy(src, dst, self.local.at[self.m])
        self.m += 1
        cp.start()
        self.kept.append(cp)
        return cp

    def fetch(self, src, dst):
        cp = pltpu.make_async_copy(src, dst, self.local.at[self.m])
        self.m += 1
        cp.start()
        return cp

    def gone(self, cp):
        cp.wait_send()
        self.sent = [other for other in self.sent if other is not cp]

    def written(self, cp):
        cp.wait()
        self.kept = [other for other in self.kept if other is not cp]

    def drain(self):
        for cp in self.sent:
            cp.wait_send()
        for cp in self.kept:
            cp.wait()


class Gather:
    def __init__(self, links, order, view, own=None):
        self.links, self.view = links, view
        pc = links.place
        self.pc, self.own = pc, own
        self.first, self.second = ("X", "Y") if order == "A" else ("Y", "X")
        self.rf = pc.flip(pc.r, self.first)
        self.rs = pc.flip(pc.r, self.second)
        self.rfs = pc.flip(self.rf, self.second)
        self.cps = [{}, {}]

    def put(self, slot, name, r, peer, src=None):
        b = self.pc.zh if slot == 0 else 1 - self.pc.zh
        src = self.view(b, r) if src is None else src
        self.cps[slot][name] = self.links.go(src, self.view(b, r), peer)

    def launch(self, slot, src=None):
        r = self.pc.r
        self.put(slot, "f", r, self.first, src)
        self.put(slot, "sa", r, self.second, src)
        self.put(slot, "c0", r, "C", src)

    def cross(self):
        self.put(0, "z", self.pc.r, "Q", self.own)

    def start(self):
        self.launch(0, self.own)
        self.cross()

    def other(self):
        self.cps[0]["z"].wait_recv()
        self.launch(1)

    def step1(self, slot):
        self.cps[slot]["f"].wait_recv()
        self.put(slot, "sb", self.rf, self.second)
        self.put(slot, "c1", self.rf, "C")

    def step2(self, slot):
        self.cps[slot]["sa"].wait_recv()
        self.put(slot, "c2", self.rs, "C")
        self.cps[slot]["sb"].wait_recv()
        self.put(slot, "c3", self.rfs, "C")

    def step3(self, slot):
        for name in ("c0", "c1", "c2", "c3"):
            self.cps[slot][name].wait_recv()


def last_id(ids, kk, half, s):
    at = 255 + 256 * half
    return ids[kk, s : s + 1, at : at + 1]


def prior_id(pc, ids, s):
    before = jnp.where(pc.zh == 1, last_id(ids, pc.k, 0, s), last_id(ids, (pc.k + 3) % 4, 1, s))
    return jnp.where((pc.zh == 1) | (pc.k > 0), before, -1.0)


def same(a, b):
    return jnp.where(a == b, 1.0, 0.0)


def fill_decay(rate, grid, wend, gin):
    ti = lax.broadcasted_iota(jnp.int32, (CH, CH), 0).astype(F32)
    si = lax.broadcasted_iota(jnp.int32, (CH, CH), 1).astype(F32)
    dist = ti - si
    pos = lax.broadcasted_iota(jnp.int32, (CH, DH), 0).astype(F32)

    def head(h, _):
        lane = rate[h, 0:1, :]
        both = jnp.concatenate([lane, lane], axis=1)
        grid[h] = jnp.where(dist >= 0.0, jnp.exp(-both * jnp.maximum(dist, 0.0)), 0.0)
        wend[h] = jnp.exp(-lane * (CH - 1.0 - pos))
        gin[h] = jnp.exp(-lane * (pos + 1.0))
        return 0

    lax.fori_loop(0, 4, head, 0)


def fill_masks(pc, ids, mask, endf, inf):
    for s in range(2):
        row = ids[pc.k, s : s + 1, pl.ds(pl.multiple_of(pc.zh * CH, CH), CH)]
        along = jnp.broadcast_to(row, (CH, CH))
        down = along.T
        mask[s] = same(along, down)
        col = down[:, :DH]
        endf[s] = same(col, jnp.broadcast_to(row[:, CH - 1 : CH], (CH, DH)))
        inf[s] = same(col, jnp.broadcast_to(prior_id(pc, ids, s), (CH, DH)))


class Scatter:
    def __init__(self, links, kind, bufs):
        self.links, self.kind = links, kind
        pc = links.place
        self.pc = pc
        self.acc, self.sc, self.rc, self.sf, self.rf, self.ss, self.rs, self.sz, self.rz = bufs
        self.c_cp, self.f_cp, self.s_cp = {}, {}, {}
        self.last = 2 * pc.x + pc.y

    def way(self, b):
        x, y = self.pc.x, self.pc.y
        if b == 0:
            return "X", "Y", x, y, lambda f, m: 2 * f + m
        return "Y", "X", y, x, lambda f, m: 2 * m + f

    def core_stage(self, b, product, after=None):
        if after is not None:
            self.links.gone(after.c_cp[b])

        def pair(i, _):
            p = product(b, i)
            lo, hi = (p[:128], p[128:]) if self.kind == "rows" else (p[:, :128], p[:, 128:])
            self.sc[b, i] = jnp.where(self.pc.c == 0, hi, lo).astype(BF)
            self.acc[b, i] = jnp.where(self.pc.c == 0, lo, hi).astype(self.acc.dtype)
            return 0

        lax.fori_loop(0, 4, pair, 0)
        self.c_cp[b] = self.links.go(self.sc.at[b], self.rc.at[b], "C")

    def add(self, b, i, got):
        return self.acc[b, i].astype(F32) + got.astype(F32)

    def first_stage(self, b, joined=False):
        first, _, fv, _, at = self.way(b)
        if not joined:
            self.c_cp[b].wait_recv()
        for m in range(2):
            i = at(1 - fv, m)
            self.sf[b, m] = (self.acc[b, i] if joined else self.add(b, i, self.rc[b, i])).astype(BF)
        self.f_cp[b] = self.links.go(self.sf.at[b], self.rf.at[b], first)
        if not joined:
            for m in range(2):
                i = at(fv, m)
                self.acc[b, i] = self.add(b, i, self.rc[b, i]).astype(self.acc.dtype)

    def join(self, b):
        self.c_cp[b].wait_recv()
        for i in range(4):
            self.acc[b, i] = self.add(b, i, self.rc[b, i]).astype(self.acc.dtype)

    def second_stage(self, b):
        _, second, fv, sv, at = self.way(b)
        self.f_cp[b].wait_recv()
        self.ss[b] = self.add(b, at(fv, 1 - sv), self.rf[b, 1 - sv]).astype(BF)
        self.s_cp[b] = self.links.go(self.ss.at[b], self.rs.at[b], second)
        self.acc[b, self.last] = self.add(b, self.last, self.rf[b, sv]).astype(self.acc.dtype)

    def plane_stage(self):
        away = 1 - self.pc.zh
        for b in range(2):
            self.s_cp[b].wait_recv()
        self.sz[...] = self.add(away, self.last, self.rs[away]).astype(BF)
        self.z_cp = self.links.go(self.sz, self.rz, "Q")

    def total(self):
        zh = self.pc.zh
        self.z_cp.wait_recv()
        return self.add(zh, self.last, self.rs[zh]) + self.rz[...].astype(F32)


def scatter_bufs(slab, acc=F32, core=2):
    vm = pltpu.VMEM
    return [vm((2, 4) + slab, acc)] + [vm((2, 4) + slab, BF)] * core + [
        vm((2, 2) + slab, BF), vm((2, 2) + slab, BF), vm((2,) + slab, BF), vm((2,) + slab, BF),
        vm(slab, BF), vm(slab, BF),
    ]


def forward_and_glu(
    rate_in, tok, cot, seg, wq, wk, wv, wg, wo_in, gl_in, gr_in, gd_in,
    n1_o, n2_o, pkq_o, pg_o, qkv_o, p_o, att_o, mix_o, sb_o, w_o, wo_o, ids_o, rate_o,
    dr_o, dx1_o, fs_o, fo_o, dpr_o, gdown_o, left_o,
    xb, n1, ct, n2, x1, pg, qkv, pm, att, mix, sb, wb, wo, gl, gr, gd,
    ids, rate, grid, wend, gin, mask, endf, inf, uf, us, ur, ts, tr, vs, vr, pf,
    br_s, br_r, dn_r, dn, hid, dpl, dpr, tmp, dr, fs, fo, gdown, left_acc,
    *rest,
):
    down_b, left_b = rest[:9], (left_acc, rest[1], rest[9]) + (None,) * 6
    send, recv, local = rest[10:]
    pc = Place()
    pc.greet()
    ln = Links(pc, send, recv, local)
    own, r = pc.zh, pc.r
    far_b = 1 - own

    def mine(s):
        return pl.ds(pl.multiple_of(s * CH + pc.t * 128, 128), 128)

    def theirs(s):
        return pl.ds(pl.multiple_of(s * CH + (1 - pc.t) * 128, 128), 128)

    def wview(i):
        return lambda b, rr: wb.at[i, b, rows128(rr), :]

    def gview(w):
        return lambda b, rr: w.at[b, :, rows128(rr)]

    for hh in range(2):
        rate[own * 2 + hh] = jnp.full((8, DH), rate_in[hh], F32)
    for s in range(2):
        xb[mine(s), :] = tok[s]
        ct[mine(s), :] = cot[s]
    for i, w in enumerate((wk, wv, wq, wg)):
        wb[i, own, rows128(r), :] = w[...].astype(BF)
    wo[pl.ds(pl.multiple_of(own * 256, 256), 256), rows128(r)] = wo_in[...].astype(BF)
    ids[pc.k] = jnp.zeros((8, 512), F32)
    ids[pc.k, 0:2, :] = seg[...].astype(F32)
    pc.meet()

    g_o = Gather(ln, "A", lambda b, rr: wo.at[pl.ds(pl.multiple_of(b * 256, 256), 256), rows128(rr)])
    qkvgo = [Gather(ln, "AB"[i % 2], wview(i)) for i in range(4)] + [g_o]
    g_l, g_r, g_d = Gather(ln, "A", gview(gl)), Gather(ln, "B", gview(gr)), Gather(ln, "A", gview(gd))
    rate_cp = ln.go(rate.at[pl.ds(own * 2, 2)], rate.at[pl.ds(own * 2, 2)], "Q")
    ids_y = ln.go(ids.at[pc.k], ids.at[pc.k], "Y")
    ids_c = ln.go(ids.at[pc.k], ids.at[pc.k], "C")
    for g in qkvgo[:2]:
        g.cross()
        g.launch(0)
    x_cp = [ln.go(xb.at[mine(s)], xb.at[mine(s)], "P") for s in range(2)]
    for g in qkvgo[2:]:
        g.launch(0)
    for g in qkvgo[2:]:
        g.cross()
    ct_cp = [ln.go(ct.at[mine(0)], ct.at[mine(0)], "P")]
    for s in range(2):
        xf = tok[s].astype(F32)
        n1[mine(s), :] = (xf * inverse_norm(xf, EPSILON)).astype(BF)
    for w, w_in in ((gl, gl_in), (gr, gr_in), (gd, gd_in)):
        w[own, :, rows128(r)] = w_in[...].astype(BF)
    kf = (pc.k + 2) % 4
    ids_y.wait_recv()
    ids_f = ln.go(ids.at[kf], ids.at[kf], "C")
    for g in qkvgo:
        g.step1(0)
    rate_cp.wait_recv()
    fill_decay(rate, grid, wend, gin)
    for g in qkvgo[:2]:
        g.other()
    for g in qkvgo:
        g.step2(0)
    ids_c.wait_recv()
    ids_f.wait_recv()
    fill_masks(pc, ids, mask, endf, inf)
    for g in qkvgo[:2]:
        g.step1(1)
    g_l.launch(0)
    g_r.launch(0)
    for g in qkvgo[:2]:
        g.step2(1)
    for s in range(2):
        x_cp[s].wait_recv()
        xf = xb[theirs(s), :].astype(F32)
        n1[theirs(s), :] = (xf * inverse_norm(xf, EPSILON)).astype(BF)

    def project(i):
        for slot in range(2):
            qkvgo[i].step3(slot)

        def block(b, _):
            p = dg(n1[...], wb[i, b], 1, 0)
            if i == 0:
                x1[:, cols256(b)] = p
            elif i == 2:
                x1[:, cols256(2 + b)] = p
            elif i == 3:
                pg[:, cols256(b)] = p
            if i < 3:
                a = (p if i == 1 else p * jax.nn.sigmoid(p)).astype(BF)
                qkv[i, b * 2] = a[:, :DH]
                qkv[i, b * 2 + 1] = a[:, DH:]
            return 0

        lax.fori_loop(0, 2, block, 0)

    project(0)
    project(1)
    u_cp = []
    for s in range(2):
        rs_ = pl.ds(s * CH, CH)

        def state(h, _):
            kw = (qkv[0, h, rs_, :].astype(F32) * (wend[h] * endf[s])).astype(BF)
            u = dg(kw, qkv[1, h, rs_, :], 0, 0)
            uf[s, h] = u
            us[s, h] = u.astype(BF)
            return 0

        lax.fori_loop(0, 4, state, 0)
        u_cp.append(ln.go(us.at[s], ur.at[s], "Q"))
    for g in qkvgo[2:]:
        g.other()
    g_l.cross()
    g_r.cross()
    g_l.step1(0)
    g_r.step1(0)
    for g in qkvgo[2:]:
        g.step1(1)
    for g in qkvgo[2:]:
        g.step2(1)
    project(2)
    for s in range(2):
        rs_ = pl.ds(s * CH, CH)

        def inside(h, _):
            sc = dg(qkv[2, h, rs_, :], qkv[0, h, rs_, :], 1, 1)
            p = (sc * grid[h] * mask[s]).astype(BF)
            pm[s, h] = p
            att[h, rs_, :] = dg(p, qkv[1, h, rs_, :], 1, 0)
            return 0

        lax.fori_loop(0, 4, inside, 0)
    project(3)
    g_o.step3(0)
    g_o.step3(1)
    pkq_cp = ln.keep(x1, pkq_o)
    for i in range(4):
        ln.keep(wb.at[i], w_o.at[i])
    ln.keep(n1, n1_o)
    ln.keep(pg, pg_o)
    ln.keep(qkv, qkv_o)
    ln.keep(ids, ids_o)
    ln.keep(rate, rate_o)
    ln.keep(pm, p_o)
    ln.keep(wo, wo_o)
    g_l.step2(0)
    g_r.step2(0)
    g_d.launch(0)

    t_cp, v_cp = [], []
    for s in range(2):
        u_cp[s].wait_recv()
        fl = same(last_id(ids, pc.k, 0, s), last_id(ids, pc.k, 1, s))

        def pair(h, _):
            lane = jnp.exp(-CH * rate[h, 0:1, :]) * fl
            got = ur[s, h].astype(F32)
            wo_ = jnp.where(pc.zh == 1, jnp.ones_like(lane), lane)
            wr_ = jnp.where(pc.zh == 1, lane, jnp.ones_like(lane))
            tot = wo_ * uf[s, h] + wr_ * got
            pf[s, h] = jnp.where(pc.zh == 1, got, jnp.zeros_like(got))
            uf[s, h] = tot
            ts[s, h] = tot.astype(BF)
            return 0

        lax.fori_loop(0, 4, pair, 0)
        t_cp.append(ln.go(ts.at[s], tr.at[s], "C"))
    for s in range(2):
        t_cp[s].wait_recv()
        prior = prior_id(pc, ids, s)
        low = last_id(ids, pc.y * 2, 1, s)
        fl = same(low, last_id(ids, pc.y * 2 + 1, 1, s))
        fp = same(low, prior) * jnp.where(pc.c == 1, 1.0, 0.0)

        def quad(h, _):
            one = rate[h, 0:1, :]
            lane = jnp.exp(-2.0 * CH * one) * fl
            got = tr[s, h].astype(F32)
            wo_ = jnp.where(pc.c == 1, jnp.ones_like(lane), lane)
            wr_ = jnp.where(pc.c == 1, lane, jnp.ones_like(lane))
            vs[s, h] = (wo_ * uf[s, h] + wr_ * got).astype(BF)
            pf[s, h] = pf[s, h] + (jnp.exp(-(CH * 1.0) * pc.zh.astype(F32) * one) * fp) * got
            return 0

        lax.fori_loop(0, 4, quad, 0)
        v_cp.append(ln.go(vs.at[s], vr.at[s], "Y"))
    ln.written(pkq_cp)
    b_cp = []
    for s in range(2):
        v_cp[s].wait_recv()
        fp = same(last_id(ids, 1, 1, s), prior_id(pc, ids, s)) * jnp.where(pc.y == 1, 1.0, 0.0)
        far = (2 * pc.c + pc.zh).astype(F32) * CH
        rs_ = pl.ds(s * CH, CH)

        def enter(h, _):
            got = vr[s, h].astype(F32)
            st = pf[s, h] + (jnp.exp(-far * rate[h, 0:1, :]) * fp) * got
            low_st = st.astype(BF)
            sb[s, h] = low_st
            o = att[h, rs_, :] + (gin[h] * inf[s]) * dg(qkv[2, h, rs_, :], low_st, 1, 0)
            att[h, rs_, :] = o
            on = o * inverse_norm(o, HEAD_FLOOR)
            mix[rs_, rows128(h)] = (on * jax.nn.sigmoid(pg[rs_, rows128(h)])).astype(BF)
            return 0

        lax.fori_loop(0, 4, enter, 0)
        part = dg(mix[rs_, :], wo[...], 1, 0)
        br_s[rs_, :] = part.astype(BF)
        b_cp.append(ln.go(br_s.at[rs_], br_r.at[rs_], "P"))
        x1[rs_, :] = xb[rs_, :].astype(F32) + part
        if s == 0:
            g_d.cross()
            g_d.step1(0)
            g_l.other()
    ct_cp.append(ln.go(ct.at[mine(1)], ct.at[mine(1)], "P"))
    ln.keep(att, att_o)
    ln.keep(mix, mix_o)
    ln.keep(sb, sb_o)
    g_r.other()
    g_d.step2(0)
    g_l.step1(1)
    g_r.step1(1)
    for g in (g_l, g_r, g_d):
        g.step3(0)
    g_l.step2(1)
    g_r.step2(1)
    d_cp = []

    def units(s, b):
        rs_ = pl.ds(s * CH, CH)
        a = dg(n2[rs_, :], gl[b], 1, 1)
        c = dg(n2[rs_, :], gr[b], 1, 1)
        hid[b, rs_, :] = (a * c).astype(BF)
        dh = dg(ct[rs_, :], gd[b], 1, 1)
        dpl[b, rs_, :] = (dh * c).astype(BF)
        dpr[b, rs_, :] = (dh * a).astype(BF)

    for s in range(2):
        rs_ = pl.ds(s * CH, CH)
        b_cp[s].wait_recv()
        v = x1[rs_, :] + br_r[rs_, :].astype(F32)
        x1[rs_, :] = v
        n2[rs_, :] = (v * inverse_norm(v, EPSILON)).astype(BF)
        if s == 0:
            g_d.other()
        ct_cp[s].wait_recv()
        units(s, own)
        if s == 0:
            g_d.step1(1)
            g_l.step3(1)
            g_r.step3(1)
            g_d.step2(1)
            g_d.step3(1)
        units(s, far_b)
        part = (
            dg(dpl[0, rs_, :], gl[0], 1, 0) + dg(dpr[0, rs_, :], gr[0], 1, 0)
            + dg(dpl[1, rs_, :], gl[1], 1, 0) + dg(dpr[1, rs_, :], gr[1], 1, 0)
        )
        dn[rs_, :] = part
        ln.gone(b_cp[s])
        br_s[rs_, :] = part.astype(BF)
        d_cp.append(ln.go(br_s.at[rs_], dn_r.at[rs_], "P"))
    ln.keep(n2, n2_o)
    ln.keep(dpr, dpr_o)

    down = Scatter(ln, "cols", down_b)
    left = Scatter(ln, "cols", left_b)
    for b in range(2):
        down.core_stage(b, lambda b, i: dg(hid[b], ct[:, cols256(i)], 0, 0))

    def turn(s):
        rs_ = pl.ds(s * CH, CH)
        d_cp[s].wait_recv()
        g = ct[rs_, :].astype(F32) + norm_slope(x1[rs_, :], dn[rs_, :] + dn_r[rs_, :].astype(F32), EPSILON)
        dn[rs_, :] = g
        dr[rs_, :] = g.astype(BF)
        ln.keep(dr.at[rs_], dr_o.at[rs_])
        ln.keep(dn.at[mine(s)], dx1_o.at[s])

    def feed(s):
        rs_ = pl.ds(s * CH, CH)
        tmp[...] = dg(hid[0, rs_, :], gd[0], 1, 0) + dg(hid[1, rs_, :], gd[1], 1, 0)
        fs[s] = tmp[rows128(1 - pc.t), :].astype(BF)
        fo[s] = x1[mine(s), :] + tmp[rows128(pc.t), :]

    feed(0)
    for b in range(2):
        down.first_stage(b)
    for b in range(2):
        left.core_stage(b, lambda b, i: dg(dpl[b], n2[:, cols256(i)], 0, 0), down)
    turn(0)
    feed(1)
    ln.keep(fs, fs_o)
    ln.keep(fo, fo_o)
    for b in range(2):
        down.second_stage(b)
    for b in range(2):
        left.join(b)
    ln.keep(left.acc, left_o)
    down.plane_stage()
    turn(1)
    gdown[...] = down.total()
    ln.keep(gdown, gdown_o)
    ln.drain()


def call_forward(rate, tok, cot, seg, ws, wo, gl, gr, gd):
    sd, vm = jax.ShapeDtypeStruct, pltpu.VMEM
    ff = gl.shape[0]
    act = (512, 1024)
    st = (2, 4, DH, DH)
    outs = [
        sd(act, BF), sd(act, BF), sd(act, F32), sd((512, 512), F32), sd((3, 4, 512, DH), BF),
        sd((2, 4, CH, CH), BF), sd((4, 512, DH), F32), sd((512, 512), BF), sd(st, BF),
        sd((4, 2, 1024, 256), BF), sd(act, BF), sd((4, 8, 512), F32), sd((4, 8, DH), F32),
        sd(act, BF), sd((2, 128, 1024), F32), sd((2, 128, 1024), BF), sd((2, 128, 1024), F32),
        sd((2, 512, ff), BF), sd((ff, 128), F32), sd((2, 4, ff, 128), BF),
    ]
    scratch = [
        vm(act, BF), vm(act, BF), vm(act, BF), vm(act, BF), vm(act, F32), vm((512, 512), F32),
        vm((3, 4, 512, DH), BF), vm((2, 4, CH, CH), BF), vm((4, 512, DH), F32), vm((512, 512), BF),
        vm(st, BF), vm((4, 2, 1024, 256), BF), vm(act, BF),
        vm((2, ff, 1024), BF), vm((2, ff, 1024), BF), vm((2, ff, 1024), BF),
        vm((4, 8, 512), F32), vm((4, 8, DH), F32),
        vm((4, CH, CH), F32), vm((4, CH, DH), F32), vm((4, CH, DH), F32),
        vm((2, CH, CH), F32), vm((2, CH, DH), F32), vm((2, CH, DH), F32),
        vm(st, F32), vm(st, BF), vm(st, BF), vm(st, BF), vm(st, BF), vm(st, BF), vm(st, BF), vm(st, F32),
        vm(act, BF), vm(act, BF), vm(act, BF), vm(act, F32),
        vm((2, 512, ff), BF), vm((2, 512, ff), BF), vm((2, 512, ff), BF),
        vm((CH, 1024), F32), vm(act, BF), vm((2, 128, 1024), BF), vm((2, 128, 1024), F32), vm((ff, 128), F32), vm((2, 4, ff, 128), BF),
        *scatter_bufs((ff, 128), BF), vm((2, 4, ff, 128), BF),
        pltpu.SemaphoreType.DMA((160,)), pltpu.SemaphoreType.DMA((160,)), pltpu.SemaphoreType.DMA((40,)),
    ]
    vin = pl.BlockSpec(memory_space=pltpu.VMEM)
    return pl.pallas_call(
        forward_and_glu,
        out_shape=outs,
        in_specs=[pl.BlockSpec(memory_space=pltpu.SMEM)] + [vin] * 11,
        out_specs=[pl.BlockSpec(memory_space=pl.ANY)] * len(outs),
        scratch_shapes=scratch,
        compiler_params=pltpu.CompilerParams(
            collective_id=0, has_side_effects=True, vmem_limit_bytes=63 * MIB
        ),
        name="forward_and_glu",
    )(rate, tok, cot, seg, *ws, wo, gl, gr, gd)


def silu_slope(v):
    g = jax.nn.sigmoid(v)
    return g * (1.0 + v * (1.0 - g))


N_BACK_IN = 20


def cut_bufs(refs):
    sets = []
    for n in (6, 9, 9, 9, 9, 9, 9):
        sets.append(tuple(refs[:n]))
        refs = refs[n:]
    return sets, refs


def attn_backward(*refs):
    ins, refs = refs[:N_BACK_IN], refs[N_BACK_IN:]
    outs, refs = refs[:9], refs[9:]
    bufs, refs = refs[:N_BACK_IN], refs[N_BACK_IN:]
    out_o, gtok_o, gq_o, gk_o, gv_o, gg_o, go_o, gl_o, gr_o = outs
    (ids, rate, dr, wo, att, pg, qkv, left_acc, n2, dpr, pm, sb, pkq, n1, mix, wb, fs, fo, dx1, x) = bufs
    (
        grid, wend, gin, mask, endf, inf, dm, dob, dp, vf, vs, vr, ts, tr, ws, wr, rf, du,
        tmp, nsend, nrecv, frecv, gtok, gw, gout, gleft, gright,
    ) = refs[:27]
    refs = refs[27:]
    sc_bufs, refs = cut_bufs(refs)
    send, recv, local = refs
    pc = Place()
    pc.greet()
    ln = Links(pc, send, recv, local)
    got = [ln.fetch(a, b) for a, b in zip(ins, bufs)]

    def ready(n):
        while len(got) > N_BACK_IN - n:
            got.pop(0).wait()

    pc.meet()
    ready(2)
    fill_decay(rate, grid, wend, gin)
    fill_masks(pc, ids, mask, endf, inf)
    ready(4)

    def mine(s):
        return pl.ds(pl.multiple_of(s * CH + pc.t * 128, 128), 128)

    def through(b, _):
        dm[:, cols256(b)] = dg(dr[...], wo[cols256(b), :], 1, 1)
        return 0

    lax.fori_loop(0, 2, through, 0)
    ready(7)
    v_cp = []
    for s in range(2):
        rs_ = pl.ds(s * CH, CH)

        def outer(h, _):
            d, o = dm[rs_, rows128(h)], att[h, rs_, :]
            g = jax.nn.sigmoid(pg[rs_, rows128(h)])
            inv = inverse_norm(o, HEAD_FLOOR)
            dp[3, rs_, rows128(h)] = (d * (o * inv) * g * (1.0 - g)).astype(BF)
            e = d * g
            inner = jnp.mean(e * o, axis=-1, keepdims=True)
            do = (inv * (e - o * (inner * inv * inv))).astype(BF)
            dob[h, rs_, :] = do
            gq = (qkv[2, h, rs_, :].astype(F32) * (gin[h] * inf[s])).astype(BF)
            v = dg(gq, do, 0, 0)
            vf[s, h] = v
            vs[s, h] = v.astype(BF)
            return 0

        lax.fori_loop(0, 4, outer, 0)
        v_cp.append(ln.go(vs.at[s], vr.at[s], "Q"))

    left = Scatter(ln, "cols", (left_acc, None, None) + sc_bufs[0])
    right = Scatter(ln, "cols", sc_bufs[1])
    s_out = Scatter(ln, "cols", sc_bufs[2])
    s_w = [Scatter(ln, "rows", sc_bufs[3 + i]) for i in range(4)]

    def product(i):
        return lambda b, j: dg(n1[:, cols256(j)], dp[i, :, cols256(b)], 0, 0)

    ready(8)
    for b in range(2):
        left.first_stage(b, True)
    ready(10)
    for b in range(2):
        right.core_stage(b, lambda b, i: dg(dpr[b], n2[:, cols256(i)], 0, 0))
    ready(13)

    for s in range(2):
        rs_ = pl.ds(s * CH, CH)

        def inside(h, _):
            do, q, k = dob[h, rs_, :], qkv[2, h, rs_, :], qkv[0, h, rs_, :]
            dsc = (dg(do, qkv[1, h, rs_, :], 1, 1) * grid[h] * mask[s]).astype(BF)
            dq = dg(dsc, k, 1, 0) + (gin[h] * inf[s]) * dg(do, sb[s, h], 1, 1)
            dp[2, rs_, rows128(h)] = (dq * silu_slope(pkq[rs_, rows128(4 + h)])).astype(BF)
            dm[rs_, rows128(h)] = dg(dsc, q, 0, 0)
            att[h, rs_, :] = dg(pm[s, h], do, 0, 0)
            return 0

        lax.fori_loop(0, 4, inside, 0)

    for b in range(2):
        right.first_stage(b)
    ready(20)
    f_cp = ln.go(fs, frecv, "P")
    for b in range(2):
        s_out.core_stage(b, lambda b, i: dg(mix[:, cols256(b)], dr[:, cols256(i)], 0, 0))
    for i in (3, 2):
        for b in range(2):
            s_w[i].core_stage(b, product(i))
    t_cp, w_cp = [], []
    for s in range(2):
        v_cp[s].wait_recv()
        before = jnp.where(pc.k > 0, last_id(ids, (pc.k + 3) % 4, 1, s), -1.0)
        fb = same(before, last_id(ids, pc.k, 0, s))

        def pair(h, _):
            lane = jnp.exp(-CH * rate[h, 0:1, :]) * fb
            g = vr[s, h].astype(F32)
            wo_ = jnp.where(pc.zh == 0, jnp.ones_like(lane), lane)
            wr_ = jnp.where(pc.zh == 0, lane, jnp.ones_like(lane))
            tot = wo_ * vf[s, h] + wr_ * g
            rf[s, h] = jnp.where(pc.zh == 0, g, jnp.zeros_like(g))
            vf[s, h] = tot
            ts[s, h] = tot.astype(BF)
            return 0

        lax.fori_loop(0, 4, pair, 0)
        t_cp.append(ln.go(ts.at[s], tr.at[s], "C"))
    for b in range(2):
        left.second_stage(b)
    for s in range(2):
        t_cp[s].wait_recv()
        low = last_id(ids, pc.y * 2, 1, s)
        before = jnp.where(pc.y > 0, last_id(ids, (pc.y * 2 + 3) % 4, 1, s), -1.0)
        fb = same(before, low)
        here = jnp.where(pc.zh == 1, last_id(ids, pc.k, 1, s), last_id(ids, pc.k, 0, s))
        fp = same(here, low) * jnp.where(pc.c == 0, 1.0, 0.0)
        far = (1 - pc.zh).astype(F32) * CH

        def quad(h, _):
            one = rate[h, 0:1, :]
            lane = jnp.exp(-2.0 * CH * one) * fb
            g = tr[s, h].astype(F32)
            wo_ = jnp.where(pc.c == 0, jnp.ones_like(lane), lane)
            wr_ = jnp.where(pc.c == 0, lane, jnp.ones_like(lane))
            ws[s, h] = (wo_ * vf[s, h] + wr_ * g).astype(BF)
            rf[s, h] = rf[s, h] + (jnp.exp(-far * one) * fp) * g
            return 0

        lax.fori_loop(0, 4, quad, 0)
        w_cp.append(ln.go(ws.at[s], wr.at[s], "Y"))
    for b in range(2):
        right.second_stage(b)
        s_out.first_stage(b)
    for i in (3, 2):
        for b in range(2):
            s_w[i].first_stage(b)
    n_cp = []
    for s in range(2):
        w_cp[s].wait_recv()
        here = jnp.where(pc.zh == 1, last_id(ids, pc.k, 1, s), last_id(ids, pc.k, 0, s))
        fp = same(here, last_id(ids, 1, 1, s)) * jnp.where(pc.y == 0, 1.0, 0.0)
        far = (2 * (1 - pc.c) + (1 - pc.zh)).astype(F32) * CH
        rs_ = pl.ds(s * CH, CH)

        def close(h, _):
            d = (rf[s, h] + (jnp.exp(-far * rate[h, 0:1, :]) * fp) * wr[s, h].astype(F32)).astype(BF)
            k, v = qkv[0, h, rs_, :], qkv[1, h, rs_, :]
            w = wend[h] * endf[s]
            kw = (k.astype(F32) * w).astype(BF)
            dp[1, rs_, rows128(h)] = (att[h, rs_, :] + dg(kw, d, 1, 0)).astype(BF)
            dk = dm[rs_, rows128(h)] + w * dg(v, d, 1, 1)
            dp[0, rs_, rows128(h)] = (dk * silu_slope(pkq[rs_, rows128(h)])).astype(BF)
            return 0

        lax.fori_loop(0, 4, close, 0)
        acc = None
        for i in range(4):
            for b in range(2):
                p = dg(dp[i, rs_, b * 256 : (b + 1) * 256], wb[i, b], 1, 1)
                acc = p if acc is None else acc + p
        tmp[...] = acc
        nsend[s] = tmp[rows128(1 - pc.t), :].astype(BF)
        n_cp.append(ln.go(nsend.at[s], nrecv.at[s], "P"))
        gtok[s] = tmp[rows128(pc.t), :]
    for i in (0, 1):
        for b in range(2):
            s_w[i].core_stage(b, product(i))
    left.plane_stage()
    right.plane_stage()
    for b in range(2):
        s_out.second_stage(b)
    for i in (3, 2):
        for b in range(2):
            s_w[i].second_stage(b)
    for i in (0, 1):
        for b in range(2):
            s_w[i].first_stage(b)
    s_out.plane_stage()
    for i in (3, 2):
        s_w[i].plane_stage()
    f_cp.wait_recv()
    frecv[...] = (fo[...] + frecv[...].astype(F32)).astype(BF)
    ln.keep(frecv, out_o)
    for s in range(2):
        n_cp[s].wait_recv()
        dn = gtok[s] + nrecv[s].astype(F32)
        gtok[s] = dx1[s] + norm_slope(x[s].astype(F32), dn, EPSILON)
    ln.keep(gtok, gtok_o)
    for i in (0, 1):
        for b in range(2):
            s_w[i].second_stage(b)
    gleft[...] = left.total()
    ln.keep(gleft, gl_o)
    gright[...] = right.total()
    ln.keep(gright, gr_o)
    for i in (0, 1):
        s_w[i].plane_stage()
    gout[...] = s_out.total()
    ln.keep(gout, go_o)
    for i, o in ((3, gg_o), (2, gq_o), (0, gk_o), (1, gv_o)):
        gw[i] = s_w[i].total()
        ln.keep(gw.at[i], o)
    ln.drain()


def call_backward(*args):
    sd, vm = jax.ShapeDtypeStruct, pltpu.VMEM
    ff = args[9].shape[2]
    outs = [
        sd((2, 128, 1024), BF), sd((2, 128, 1024), F32),
        sd((128, 256), F32), sd((128, 256), F32), sd((128, 256), F32), sd((128, 256), F32),
        sd((256, 128), F32), sd((ff, 128), F32), sd((ff, 128), F32),
    ]
    st = (2, 4, DH, DH)
    scratch = [vm(a.shape, a.dtype) for a in args] + [
        vm((4, CH, CH), F32), vm((4, CH, DH), F32), vm((4, CH, DH), F32),
        vm((2, CH, CH), F32), vm((2, CH, DH), F32), vm((2, CH, DH), F32),
        vm((512, 512), F32), vm((4, 512, DH), BF), vm((4, 512, 512), BF),
        vm(st, F32), vm(st, BF), vm(st, BF), vm(st, BF), vm(st, BF), vm(st, BF), vm(st, BF),
        vm(st, F32), vm((8, 128), BF),
        vm((CH, 1024), F32), vm((2, 128, 1024), BF), vm((2, 128, 1024), BF), vm((2, 128, 1024), BF),
        vm((2, 128, 1024), F32), vm((4, 128, 256), F32),
        vm((256, 128), F32), vm((ff, 128), F32), vm((ff, 128), F32),
        *scatter_bufs((ff, 128), BF, 0)[1:], *scatter_bufs((ff, 128), BF),
        *scatter_bufs((256, 128)), *scatter_bufs((128, 256)), *scatter_bufs((128, 256)),
        *scatter_bufs((128, 256)), *scatter_bufs((128, 256)),
        pltpu.SemaphoreType.DMA((64,)), pltpu.SemaphoreType.DMA((64,)), pltpu.SemaphoreType.DMA((40,)),
    ]
    return pl.pallas_call(
        attn_backward,
        out_shape=outs,
        in_specs=[pl.BlockSpec(memory_space=pl.ANY)] * len(args),
        out_specs=[pl.BlockSpec(memory_space=pl.ANY)] * len(outs),
        scratch_shapes=scratch,
        compiler_params=pltpu.CompilerParams(
            collective_id=2, has_side_effects=True, vmem_limit_bytes=63 * MIB
        ),
        name="attention_backward",
    )(*args)


def entering(x, axis, join, neutral):
    place = lax.axis_index(axis)
    gathered = jax.tree.map(
        lambda a, kind: lax.all_gather(a.astype(kind), axis),
        x,
        (jnp.bfloat16, jnp.bfloat16, jnp.bfloat16, jnp.bfloat16),
    )
    state = jax.tree.map(lambda a, e: jnp.zeros_like(a) + jnp.asarray(e, a.dtype), x, neutral)

    def one(lap, state):
        return join(
            state,
            jax.tree.map(
                lambda a, own: lax.dynamic_index_in_dim(a, lap, 0, False).astype(own.dtype),
                gathered,
                x,
            ),
        )

    return lax.fori_loop(0, place, one, state)


def entering_2(x, axis, join, neutral):
    count = lax.axis_size(axis)
    place = lax.axis_index(axis)
    ahead = count - 1 - place
    gathered = jax.tree.map(
        lambda a, kind: lax.all_gather(a.astype(kind), axis), x, (jnp.bfloat16, jnp.bfloat16)
    )
    state = jax.tree.map(lambda a, e: jnp.zeros_like(a) + jnp.asarray(e, a.dtype), x, neutral)

    def one(lap, state):
        source = count - 1 - lap
        return join(
            state,
            jax.tree.map(
                lambda a, own: lax.dynamic_index_in_dim(a, source, 0, False).astype(own.dtype),
                gathered,
                x,
            ),
        )

    return lax.fori_loop(0, ahead, one, state)


def normalize(values, floor_value=EPSILON):
    return values * lax.rsqrt(jnp.mean(values * values, axis=-1, keepdims=True) + floor_value)


def norm_backward(values, upstream, floor_value=EPSILON):
    inverse = lax.rsqrt(jnp.mean(values * values, axis=-1, keepdims=True) + floor_value)
    inner_mean = jnp.mean(upstream * values, axis=-1, keepdims=True)
    return inverse * (upstream - values * inner_mean * inverse * inverse)


def silu_grad(values):
    sigmoid_value = jax.nn.sigmoid(values)
    return sigmoid_value * (1.0 + values * (1.0 - sigmoid_value))


def chain_forward(earlier, later):
    early_first, early_last, early_decay, early_state = earlier
    late_first, late_last, late_decay, late_state = later
    linked = (late_first == early_last) | (early_last < 0.0) | (late_first < 0.0)
    carried = jnp.where(linked[:, None], late_decay, 0.0)
    first_seg = jnp.where(early_first < 0.0, late_first, early_first)
    last_seg = jnp.where(late_last < 0.0, early_last, late_last)
    return (
        first_seg,
        last_seg,
        early_decay * carried,
        late_state + carried[:, :, None, None] * early_state,
    )


def chain_backward(earlier, later):
    return (earlier[0] * later[0], later[1] + later[0][:, :, None, None] * earlier[1])


def shards(
    tokens,
    segment_ids,
    decay_rate,
    w_query,
    w_key,
    w_value,
    w_gate,
    w_out,
    glu_left,
    glu_right,
    glu_down,
    cotangent,
):
    shard_len, seq_count, model_width = tokens.shape
    tok_float = tokens.astype(jnp.float32)
    normed_part = normalize(tok_float).astype(jnp.bfloat16)
    gathered = (
        lax.all_gather(w_query.astype(jnp.bfloat16), ("fsdp", "ctx"), axis=0, tiled=True),
        lax.all_gather(w_key.astype(jnp.bfloat16), ("fsdp", "ctx"), axis=0, tiled=True),
        lax.all_gather(w_value.astype(jnp.bfloat16), ("fsdp", "ctx"), axis=0, tiled=True),
        lax.all_gather(w_gate.astype(jnp.bfloat16), ("fsdp", "ctx"), axis=0, tiled=True),
        lax.all_gather(w_out.astype(jnp.bfloat16), ("fsdp", "ctx"), axis=1, tiled=True),
        lax.all_gather(glu_left.astype(jnp.bfloat16), ("fsdp", "ctx"), axis=0, tiled=True),
        lax.all_gather(glu_right.astype(jnp.bfloat16), ("fsdp", "ctx"), axis=0, tiled=True),
        lax.all_gather(glu_down.astype(jnp.bfloat16), ("fsdp", "ctx"), axis=1, tiled=True),
    )
    full_query, full_key, full_value, full_gate, full_out, full_left, full_right, full_down = (
        gathered
    )
    normed = lax.all_gather(normed_part, "tp", axis=0, tiled=True)
    block_len = normed.shape[0]
    total_rows = block_len * seq_count
    normed_flat = normed.reshape(total_rows, model_width)
    local_width = full_query.shape[1]
    head_count = local_width // DH
    head_shape = (block_len, seq_count, head_count, DH)
    proj_query = jnp.dot(normed_flat, full_query, preferred_element_type=jnp.float32)
    proj_key = jnp.dot(normed_flat, full_key, preferred_element_type=jnp.float32)
    proj_value = jnp.dot(normed_flat, full_value, preferred_element_type=jnp.float32)
    proj_gate = jnp.dot(normed_flat, full_gate, preferred_element_type=jnp.float32)
    queries = jax.nn.silu(proj_query).astype(jnp.bfloat16).reshape(head_shape)
    keys_low = jax.nn.silu(proj_key).astype(jnp.bfloat16).reshape(head_shape)
    values_low = proj_value.astype(jnp.bfloat16).reshape(head_shape)
    seg_pos = segment_ids.T
    seg_float = seg_pos.astype(jnp.float32)
    position = jnp.arange(block_len).astype(jnp.float32)
    distance = position[:, None] - position[None, :]
    same_doc = (segment_ids[:, :, None] == segment_ids[:, None, :]) & (distance >= 0.0)[None]
    decay_grid = jnp.where(
        same_doc[:, None],
        jnp.exp(-decay_rate[None, :, None, None] * jnp.maximum(distance, 0.0)[None, None]),
        0.0,
    )
    end_weight = jnp.where(
        (seg_pos == seg_pos[-1:])[:, :, None],
        jnp.exp(-(block_len - 1.0 - position)[:, None, None] * decay_rate[None, None, :]),
        0.0,
    )
    keys_end = (keys_low.astype(jnp.float32) * end_weight[..., None]).astype(jnp.bfloat16)
    update = jnp.einsum("tbhd,tbhe->bhde", keys_end, values_low, preferred_element_type=jnp.float32)
    first_seg = seg_float[0]
    last_seg = seg_float[-1]
    span_decay = jnp.where(
        (first_seg == last_seg)[:, None], jnp.exp(-block_len * decay_rate)[None, :], 0.0
    )
    identity = (
        -jnp.ones((seq_count,), jnp.float32),
        -jnp.ones((seq_count,), jnp.float32),
        jnp.ones((seq_count, head_count), jnp.float32),
        jnp.zeros((seq_count, head_count, DH, DH), jnp.float32),
    )
    scanned = entering((first_seg, last_seg, span_decay, update), "ctx", chain_forward, identity)
    prior_last = scanned[1]
    state_low = scanned[3].astype(jnp.bfloat16)
    inflow = jnp.where(
        (seg_pos == prior_last[None, :])[:, :, None],
        jnp.exp(-(position + 1.0)[:, None, None] * decay_rate[None, None, :]),
        0.0,
    )
    scores = jnp.einsum("tbhd,sbhd->bhts", queries, keys_low, preferred_element_type=jnp.float32)
    weights_low = (scores * decay_grid).astype(jnp.bfloat16)
    intra = jnp.einsum(
        "bhts,sbhd->tbhd", weights_low, values_low, preferred_element_type=jnp.float32
    )
    inter = (
        jnp.einsum("tbhd,bhde->tbhe", queries, state_low, preferred_element_type=jnp.float32)
        * inflow[..., None]
    )
    attended = intra + inter
    attended_norm = normalize(attended, HEAD_FLOOR)
    gate_value = jax.nn.sigmoid(proj_gate).reshape(head_shape)
    mixed_heads = (
        (attended_norm * gate_value).astype(jnp.bfloat16).reshape(block_len, seq_count, local_width)
    )
    row_count = shard_len * lax.axis_size("tp")
    piece_rows = mixed_heads.reshape(row_count * seq_count, local_width)
    branch = lax.psum_scatter(
        jnp.dot(piece_rows, full_out, preferred_element_type=jnp.float32).reshape(
            row_count, seq_count, model_width
        ),
        "tp",
        scatter_dimension=0,
        tiled=True,
    )
    residual = tok_float + branch
    second_part = normalize(residual).astype(jnp.bfloat16)
    second = lax.all_gather(second_part, "tp", axis=0, tiled=True)
    second_flat = second.reshape(total_rows, model_width)
    left_proj = jnp.dot(second_flat, full_left, preferred_element_type=jnp.float32)
    right_proj = jnp.dot(second_flat, full_right, preferred_element_type=jnp.float32)
    hidden = (left_proj * right_proj).astype(jnp.bfloat16)
    ffn_width = hidden.shape[1]
    hidden_blocks = hidden.reshape(block_len, seq_count, ffn_width)
    row_count = shard_len * lax.axis_size("tp")
    piece_rows = hidden_blocks.reshape(row_count * seq_count, ffn_width)
    ffn_branch = lax.psum_scatter(
        jnp.dot(piece_rows, full_down, preferred_element_type=jnp.float32)
        .reshape(row_count, seq_count, model_width)
        .astype(jnp.bfloat16),
        "tp",
        scatter_dimension=0,
        tiled=True,
    ).astype(jnp.float32)
    output = (residual + ffn_branch).astype(jnp.bfloat16)
    upstream = lax.all_gather(cotangent, "tp", axis=0, tiled=True).reshape(total_rows, model_width)
    grad_down = jnp.dot(hidden.T, upstream, preferred_element_type=jnp.float32)
    grad_hidden = jnp.dot(upstream, full_down.T, preferred_element_type=jnp.float32)
    grad_left_proj = (grad_hidden * right_proj).astype(jnp.bfloat16)
    grad_right_proj = (grad_hidden * left_proj).astype(jnp.bfloat16)
    grad_left = jnp.dot(second_flat.T, grad_left_proj, preferred_element_type=jnp.float32)
    grad_right = jnp.dot(second_flat.T, grad_right_proj, preferred_element_type=jnp.float32)
    left_blocks = grad_left_proj.reshape(block_len, seq_count, ffn_width)
    right_blocks = grad_right_proj.reshape(block_len, seq_count, ffn_width)
    row_count = shard_len * lax.axis_size("tp")
    left_rows = left_blocks.reshape(row_count * seq_count, ffn_width)
    right_rows = right_blocks.reshape(row_count * seq_count, ffn_width)
    summed = jnp.dot(left_rows, full_left.T, preferred_element_type=jnp.float32) + jnp.dot(
        right_rows, full_right.T, preferred_element_type=jnp.float32
    )
    grad_second = lax.psum_scatter(
        summed.reshape(row_count, seq_count, model_width), "tp", scatter_dimension=0, tiled=True
    )
    grad_residual = cotangent.astype(jnp.float32) + norm_backward(residual, grad_second)
    branch_low = grad_residual.astype(jnp.bfloat16)
    grad_branch = lax.all_gather(branch_low, "tp", axis=0, tiled=True).reshape(
        total_rows, model_width
    )
    grad_wout = jnp.dot(
        mixed_heads.reshape(total_rows, local_width).T,
        grad_branch,
        preferred_element_type=jnp.float32,
    )
    grad_mixed = jnp.dot(grad_branch, full_out.T, preferred_element_type=jnp.float32).reshape(
        head_shape
    )
    grad_gate_proj = (
        (grad_mixed * attended_norm * gate_value * (1.0 - gate_value))
        .astype(jnp.bfloat16)
        .reshape(total_rows, local_width)
    )
    grad_attended = norm_backward(attended, grad_mixed * gate_value, HEAD_FLOOR).astype(
        jnp.bfloat16
    )
    grad_weights = jnp.einsum(
        "tbhd,sbhd->bhts", grad_attended, values_low, preferred_element_type=jnp.float32
    )
    grad_scores = (grad_weights * decay_grid).astype(jnp.bfloat16)
    grad_queries = jnp.einsum(
        "bhts,sbhd->tbhd", grad_scores, keys_low, preferred_element_type=jnp.float32
    )
    grad_queries = (
        grad_queries
        + jnp.einsum(
            "tbhe,bhde->tbhd", grad_attended, state_low, preferred_element_type=jnp.float32
        )
        * inflow[..., None]
    )
    grad_keys = jnp.einsum(
        "bhts,tbhd->sbhd", grad_scores, queries, preferred_element_type=jnp.float32
    )
    grad_values = jnp.einsum(
        "bhts,tbhd->sbhd", weights_low, grad_attended, preferred_element_type=jnp.float32
    )
    weighted_queries = queries.astype(jnp.float32) * inflow[..., None]
    grad_prior_local = jnp.einsum(
        "tbhd,tbhe->bhde", weighted_queries, grad_attended.astype(jnp.float32), precision=lax.Precision.HIGHEST
    )
    link_decay = jnp.where((first_seg == prior_last)[:, None], span_decay, 0.0)
    back_identity = (
        jnp.ones((seq_count, head_count), jnp.float32),
        jnp.zeros((seq_count, head_count, DH, DH), jnp.float32),
    )
    grad_update = entering_2((link_decay, grad_prior_local), "ctx", chain_backward, back_identity)[
        1
    ]
    grad_values = grad_values + jnp.einsum(
        "tbhd,bhde->tbhe", keys_end.astype(jnp.float32), grad_update, precision=lax.Precision.HIGHEST
    )
    grad_keys = (
        grad_keys
        + jnp.einsum(
            "tbhe,bhde->tbhd", values_low.astype(jnp.float32), grad_update, precision=lax.Precision.HIGHEST
        )
        * end_weight[..., None]
    )
    grad_query_proj = (
        (grad_queries * silu_grad(proj_query).reshape(head_shape))
        .astype(jnp.bfloat16)
        .reshape(total_rows, local_width)
    )
    grad_key_proj = (
        (grad_keys * silu_grad(proj_key).reshape(head_shape))
        .astype(jnp.bfloat16)
        .reshape(total_rows, local_width)
    )
    grad_value_proj = grad_values.astype(jnp.bfloat16).reshape(total_rows, local_width)
    grad_wquery = jnp.dot(normed_flat.T, grad_query_proj, preferred_element_type=jnp.float32)
    grad_wkey = jnp.dot(normed_flat.T, grad_key_proj, preferred_element_type=jnp.float32)
    grad_wvalue = jnp.dot(normed_flat.T, grad_value_proj, preferred_element_type=jnp.float32)
    grad_wgate = jnp.dot(normed_flat.T, grad_gate_proj, preferred_element_type=jnp.float32)
    query_blocks = grad_query_proj.reshape(block_len, seq_count, local_width)
    key_blocks = grad_key_proj.reshape(block_len, seq_count, local_width)
    value_blocks = grad_value_proj.reshape(block_len, seq_count, local_width)
    gate_blocks = grad_gate_proj.reshape(block_len, seq_count, local_width)
    row_count = shard_len * lax.axis_size("tp")
    summed = jnp.zeros((row_count * seq_count, model_width), jnp.float32)
    for grad_blocks, weight_full in (
        (query_blocks, full_query),
        (key_blocks, full_key),
        (value_blocks, full_value),
        (gate_blocks, full_gate),
    ):
        piece_rows = grad_blocks.reshape(row_count * seq_count, local_width)
        summed = summed + jnp.dot(piece_rows, weight_full.T, preferred_element_type=jnp.float32)
    grad_normed = lax.psum_scatter(
        summed.reshape(row_count, seq_count, model_width).astype(jnp.bfloat16),
        "tp",
        scatter_dimension=0,
        tiled=True,
    ).astype(jnp.float32)
    grad_tokens = grad_residual + norm_backward(tok_float, grad_normed)
    every_grad = (
        lax.psum_scatter(grad_wquery, ("fsdp", "ctx"), scatter_dimension=0, tiled=True),
        lax.psum_scatter(grad_wkey, ("fsdp", "ctx"), scatter_dimension=0, tiled=True),
        lax.psum_scatter(grad_wvalue, ("fsdp", "ctx"), scatter_dimension=0, tiled=True),
        lax.psum_scatter(grad_wgate, ("fsdp", "ctx"), scatter_dimension=0, tiled=True),
        lax.psum_scatter(grad_wout, ("fsdp", "ctx"), scatter_dimension=1, tiled=True),
        lax.psum_scatter(grad_left, ("fsdp", "ctx"), scatter_dimension=0, tiled=True),
        lax.psum_scatter(grad_right, ("fsdp", "ctx"), scatter_dimension=0, tiled=True),
        lax.psum_scatter(grad_down, ("fsdp", "ctx"), scatter_dimension=1, tiled=True),
    )
    return (
        output,
        grad_tokens,
        every_grad[0],
        every_grad[1],
        every_grad[2],
        every_grad[3],
        every_grad[4],
        every_grad[5],
        every_grad[6],
        every_grad[7],
    )


def paired(
    tokens, segment_ids, decay_rate, w_query, w_key, w_value, w_gate, w_out,
    glu_left, glu_right, glu_down, cotangent,
):
    tok, cot = tokens.transpose(1, 0, 2), cotangent.transpose(1, 0, 2)
    (
        n1, n2, pkq, pg, qkv, pm, att, mix, sb, wb, wo, ids, rate,
        dr, dx1, fs, fo, dpr, g_down, left_acc,
    ) = call_forward(
        decay_rate, tok, cot, segment_ids, (w_query, w_key, w_value, w_gate), w_out,
        glu_left.T, glu_right.T, glu_down,
    )
    out, g_tok, g_q, g_k, g_v, g_g, g_o, g_left, g_right = call_backward(
        ids, rate, dr, wo, att, pg, qkv, left_acc, n2, dpr, pm, sb, pkq, n1, mix, wb, fs, fo, dx1, tok
    )
    return (
        out.transpose(1, 0, 2), g_tok.transpose(1, 0, 2),
        g_q, g_k, g_v, g_g, g_o, g_left.T, g_right.T, g_down,
    )


def solution(mesh):
    in_specs = (
        P(("ctx", "tp"), "fsdp", None),
        P("fsdp", "ctx"),
        P("tp"),
        P(("fsdp", "ctx"), "tp"),
        P(("fsdp", "ctx"), "tp"),
        P(("fsdp", "ctx"), "tp"),
        P(("fsdp", "ctx"), "tp"),
        P("tp", ("fsdp", "ctx")),
        P(("fsdp", "ctx"), "tp"),
        P(("fsdp", "ctx"), "tp"),
        P("tp", ("fsdp", "ctx")),
        P(("ctx", "tp"), "fsdp", None),
    )
    out_specs = (
        P(("ctx", "tp"), "fsdp", None),
        P(("ctx", "tp"), "fsdp", None),
        P(("fsdp", "ctx"), "tp"),
        P(("fsdp", "ctx"), "tp"),
        P(("fsdp", "ctx"), "tp"),
        P(("fsdp", "ctx"), "tp"),
        P("tp", ("fsdp", "ctx")),
        P(("fsdp", "ctx"), "tp"),
        P(("fsdp", "ctx"), "tp"),
        P("tp", ("fsdp", "ctx")),
    )
    sizes = tuple(mesh.shape[a] for a in ("fsdp", "ctx", "tp"))
    body = paired if sizes == (2, 4, 4) else shards
    return jax.shard_map(body, mesh=mesh, in_specs=in_specs, out_specs=out_specs, check_vma=False)
```

```python
import functools

import jax
import jax.numpy as jnp
from jax import lax
from jax.experimental import pallas as pl
from jax.experimental.pallas import tpu as pltpu
from jax.sharding import PartitionSpec as P

DH = 128
CH = 256
EPSILON = 1e-06
HEAD_FLOOR = 1.0
BF = jnp.bfloat16
F32 = jnp.float32
MESH = pl.DeviceIdType.MESH
MIB = 1 << 20


def dg(a, b, ca, cb):
    return lax.dot_general(a, b, (((ca,), (cb,)), ((), ())), preferred_element_type=F32)


def rows128(i):
    return pl.ds(pl.multiple_of(i * 128, 128), 128)


def cols256(i):
    return pl.ds(pl.multiple_of(i * 256, 256), 256)


def inverse_norm(v, floor_value):
    return lax.rsqrt(jnp.mean(v * v, axis=-1, keepdims=True) + floor_value)


def norm_slope(v, d, floor_value):
    inv = inverse_norm(v, floor_value)
    inner = jnp.mean(d * v, axis=-1, keepdims=True)
    return inv * (d - v * (inner * inv * inv))


class Place:
    def __init__(self):
        x, k, z = lax.axis_index("fsdp"), lax.axis_index("ctx"), lax.axis_index("tp")
        self.x, self.k, self.z = x, k, z
        self.y, self.c = k // 2, k % 2
        self.t, self.zh = z % 2, z // 2
        self.r = x * 4 + k
        self.peer = {
            "X": (1 - x, k, z),
            "Y": (x, (k + 2) % 4, z),
            "C": (x, k + 1 - 2 * self.c, z),
            "P": (x, k, z + 1 - 2 * self.t),
            "Q": (x, k, (z + 2) % 4),
        }

    def flip(self, r, axis):
        if axis == "X":
            return (r + 4) % 8
        if axis == "Y":
            return r + 2 - 4 * ((r // 2) % 2)
        return r + 1 - 2 * (r % 2)

    def greet(self):
        bar = pltpu.get_barrier_semaphore()
        for peer in self.peer.values():
            pl.semaphore_signal(bar, inc=1, device_id=peer, device_id_type=MESH)

    def meet(self):
        pl.semaphore_wait(pltpu.get_barrier_semaphore(), len(self.peer))


class Links:
    def __init__(self, place, send, recv, local):
        self.place, self.send, self.recv, self.local = place, send, recv, local
        self.n = self.m = 0
        self.sent, self.kept = [], []

    def remote(self, src, dst, peer):
        cp = pltpu.make_async_remote_copy(
            src_ref=src,
            dst_ref=dst,
            send_sem=self.send.at[self.n],
            recv_sem=self.recv.at[self.n],
            device_id=self.place.peer[peer],
            device_id_type=MESH,
        )
        self.n += 1
        return cp

    def go(self, src, dst, peer):
        cp = self.remote(src, dst, peer)
        cp.start()
        self.sent.append(cp)
        return cp

    def keep(self, src, dst):
        cp = pltpu.make_async_copy(src, dst, self.local.at[self.m])
        self.m += 1
        cp.start()
        self.kept.append(cp)
        return cp

    def fetch(self, src, dst):
        cp = pltpu.make_async_copy(src, dst, self.local.at[self.m])
        self.m += 1
        cp.start()
        return cp

    def gone(self, cp):
        cp.wait_send()
        self.sent = [other for other in self.sent if other is not cp]

    def written(self, cp):
        cp.wait()
        self.kept = [other for other in self.kept if other is not cp]

    def drain(self):
        for cp in self.sent:
            cp.wait_send()
        for cp in self.kept:
            cp.wait()


class Gather:
    def __init__(self, links, order, view, own=None):
        self.links, self.view = links, view
        pc = links.place
        self.pc, self.own = pc, own
        self.first, self.second = ("X", "Y") if order == "A" else ("Y", "X")
        self.rf = pc.flip(pc.r, self.first)
        self.rs = pc.flip(pc.r, self.second)
        self.rfs = pc.flip(self.rf, self.second)
        self.cps = [{}, {}]

    def put(self, slot, name, r, peer, src=None):
        b = self.pc.zh if slot == 0 else 1 - self.pc.zh
        src = self.view(b, r) if src is None else src
        self.cps[slot][name] = self.links.go(src, self.view(b, r), peer)

    def launch(self, slot, src=None):
        r = self.pc.r
        self.put(slot, "f", r, self.first, src)
        self.put(slot, "sa", r, self.second, src)
        self.put(slot, "c0", r, "C", src)

    def cross(self):
        self.put(0, "z", self.pc.r, "Q", self.own)

    def start(self):
        self.launch(0, self.own)
        self.cross()

    def other(self):
        self.cps[0]["z"].wait_recv()
        self.launch(1)

    def step1(self, slot):
        self.cps[slot]["f"].wait_recv()
        self.put(slot, "sb", self.rf, self.second)
        self.put(slot, "c1", self.rf, "C")

    def step2(self, slot):
        self.cps[slot]["sa"].wait_recv()
        self.put(slot, "c2", self.rs, "C")
        self.cps[slot]["sb"].wait_recv()
        self.put(slot, "c3", self.rfs, "C")

    def step3(self, slot):
        for name in ("c0", "c1", "c2", "c3"):
            self.cps[slot][name].wait_recv()


def last_id(ids, kk, half, s):
    at = 255 + 256 * half
    return ids[kk, s : s + 1, at : at + 1]


def prior_id(pc, ids, s):
    before = jnp.where(pc.zh == 1, last_id(ids, pc.k, 0, s), last_id(ids, (pc.k + 3) % 4, 1, s))
    return jnp.where((pc.zh == 1) | (pc.k > 0), before, -1.0)


def same(a, b):
    return jnp.where(a == b, 1.0, 0.0)


def fill_decay(rate, grid, wend, gin):
    ti = lax.broadcasted_iota(jnp.int32, (CH, CH), 0).astype(F32)
    si = lax.broadcasted_iota(jnp.int32, (CH, CH), 1).astype(F32)
    dist = ti - si
    pos = lax.broadcasted_iota(jnp.int32, (CH, DH), 0).astype(F32)

    def head(h, _):
        lane = rate[h, 0:1, :]
        both = jnp.concatenate([lane, lane], axis=1)
        grid[h] = jnp.where(dist >= 0.0, jnp.exp(-both * jnp.maximum(dist, 0.0)), 0.0)
        wend[h] = jnp.exp(-lane * (CH - 1.0 - pos))
        gin[h] = jnp.exp(-lane * (pos + 1.0))
        return 0

    lax.fori_loop(0, 4, head, 0)


def fill_masks(pc, ids, mask, endf, inf):
    for s in range(2):
        row = ids[pc.k, s : s + 1, pl.ds(pl.multiple_of(pc.zh * CH, CH), CH)]
        along = jnp.broadcast_to(row, (CH, CH))
        down = along.T
        mask[s] = same(along, down)
        col = down[:, :DH]
        endf[s] = same(col, jnp.broadcast_to(row[:, CH - 1 : CH], (CH, DH)))
        inf[s] = same(col, jnp.broadcast_to(prior_id(pc, ids, s), (CH, DH)))


def forward_factors(pc, ids, rate, fac):
    for s in range(2):
        prior = prior_id(pc, ids, s)
        low = last_id(ids, pc.y * 2, 1, s)
        f1 = same(last_id(ids, pc.k, 0, s), last_id(ids, pc.k, 1, s))
        f2 = same(low, last_id(ids, pc.y * 2 + 1, 1, s))
        p2 = same(low, prior) * jnp.where(pc.c == 1, 1.0, 0.0)
        p3 = same(last_id(ids, 1, 1, s), prior) * jnp.where(pc.y == 1, 1.0, 0.0)
        d2 = pc.zh.astype(F32) * CH
        d3 = (2 * pc.c + pc.zh).astype(F32) * CH
        for h in range(4):
            one = rate[h, 0:1, :]
            unit = jnp.ones_like(one)
            l1, l2 = jnp.exp(-CH * one) * f1, jnp.exp(-2.0 * CH * one) * f2
            fac[s, h, 0:1, :] = jnp.where(pc.zh == 1, unit, l1)
            fac[s, h, 1:2, :] = jnp.where(pc.zh == 1, l1, unit)
            fac[s, h, 2:3, :] = jnp.where(pc.zh == 1, unit, 0.0 * unit)
            fac[s, h, 3:4, :] = jnp.where(pc.c == 1, unit, l2)
            fac[s, h, 4:5, :] = jnp.where(pc.c == 1, l2, unit)
            fac[s, h, 5:6, :] = jnp.exp(-d2 * one) * p2
            fac[s, h, 6:7, :] = jnp.exp(-d3 * one) * p3


def backward_factors(pc, ids, rate, fac):
    for s in range(2):
        low = last_id(ids, pc.y * 2, 1, s)
        prev_k = jnp.where(pc.k > 0, last_id(ids, (pc.k + 3) % 4, 1, s), -1.0)
        prev_y = jnp.where(pc.y > 0, last_id(ids, (pc.y * 2 + 3) % 4, 1, s), -1.0)
        here = jnp.where(pc.zh == 1, last_id(ids, pc.k, 1, s), last_id(ids, pc.k, 0, s))
        f1, f2 = same(prev_k, last_id(ids, pc.k, 0, s)), same(prev_y, low)
        p2 = same(here, low) * jnp.where(pc.c == 0, 1.0, 0.0)
        p3 = same(here, last_id(ids, 1, 1, s)) * jnp.where(pc.y == 0, 1.0, 0.0)
        d2 = (1 - pc.zh).astype(F32) * CH
        d3 = (2 * (1 - pc.c) + (1 - pc.zh)).astype(F32) * CH
        for h in range(4):
            one = rate[h, 0:1, :]
            unit = jnp.ones_like(one)
            l1, l2 = jnp.exp(-CH * one) * f1, jnp.exp(-2.0 * CH * one) * f2
            fac[s, h, 0:1, :] = jnp.where(pc.zh == 0, unit, l1)
            fac[s, h, 1:2, :] = jnp.where(pc.zh == 0, l1, unit)
            fac[s, h, 2:3, :] = jnp.where(pc.zh == 0, unit, 0.0 * unit)
            fac[s, h, 3:4, :] = jnp.where(pc.c == 0, unit, l2)
            fac[s, h, 4:5, :] = jnp.where(pc.c == 0, l2, unit)
            fac[s, h, 5:6, :] = jnp.exp(-d2 * one) * p2
            fac[s, h, 6:7, :] = jnp.exp(-d3 * one) * p3


def pair_sum(fac, s, own, got, total, prefix):
    for h in range(4):
        g = got[s, h].astype(F32)
        tot = fac[s, h, 0:1, :] * own[s, h] + fac[s, h, 1:2, :] * g
        prefix[s, h] = fac[s, h, 2:3, :] * g
        own[s, h] = tot
        total[s, h] = tot.astype(BF)


def quad_sum(fac, s, own, got, total, prefix):
    for h in range(4):
        g = got[s, h].astype(F32)
        total[s, h] = (fac[s, h, 3:4, :] * own[s, h] + fac[s, h, 4:5, :] * g).astype(BF)
        prefix[s, h] = prefix[s, h] + fac[s, h, 5:6, :] * g


class Scatter:
    def __init__(self, links, kind, bufs):
        self.links, self.kind = links, kind
        pc = links.place
        self.pc = pc
        self.acc, self.sc, self.rc, self.sf, self.rf, self.ss, self.rs, self.sz, self.rz = bufs
        self.c_cp, self.f_cp, self.s_cp = {}, {}, {}
        self.last = 2 * pc.x + pc.y

    def way(self, b):
        x, y = self.pc.x, self.pc.y
        if b == 0:
            return "X", "Y", x, y, lambda f, m: 2 * f + m
        return "Y", "X", y, x, lambda f, m: 2 * m + f

    def core_stage(self, b, product, after=None):
        if after is not None:
            self.links.gone(after.c_cp[b])

        def pair(i, _):
            p = product(b, i)
            lo, hi = (p[:128], p[128:]) if self.kind == "rows" else (p[:, :128], p[:, 128:])
            self.sc[b, i] = jnp.where(self.pc.c == 0, hi, lo).astype(BF)
            self.acc[b, i] = jnp.where(self.pc.c == 0, lo, hi).astype(self.acc.dtype)
            return 0

        lax.fori_loop(0, 4, pair, 0)
        self.c_cp[b] = self.links.go(self.sc.at[b], self.rc.at[b], "C")

    def add(self, b, i, got):
        return self.acc[b, i].astype(F32) + got.astype(F32)

    def first_stage(self, b, joined=False):
        first, _, fv, _, at = self.way(b)
        if not joined:
            self.c_cp[b].wait_recv()
        for m in range(2):
            i = at(1 - fv, m)
            self.sf[b, m] = (self.acc[b, i] if joined else self.add(b, i, self.rc[b, i])).astype(BF)
        self.f_cp[b] = self.links.go(self.sf.at[b], self.rf.at[b], first)
        if not joined:
            for m in range(2):
                i = at(fv, m)
                self.acc[b, i] = self.add(b, i, self.rc[b, i]).astype(self.acc.dtype)

    def join(self, b):
        self.c_cp[b].wait_recv()
        for i in range(4):
            self.acc[b, i] = self.add(b, i, self.rc[b, i]).astype(self.acc.dtype)

    def second_stage(self, b):
        _, second, fv, sv, at = self.way(b)
        self.f_cp[b].wait_recv()
        self.ss[b] = self.add(b, at(fv, 1 - sv), self.rf[b, 1 - sv]).astype(BF)
        self.s_cp[b] = self.links.go(self.ss.at[b], self.rs.at[b], second)
        self.acc[b, self.last] = self.add(b, self.last, self.rf[b, sv]).astype(self.acc.dtype)

    def plane_stage(self):
        zh = self.pc.zh
        for b in range(2):
            self.s_cp[b].wait_recv()
        self.sz[...] = self.add(1 - zh, self.last, self.rs[1 - zh]).astype(BF)
        if self.rz is not None:
            self.z_cp = self.links.go(self.sz, self.rz, "Q")

    def near(self):
        zh = self.pc.zh
        return self.add(zh, self.last, self.rs[zh])

    def total(self):
        self.z_cp.wait_recv()
        return self.near() + self.rz[...].astype(F32)


def scatter_bufs(slab, acc=F32, core=2):
    vm = pltpu.VMEM
    return [vm((2, 4) + slab, acc)] + [vm((2, 4) + slab, BF)] * core + [
        vm((2, 2) + slab, BF), vm((2, 2) + slab, BF), vm((2,) + slab, BF), vm((2,) + slab, BF),
        vm(slab, BF), vm(slab, BF),
    ]


def forward_and_glu(
    rate_in, tok, cot, seg, wq, wk, wv, wg, wo_in, gl_in, gr_in, gd_in,
    n1_o, n2_o, pkq_o, pg_o, qkv_o, p_o, att_o, mix_o, sb_o, w_o, wo_o, ids_o, rate_o,
    dr_o, dx1_o, fs_o, fo_o, dpr_o, gdown_o, dsz_o, left_o,
    xb, n1, ct, n2, x1, pg, qkv, pm, att, mix, sb, wb, wo, gl, gr, gd,
    ids, rate, fac, grid, wend, gin, mask, endf, inf, uf, us, ur, ts, tr, vs, vr, pf,
    br_s, br_r, dn_r, dn, hid, dpl, dpr, tmp, dr, fs, fo, gdown, left_acc,
    *rest,
):
    down_b, left_b = rest[:8] + (None,), (left_acc, rest[1], rest[8]) + (None,) * 6
    send, recv, local = rest[9:]
    pc = Place()
    pc.greet()
    ln = Links(pc, send, recv, local)
    own, r = pc.zh, pc.r
    far_b = 1 - own

    def mine(s):
        return pl.ds(pl.multiple_of(s * CH + pc.t * 128, 128), 128)

    def theirs(s):
        return pl.ds(pl.multiple_of(s * CH + (1 - pc.t) * 128, 128), 128)

    def wview(i):
        return lambda b, rr: wb.at[i, b, rows128(rr), :]

    def gview(w):
        return lambda b, rr: w.at[b, rows128(rr), :]

    for hh in range(2):
        rate[own * 2 + hh] = jnp.full((8, DH), rate_in[hh], F32)
    for s in range(2):
        xb[mine(s), :] = tok[s]
        ct[mine(s), :] = cot[s]
    for i, w in enumerate((wk, wv, wq, wg)):
        wb[i, own, rows128(r), :] = w[...].astype(BF)
    wo[own, rows128(r), :] = wo_in[...].T.astype(BF)
    ids[pc.k] = jnp.zeros((8, 512), F32)
    ids[pc.k, 0:2, :] = seg[...].astype(F32)
    pc.meet()

    g_o = Gather(ln, "A", gview(wo))
    qkvgo = [Gather(ln, "AB"[i % 2], wview(i)) for i in range(4)] + [g_o]
    g_l, g_r, g_d = Gather(ln, "A", gview(gl)), Gather(ln, "B", gview(gr)), Gather(ln, "A", gview(gd))
    rate_cp = ln.go(rate.at[pl.ds(own * 2, 2)], rate.at[pl.ds(own * 2, 2)], "Q")
    ids_y = ln.go(ids.at[pc.k], ids.at[pc.k], "Y")
    ids_c = ln.go(ids.at[pc.k], ids.at[pc.k], "C")
    for g in qkvgo[:2]:
        g.cross()
        g.launch(0)
    x_cp = [ln.go(xb.at[mine(s)], xb.at[mine(s)], "P") for s in range(2)]
    for g in qkvgo[2:]:
        g.launch(0)
    for g in qkvgo[2:]:
        g.cross()
    for s in range(2):
        xf = tok[s].astype(F32)
        n1[mine(s), :] = (xf * inverse_norm(xf, EPSILON)).astype(BF)
    for w, w_in in ((gl, gl_in), (gr, gr_in), (gd, gd_in)):
        w[own, rows128(r), :] = w_in[...].T.astype(BF)
    kf = (pc.k + 2) % 4
    ids_y.wait_recv()
    ids_f = ln.go(ids.at[kf], ids.at[kf], "C")
    for g in qkvgo:
        g.step1(0)
    rate_cp.wait_recv()
    fill_decay(rate, grid, wend, gin)
    for g in qkvgo[:2]:
        g.other()
    for g in qkvgo:
        g.step2(0)
    ids_c.wait_recv()
    ids_f.wait_recv()
    fill_masks(pc, ids, mask, endf, inf)
    forward_factors(pc, ids, rate, fac)
    for g in qkvgo[:2]:
        g.step1(1)
    g_l.launch(0)
    g_r.launch(0)
    for g in qkvgo[:2]:
        g.step2(1)
    for s in range(2):
        x_cp[s].wait_recv()
        xf = xb[theirs(s), :].astype(F32)
        n1[theirs(s), :] = (xf * inverse_norm(xf, EPSILON)).astype(BF)

    def project(i):
        for slot in range(2):
            qkvgo[i].step3(slot)

        def block(b, _):
            p = dg(n1[...], wb[i, b], 1, 0)
            if i == 0:
                x1[:, cols256(b)] = p
            elif i == 2:
                x1[:, cols256(2 + b)] = p
            elif i == 3:
                pg[:, cols256(b)] = p
            if i < 3:
                a = (p if i == 1 else p * jax.nn.sigmoid(p)).astype(BF)
                qkv[i, b * 2] = a[:, :DH]
                qkv[i, b * 2 + 1] = a[:, DH:]
            return 0

        lax.fori_loop(0, 2, block, 0)

    project(0)
    project(1)
    u_cp = []
    for s in range(2):
        rs_ = pl.ds(s * CH, CH)

        def state(h, _):
            kw = (qkv[0, h, rs_, :].astype(F32) * (wend[h] * endf[s])).astype(BF)
            u = dg(kw, qkv[1, h, rs_, :], 0, 0)
            uf[s, h] = u
            us[s, h] = u.astype(BF)
            return 0

        lax.fori_loop(0, 4, state, 0)
        u_cp.append(ln.go(us.at[s], ur.at[s], "Q"))
    ct_cp = [ln.go(ct.at[mine(0)], ct.at[mine(0)], "P")]
    for g in qkvgo[2:]:
        g.other()
    g_l.cross()
    g_r.cross()
    g_l.step1(0)
    g_r.step1(0)
    for g in qkvgo[2:]:
        g.step1(1)
    for g in qkvgo[2:]:
        g.step2(1)
    project(2)
    for s in range(2):
        rs_ = pl.ds(s * CH, CH)

        def inside(h, _):
            sc = dg(qkv[2, h, rs_, :], qkv[0, h, rs_, :], 1, 1)
            p = (sc * grid[h] * mask[s]).astype(BF)
            pm[s, h] = p
            att[h, rs_, :] = dg(p, qkv[1, h, rs_, :], 1, 0)
            return 0

        lax.fori_loop(0, 4, inside, 0)
    project(3)
    g_o.step3(0)
    g_o.step3(1)
    pkq_cp = ln.keep(x1, pkq_o)
    for i in range(4):
        ln.keep(wb.at[i], w_o.at[i])
    ln.keep(n1, n1_o)
    ln.keep(pg, pg_o)
    ln.keep(qkv, qkv_o)
    ln.keep(ids, ids_o)
    ln.keep(rate, rate_o)
    ln.keep(pm, p_o)
    ln.keep(wo, wo_o)
    g_l.step2(0)
    g_r.step2(0)
    g_d.launch(0)

    v_cp = []
    for s in range(2):
        u_cp[s].wait_recv()
        pair_sum(fac, s, uf, ur, ts, pf)
        t_cp = ln.go(ts.at[s], tr.at[s], "C")
        t_cp.wait_recv()
        quad_sum(fac, s, uf, tr, vs, pf)
        v_cp.append(ln.go(vs.at[s], vr.at[s], "Y"))
    ln.written(pkq_cp)
    b_cp = []
    for s in range(2):
        v_cp[s].wait_recv()
        rs_ = pl.ds(s * CH, CH)

        def enter(h, _):
            low_st = (pf[s, h] + fac[s, h, 6:7, :] * vr[s, h].astype(F32)).astype(BF)
            sb[s, h] = low_st
            o = att[h, rs_, :] + (gin[h] * inf[s]) * dg(qkv[2, h, rs_, :], low_st, 1, 0)
            att[h, rs_, :] = o
            on = o * inverse_norm(o, HEAD_FLOOR)
            mix[rs_, rows128(h)] = (on * jax.nn.sigmoid(pg[rs_, rows128(h)])).astype(BF)
            return 0

        lax.fori_loop(0, 4, enter, 0)
        part = dg(mix[rs_, :256], wo[0], 1, 1) + dg(mix[rs_, 256:], wo[1], 1, 1)
        br_s[rs_, :] = part.astype(BF)
        b_cp.append(ln.go(br_s.at[rs_], br_r.at[rs_], "P"))
        x1[rs_, :] = xb[rs_, :].astype(F32) + part
        if s == 0:
            g_d.cross()
            g_d.step1(0)
            g_l.other()
    ln.keep(att, att_o)
    ln.keep(mix, mix_o)
    ln.keep(sb, sb_o)
    ct_cp.append(ln.go(ct.at[mine(1)], ct.at[mine(1)], "P"))
    g_r.other()
    g_d.step2(0)
    g_l.step1(1)
    g_r.step1(1)
    for g in (g_l, g_r, g_d):
        g.step3(0)
    g_l.step2(1)
    g_r.step2(1)
    d_cp = []

    def units(s, b):
        rs_ = pl.ds(s * CH, CH)
        a = dg(n2[rs_, :], gl[b], 1, 0)
        c = dg(n2[rs_, :], gr[b], 1, 0)
        hid[b, rs_, :] = (a * c).astype(BF)
        dh = dg(ct[rs_, :], gd[b], 1, 0)
        dpl[b, rs_, :] = (dh * c).astype(BF)
        dpr[b, rs_, :] = (dh * a).astype(BF)

    for s in range(2):
        rs_ = pl.ds(s * CH, CH)
        b_cp[s].wait_recv()
        v = x1[rs_, :] + br_r[rs_, :].astype(F32)
        x1[rs_, :] = v
        n2[rs_, :] = (v * inverse_norm(v, EPSILON)).astype(BF)
        if s == 0:
            g_d.other()
        ct_cp[s].wait_recv()
        units(s, own)
        if s == 0:
            g_d.step1(1)
            g_l.step3(1)
            g_r.step3(1)
            g_d.step2(1)
            g_d.step3(1)
        units(s, far_b)
        part = (
            dg(dpl[0, rs_, :], gl[0], 1, 1) + dg(dpr[0, rs_, :], gr[0], 1, 1)
            + dg(dpl[1, rs_, :], gl[1], 1, 1) + dg(dpr[1, rs_, :], gr[1], 1, 1)
        )
        dn[rs_, :] = part
        ln.gone(b_cp[s])
        br_s[rs_, :] = part.astype(BF)
        d_cp.append(ln.go(br_s.at[rs_], dn_r.at[rs_], "P"))
    ln.keep(n2, n2_o)
    ln.keep(dpr, dpr_o)

    down = Scatter(ln, "cols", down_b)
    left = Scatter(ln, "cols", left_b)
    for b in range(2):
        down.core_stage(b, lambda b, i: dg(hid[b], ct[:, cols256(i)], 0, 0))

    def turn(s):
        rs_ = pl.ds(s * CH, CH)
        d_cp[s].wait_recv()
        g = ct[rs_, :].astype(F32) + norm_slope(x1[rs_, :], dn[rs_, :] + dn_r[rs_, :].astype(F32), EPSILON)
        dn[rs_, :] = g
        dr[rs_, :] = g.astype(BF)
        ln.keep(dr.at[rs_], dr_o.at[rs_])
        ln.keep(dn.at[mine(s)], dx1_o.at[s])

    def feed(s):
        rs_ = pl.ds(s * CH, CH)
        tmp[...] = dg(hid[0, rs_, :], gd[0], 1, 1) + dg(hid[1, rs_, :], gd[1], 1, 1)
        fs[s] = tmp[rows128(1 - pc.t), :].astype(BF)
        fo[s] = x1[mine(s), :] + tmp[rows128(pc.t), :]

    feed(0)
    for b in range(2):
        down.first_stage(b)
    for b in range(2):
        left.core_stage(b, lambda b, i: dg(dpl[b], n2[:, cols256(i)], 0, 0), down)
    turn(0)
    for b in range(2):
        down.second_stage(b)
    feed(1)
    ln.keep(fs, fs_o)
    ln.keep(fo, fo_o)
    for b in range(2):
        left.join(b)
    ln.keep(left.acc, left_o)
    down.plane_stage()
    ln.keep(down.sz, dsz_o)
    gdown[...] = down.near()
    ln.keep(gdown, gdown_o)
    turn(1)
    ln.drain()


def call_forward(rate, tok, cot, seg, ws, wo, gl, gr, gd):
    sd, vm = jax.ShapeDtypeStruct, pltpu.VMEM
    ff = gl.shape[0]
    act = (512, 1024)
    st = (2, 4, DH, DH)
    outs = [
        sd(act, BF), sd(act, BF), sd(act, F32), sd((512, 512), F32), sd((3, 4, 512, DH), BF),
        sd((2, 4, CH, CH), BF), sd((4, 512, DH), F32), sd((512, 512), BF), sd(st, BF),
        sd((4, 2, 1024, 256), BF), sd((2, 1024, 256), BF), sd((4, 8, 512), F32), sd((4, 8, DH), F32),
        sd(act, BF), sd((2, 128, 1024), F32), sd((2, 128, 1024), BF), sd((2, 128, 1024), F32),
        sd((2, 512, ff), BF), sd((ff, 128), F32), sd((ff, 128), BF), sd((2, 4, ff, 128), BF),
    ]
    scratch = [
        vm(act, BF), vm(act, BF), vm(act, BF), vm(act, BF), vm(act, F32), vm((512, 512), F32),
        vm((3, 4, 512, DH), BF), vm((2, 4, CH, CH), BF), vm((4, 512, DH), F32), vm((512, 512), BF),
        vm(st, BF), vm((4, 2, 1024, 256), BF), vm((2, 1024, 256), BF),
        vm((2, 1024, ff), BF), vm((2, 1024, ff), BF), vm((2, 1024, ff), BF),
        vm((4, 8, 512), F32), vm((4, 8, DH), F32), vm((2, 4, 8, DH), F32),
        vm((4, CH, CH), F32), vm((4, CH, DH), F32), vm((4, CH, DH), F32),
        vm((2, CH, CH), F32), vm((2, CH, DH), F32), vm((2, CH, DH), F32),
        vm(st, F32), vm(st, BF), vm(st, BF), vm(st, BF), vm(st, BF), vm(st, BF), vm(st, BF), vm(st, F32),
        vm(act, BF), vm(act, BF), vm(act, BF), vm(act, F32),
        vm((2, 512, ff), BF), vm((2, 512, ff), BF), vm((2, 512, ff), BF),
        vm((CH, 1024), F32), vm(act, BF), vm((2, 128, 1024), BF), vm((2, 128, 1024), F32), vm((ff, 128), F32), vm((2, 4, ff, 128), BF),
        *scatter_bufs((ff, 128), BF)[:-1], vm((2, 4, ff, 128), BF),
        pltpu.SemaphoreType.DMA((160,)), pltpu.SemaphoreType.DMA((160,)), pltpu.SemaphoreType.DMA((40,)),
    ]
    vin = pl.BlockSpec(memory_space=pltpu.VMEM)
    return pl.pallas_call(
        forward_and_glu,
        out_shape=outs,
        in_specs=[pl.BlockSpec(memory_space=pltpu.SMEM)] + [vin] * 11,
        out_specs=[pl.BlockSpec(memory_space=pl.ANY)] * len(outs),
        scratch_shapes=scratch,
        compiler_params=pltpu.CompilerParams(
            collective_id=0, has_side_effects=True, vmem_limit_bytes=63 * MIB
        ),
        name="forward_and_glu",
    )(rate, tok, cot, seg, *ws, wo, gl, gr, gd)


def silu_slope(v):
    g = jax.nn.sigmoid(v)
    return g * (1.0 + v * (1.0 - g))


N_BACK_IN = 22


def cut_bufs(refs):
    sets = []
    for n in (6, 9, 9, 9, 9, 9, 9):
        sets.append(tuple(refs[:n]))
        refs = refs[n:]
    return sets, refs


def attn_backward(*refs):
    ins, refs = refs[:N_BACK_IN], refs[N_BACK_IN:]
    outs, refs = refs[:10], refs[10:]
    bufs, refs = refs[:N_BACK_IN], refs[N_BACK_IN:]
    out_o, gtok_o, gq_o, gk_o, gv_o, gg_o, go_o, gl_o, gr_o, gd_o = outs
    (
        ids, rate, fs, left_acc, dr, wo, att, pg, qkv, n2, dpr, pm, sb, pkq, dsz, mix, n1, wb, fo, dx1, x, dnear
    ) = bufs
    (
        fac, grid, wend, gin, mask, endf, inf, dm, dob, dp, vf, vs, vr, ts, tr, ws, wr, rf, du,
        tmp, nsend, nrecv, frecv, drz, gtok, gw, gout, gleft, gright,
    ) = refs[:29]
    refs = refs[29:]
    sc_bufs, refs = cut_bufs(refs)
    send, recv, local = refs
    pc = Place()
    pc.greet()
    ln = Links(pc, send, recv, local)
    got = [ln.fetch(a, b) for a, b in zip(ins, bufs)]

    def ready(n):
        while len(got) > N_BACK_IN - n:
            got.pop(0).wait()

    pc.meet()
    left = Scatter(ln, "cols", (left_acc, None, None) + sc_bufs[0])
    right = Scatter(ln, "cols", sc_bufs[1])
    s_out = Scatter(ln, "cols", sc_bufs[2])
    s_w = [Scatter(ln, "rows", sc_bufs[3 + i]) for i in range(4)]
    ready(3)
    f_cp = ln.go(fs, frecv, "P")
    fill_decay(rate, grid, wend, gin)
    fill_masks(pc, ids, mask, endf, inf)
    backward_factors(pc, ids, rate, fac)
    ready(4)
    for b in range(2):
        left.first_stage(b, True)
    ready(6)

    def mine(s):
        return pl.ds(pl.multiple_of(s * CH + pc.t * 128, 128), 128)

    def through(b, _):
        dm[:, cols256(b)] = dg(dr[...], wo[b], 1, 0)
        return 0

    lax.fori_loop(0, 2, through, 0)
    ready(9)
    v_cp = []
    for s in range(2):
        rs_ = pl.ds(s * CH, CH)

        def outer(h, _):
            d, o = dm[rs_, rows128(h)], att[h, rs_, :]
            g = jax.nn.sigmoid(pg[rs_, rows128(h)])
            inv = inverse_norm(o, HEAD_FLOOR)
            dp[3, rs_, rows128(h)] = (d * (o * inv) * g * (1.0 - g)).astype(BF)
            e = d * g
            inner = jnp.mean(e * o, axis=-1, keepdims=True)
            do = (inv * (e - o * (inner * inv * inv))).astype(BF)
            dob[h, rs_, :] = do
            gq = (qkv[2, h, rs_, :].astype(F32) * (gin[h] * inf[s])).astype(BF)
            v = dg(gq, do, 0, 0)
            vf[s, h] = v
            vs[s, h] = v.astype(BF)
            return 0

        lax.fori_loop(0, 4, outer, 0)
        v_cp.append(ln.go(vs.at[s], vr.at[s], "Q"))

    def product(i):
        return lambda b, j: dg(n1[:, cols256(j)], dp[i, :, cols256(b)], 0, 0)

    ready(11)
    for b in range(2):
        right.core_stage(b, lambda b, i: dg(dpr[b], n2[:, cols256(i)], 0, 0))
    for b in range(2):
        left.second_stage(b)
    ready(15)
    z_cp = ln.go(dsz, drz, "Q")
    for b in range(2):
        right.first_stage(b)

    def inner(s):
        rs_ = pl.ds(s * CH, CH)

        def inside(h, _):
            do, q, k = dob[h, rs_, :], qkv[2, h, rs_, :], qkv[0, h, rs_, :]
            dsc = (dg(do, qkv[1, h, rs_, :], 1, 1) * grid[h] * mask[s]).astype(BF)
            dq = dg(dsc, k, 1, 0) + (gin[h] * inf[s]) * dg(do, sb[s, h], 1, 1)
            dp[2, rs_, rows128(h)] = (dq * silu_slope(pkq[rs_, rows128(4 + h)])).astype(BF)
            dm[rs_, rows128(h)] = dg(dsc, q, 0, 0)
            att[h, rs_, :] = dg(pm[s, h], do, 0, 0)
            return 0

        lax.fori_loop(0, 4, inside, 0)

    def pair_up(s):
        v_cp[s].wait_recv()
        pair_sum(fac, s, vf, vr, ts, rf)
        return ln.go(ts.at[s], tr.at[s], "C")

    def quad_up(s):
        t_cp[s].wait_recv()
        quad_sum(fac, s, vf, tr, ws, rf)
        return ln.go(ws.at[s], wr.at[s], "Y")

    def close_up(s):
        w_cp[s].wait_recv()
        rs_ = pl.ds(s * CH, CH)

        def close(h, _):
            d = (rf[s, h] + fac[s, h, 6:7, :] * wr[s, h].astype(F32)).astype(BF)
            k, v = qkv[0, h, rs_, :], qkv[1, h, rs_, :]
            w = wend[h] * endf[s]
            kw = (k.astype(F32) * w).astype(BF)
            dp[1, rs_, rows128(h)] = (att[h, rs_, :] + dg(kw, d, 1, 0)).astype(BF)
            dk = dm[rs_, rows128(h)] + w * dg(v, d, 1, 1)
            dp[0, rs_, rows128(h)] = (dk * silu_slope(pkq[rs_, rows128(h)])).astype(BF)
            return 0

        lax.fori_loop(0, 4, close, 0)

    def through_weights(s):
        rs_ = pl.ds(s * CH, CH)
        acc = None
        for i in range(4):
            for b in range(2):
                p = dg(dp[i, rs_, b * 256 : (b + 1) * 256], wb[i, b], 1, 1)
                acc = p if acc is None else acc + p
        tmp[...] = acc
        nsend[s] = tmp[rows128(1 - pc.t), :].astype(BF)
        gtok[s] = tmp[rows128(pc.t), :]
        return ln.go(nsend.at[s], nrecv.at[s], "P")

    def out_core(b):
        s_out.core_stage(b, lambda b, i: dg(mix[:, cols256(b)], dr[:, cols256(i)], 0, 0))

    inner(0)
    t_cp = [pair_up(0)]
    t_cp.append(pair_up(1))
    ready(17)
    for b in range(2):
        out_core(b)
    w_cp = [quad_up(0), quad_up(1)]
    inner(1)
    for b in range(2):
        right.second_stage(b)
    for b in range(2):
        s_out.first_stage(b)
    left.plane_stage()
    for b in range(2):
        s_w[3].core_stage(b, product(3))
    ready(22)
    close_up(0)
    close_up(1)
    for b in range(2):
        s_w[3].first_stage(b)
    for i in (0, 1):
        for b in range(2):
            s_w[i].core_stage(b, product(i))
    for b in range(2):
        s_out.second_stage(b)
    right.plane_stage()
    n_cp = [through_weights(0)]
    for i in (0, 1):
        for b in range(2):
            s_w[i].first_stage(b)
    for b in range(2):
        s_w[3].second_stage(b)
    n_cp.append(through_weights(1))
    for b in range(2):
        s_w[2].core_stage(b, product(2))
    for i in (0, 1):
        for b in range(2):
            s_w[i].second_stage(b)
    s_out.plane_stage()
    s_w[3].plane_stage()
    for b in range(2):
        s_w[2].first_stage(b)
    for i in (0, 1):
        s_w[i].plane_stage()
    for b in range(2):
        s_w[2].second_stage(b)
    s_w[2].plane_stage()
    f_cp.wait_recv()
    frecv[...] = (fo[...] + frecv[...].astype(F32)).astype(BF)
    ln.keep(frecv, out_o)
    for s in range(2):
        n_cp[s].wait_recv()
        dn = gtok[s] + nrecv[s].astype(F32)
        gtok[s] = dx1[s] + norm_slope(x[s].astype(F32), dn, EPSILON)
    ln.keep(gtok, gtok_o)
    z_cp.wait_recv()
    dnear[...] = dnear[...] + drz[...].astype(F32)
    ln.keep(dnear, gd_o)
    gleft[...] = left.total()
    ln.keep(gleft, gl_o)
    gright[...] = right.total()
    ln.keep(gright, gr_o)
    gout[...] = s_out.total()
    ln.keep(gout, go_o)
    for i, o in ((3, gg_o), (2, gq_o), (0, gk_o), (1, gv_o)):
        gw[i] = s_w[i].total()
        ln.keep(gw.at[i], o)
    ln.drain()


def call_backward(*args):
    sd, vm = jax.ShapeDtypeStruct, pltpu.VMEM
    ff = args[10].shape[2]
    outs = [
        sd((2, 128, 1024), BF), sd((2, 128, 1024), F32),
        sd((128, 256), F32), sd((128, 256), F32), sd((128, 256), F32), sd((128, 256), F32),
        sd((256, 128), F32), sd((ff, 128), F32), sd((ff, 128), F32), sd((ff, 128), F32),
    ]
    st = (2, 4, DH, DH)
    scratch = [vm(a.shape, a.dtype) for a in args] + [
        vm((2, 4, 8, DH), F32), vm((4, CH, CH), F32), vm((4, CH, DH), F32), vm((4, CH, DH), F32),
        vm((2, CH, CH), F32), vm((2, CH, DH), F32), vm((2, CH, DH), F32),
        vm((512, 512), F32), vm((4, 512, DH), BF), vm((4, 512, 512), BF),
        vm(st, F32), vm(st, BF), vm(st, BF), vm(st, BF), vm(st, BF), vm(st, BF), vm(st, BF),
        vm(st, F32), vm((8, 128), BF),
        vm((CH, 1024), F32), vm((2, 128, 1024), BF), vm((2, 128, 1024), BF), vm((2, 128, 1024), BF),
        vm((ff, 128), BF), vm((2, 128, 1024), F32), vm((4, 128, 256), F32),
        vm((256, 128), F32), vm((ff, 128), F32), vm((ff, 128), F32),
        *scatter_bufs((ff, 128), BF, 0)[1:], *scatter_bufs((ff, 128), BF),
        *scatter_bufs((256, 128)), *scatter_bufs((128, 256)), *scatter_bufs((128, 256)),
        *scatter_bufs((128, 256)), *scatter_bufs((128, 256)),
        pltpu.SemaphoreType.DMA((64,)), pltpu.SemaphoreType.DMA((64,)), pltpu.SemaphoreType.DMA((40,)),
    ]
    return pl.pallas_call(
        attn_backward,
        out_shape=outs,
        in_specs=[pl.BlockSpec(memory_space=pl.ANY)] * len(args),
        out_specs=[pl.BlockSpec(memory_space=pl.ANY)] * len(outs),
        scratch_shapes=scratch,
        compiler_params=pltpu.CompilerParams(
            collective_id=2, has_side_effects=True, vmem_limit_bytes=63 * MIB
        ),
        name="attention_backward",
    )(*args)


def entering(x, axis, join, neutral):
    place = lax.axis_index(axis)
    gathered = jax.tree.map(
        lambda a, kind: lax.all_gather(a.astype(kind), axis),
        x,
        (jnp.bfloat16, jnp.bfloat16, jnp.bfloat16, jnp.bfloat16),
    )
    state = jax.tree.map(lambda a, e: jnp.zeros_like(a) + jnp.asarray(e, a.dtype), x, neutral)

    def one(lap, state):
        return join(
            state,
            jax.tree.map(
                lambda a, own: lax.dynamic_index_in_dim(a, lap, 0, False).astype(own.dtype),
                gathered,
                x,
            ),
        )

    return lax.fori_loop(0, place, one, state)


def entering_2(x, axis, join, neutral):
    count = lax.axis_size(axis)
    place = lax.axis_index(axis)
    ahead = count - 1 - place
    gathered = jax.tree.map(
        lambda a, kind: lax.all_gather(a.astype(kind), axis), x, (jnp.bfloat16, jnp.bfloat16)
    )
    state = jax.tree.map(lambda a, e: jnp.zeros_like(a) + jnp.asarray(e, a.dtype), x, neutral)

    def one(lap, state):
        source = count - 1 - lap
        return join(
            state,
            jax.tree.map(
                lambda a, own: lax.dynamic_index_in_dim(a, source, 0, False).astype(own.dtype),
                gathered,
                x,
            ),
        )

    return lax.fori_loop(0, ahead, one, state)


def normalize(values, floor_value=EPSILON):
    return values * lax.rsqrt(jnp.mean(values * values, axis=-1, keepdims=True) + floor_value)


def norm_backward(values, upstream, floor_value=EPSILON):
    inverse = lax.rsqrt(jnp.mean(values * values, axis=-1, keepdims=True) + floor_value)
    inner_mean = jnp.mean(upstream * values, axis=-1, keepdims=True)
    return inverse * (upstream - values * inner_mean * inverse * inverse)


def silu_grad(values):
    sigmoid_value = jax.nn.sigmoid(values)
    return sigmoid_value * (1.0 + values * (1.0 - sigmoid_value))


def chain_forward(earlier, later):
    early_first, early_last, early_decay, early_state = earlier
    late_first, late_last, late_decay, late_state = later
    linked = (late_first == early_last) | (early_last < 0.0) | (late_first < 0.0)
    carried = jnp.where(linked[:, None], late_decay, 0.0)
    first_seg = jnp.where(early_first < 0.0, late_first, early_first)
    last_seg = jnp.where(late_last < 0.0, early_last, late_last)
    return (
        first_seg,
        last_seg,
        early_decay * carried,
        late_state + carried[:, :, None, None] * early_state,
    )


def chain_backward(earlier, later):
    return (earlier[0] * later[0], later[1] + later[0][:, :, None, None] * earlier[1])


def shards(
    tokens,
    segment_ids,
    decay_rate,
    w_query,
    w_key,
    w_value,
    w_gate,
    w_out,
    glu_left,
    glu_right,
    glu_down,
    cotangent,
):
    shard_len, seq_count, model_width = tokens.shape
    tok_float = tokens.astype(jnp.float32)
    normed_part = normalize(tok_float).astype(jnp.bfloat16)
    gathered = (
        lax.all_gather(w_query.astype(jnp.bfloat16), ("fsdp", "ctx"), axis=0, tiled=True),
        lax.all_gather(w_key.astype(jnp.bfloat16), ("fsdp", "ctx"), axis=0, tiled=True),
        lax.all_gather(w_value.astype(jnp.bfloat16), ("fsdp", "ctx"), axis=0, tiled=True),
        lax.all_gather(w_gate.astype(jnp.bfloat16), ("fsdp", "ctx"), axis=0, tiled=True),
        lax.all_gather(w_out.astype(jnp.bfloat16), ("fsdp", "ctx"), axis=1, tiled=True),
        lax.all_gather(glu_left.astype(jnp.bfloat16), ("fsdp", "ctx"), axis=0, tiled=True),
        lax.all_gather(glu_right.astype(jnp.bfloat16), ("fsdp", "ctx"), axis=0, tiled=True),
        lax.all_gather(glu_down.astype(jnp.bfloat16), ("fsdp", "ctx"), axis=1, tiled=True),
    )
    full_query, full_key, full_value, full_gate, full_out, full_left, full_right, full_down = (
        gathered
    )
    normed = lax.all_gather(normed_part, "tp", axis=0, tiled=True)
    block_len = normed.shape[0]
    total_rows = block_len * seq_count
    normed_flat = normed.reshape(total_rows, model_width)
    local_width = full_query.shape[1]
    head_count = local_width // DH
    head_shape = (block_len, seq_count, head_count, DH)
    proj_query = jnp.dot(normed_flat, full_query, preferred_element_type=jnp.float32)
    proj_key = jnp.dot(normed_flat, full_key, preferred_element_type=jnp.float32)
    proj_value = jnp.dot(normed_flat, full_value, preferred_element_type=jnp.float32)
    proj_gate = jnp.dot(normed_flat, full_gate, preferred_element_type=jnp.float32)
    queries = jax.nn.silu(proj_query).astype(jnp.bfloat16).reshape(head_shape)
    keys_low = jax.nn.silu(proj_key).astype(jnp.bfloat16).reshape(head_shape)
    values_low = proj_value.astype(jnp.bfloat16).reshape(head_shape)
    seg_pos = segment_ids.T
    seg_float = seg_pos.astype(jnp.float32)
    position = jnp.arange(block_len).astype(jnp.float32)
    distance = position[:, None] - position[None, :]
    same_doc = (segment_ids[:, :, None] == segment_ids[:, None, :]) & (distance >= 0.0)[None]
    decay_grid = jnp.where(
        same_doc[:, None],
        jnp.exp(-decay_rate[None, :, None, None] * jnp.maximum(distance, 0.0)[None, None]),
        0.0,
    )
    end_weight = jnp.where(
        (seg_pos == seg_pos[-1:])[:, :, None],
        jnp.exp(-(block_len - 1.0 - position)[:, None, None] * decay_rate[None, None, :]),
        0.0,
    )
    keys_end = (keys_low.astype(jnp.float32) * end_weight[..., None]).astype(jnp.bfloat16)
    update = jnp.einsum("tbhd,tbhe->bhde", keys_end, values_low, preferred_element_type=jnp.float32)
    first_seg = seg_float[0]
    last_seg = seg_float[-1]
    span_decay = jnp.where(
        (first_seg == last_seg)[:, None], jnp.exp(-block_len * decay_rate)[None, :], 0.0
    )
    identity = (
        -jnp.ones((seq_count,), jnp.float32),
        -jnp.ones((seq_count,), jnp.float32),
        jnp.ones((seq_count, head_count), jnp.float32),
        jnp.zeros((seq_count, head_count, DH, DH), jnp.float32),
    )
    scanned = entering((first_seg, last_seg, span_decay, update), "ctx", chain_forward, identity)
    prior_last = scanned[1]
    state_low = scanned[3].astype(jnp.bfloat16)
    inflow = jnp.where(
        (seg_pos == prior_last[None, :])[:, :, None],
        jnp.exp(-(position + 1.0)[:, None, None] * decay_rate[None, None, :]),
        0.0,
    )
    scores = jnp.einsum("tbhd,sbhd->bhts", queries, keys_low, preferred_element_type=jnp.float32)
    weights_low = (scores * decay_grid).astype(jnp.bfloat16)
    intra = jnp.einsum(
        "bhts,sbhd->tbhd", weights_low, values_low, preferred_element_type=jnp.float32
    )
    inter = (
        jnp.einsum("tbhd,bhde->tbhe", queries, state_low, preferred_element_type=jnp.float32)
        * inflow[..., None]
    )
    attended = intra + inter
    attended_norm = normalize(attended, HEAD_FLOOR)
    gate_value = jax.nn.sigmoid(proj_gate).reshape(head_shape)
    mixed_heads = (
        (attended_norm * gate_value).astype(jnp.bfloat16).reshape(block_len, seq_count, local_width)
    )
    row_count = shard_len * lax.axis_size("tp")
    piece_rows = mixed_heads.reshape(row_count * seq_count, local_width)
    branch = lax.psum_scatter(
        jnp.dot(piece_rows, full_out, preferred_element_type=jnp.float32).reshape(
            row_count, seq_count, model_width
        ),
        "tp",
        scatter_dimension=0,
        tiled=True,
    )
    residual = tok_float + branch
    second_part = normalize(residual).astype(jnp.bfloat16)
    second = lax.all_gather(second_part, "tp", axis=0, tiled=True)
    second_flat = second.reshape(total_rows, model_width)
    left_proj = jnp.dot(second_flat, full_left, preferred_element_type=jnp.float32)
    right_proj = jnp.dot(second_flat, full_right, preferred_element_type=jnp.float32)
    hidden = (left_proj * right_proj).astype(jnp.bfloat16)
    ffn_width = hidden.shape[1]
    hidden_blocks = hidden.reshape(block_len, seq_count, ffn_width)
    row_count = shard_len * lax.axis_size("tp")
    piece_rows = hidden_blocks.reshape(row_count * seq_count, ffn_width)
    ffn_branch = lax.psum_scatter(
        jnp.dot(piece_rows, full_down, preferred_element_type=jnp.float32)
        .reshape(row_count, seq_count, model_width)
        .astype(jnp.bfloat16),
        "tp",
        scatter_dimension=0,
        tiled=True,
    ).astype(jnp.float32)
    output = (residual + ffn_branch).astype(jnp.bfloat16)
    upstream = lax.all_gather(cotangent, "tp", axis=0, tiled=True).reshape(total_rows, model_width)
    grad_down = jnp.dot(hidden.T, upstream, preferred_element_type=jnp.float32)
    grad_hidden = jnp.dot(upstream, full_down.T, preferred_element_type=jnp.float32)
    grad_left_proj = (grad_hidden * right_proj).astype(jnp.bfloat16)
    grad_right_proj = (grad_hidden * left_proj).astype(jnp.bfloat16)
    grad_left = jnp.dot(second_flat.T, grad_left_proj, preferred_element_type=jnp.float32)
    grad_right = jnp.dot(second_flat.T, grad_right_proj, preferred_element_type=jnp.float32)
    left_blocks = grad_left_proj.reshape(block_len, seq_count, ffn_width)
    right_blocks = grad_right_proj.reshape(block_len, seq_count, ffn_width)
    row_count = shard_len * lax.axis_size("tp")
    left_rows = left_blocks.reshape(row_count * seq_count, ffn_width)
    right_rows = right_blocks.reshape(row_count * seq_count, ffn_width)
    summed = jnp.dot(left_rows, full_left.T, preferred_element_type=jnp.float32) + jnp.dot(
        right_rows, full_right.T, preferred_element_type=jnp.float32
    )
    grad_second = lax.psum_scatter(
        summed.reshape(row_count, seq_count, model_width), "tp", scatter_dimension=0, tiled=True
    )
    grad_residual = cotangent.astype(jnp.float32) + norm_backward(residual, grad_second)
    branch_low = grad_residual.astype(jnp.bfloat16)
    grad_branch = lax.all_gather(branch_low, "tp", axis=0, tiled=True).reshape(
        total_rows, model_width
    )
    grad_wout = jnp.dot(
        mixed_heads.reshape(total_rows, local_width).T,
        grad_branch,
        preferred_element_type=jnp.float32,
    )
    grad_mixed = jnp.dot(grad_branch, full_out.T, preferred_element_type=jnp.float32).reshape(
        head_shape
    )
    grad_gate_proj = (
        (grad_mixed * attended_norm * gate_value * (1.0 - gate_value))
        .astype(jnp.bfloat16)
        .reshape(total_rows, local_width)
    )
    grad_attended = norm_backward(attended, grad_mixed * gate_value, HEAD_FLOOR).astype(
        jnp.bfloat16
    )
    grad_weights = jnp.einsum(
        "tbhd,sbhd->bhts", grad_attended, values_low, preferred_element_type=jnp.float32
    )
    grad_scores = (grad_weights * decay_grid).astype(jnp.bfloat16)
    grad_queries = jnp.einsum(
        "bhts,sbhd->tbhd", grad_scores, keys_low, preferred_element_type=jnp.float32
    )
    grad_queries = (
        grad_queries
        + jnp.einsum(
            "tbhe,bhde->tbhd", grad_attended, state_low, preferred_element_type=jnp.float32
        )
        * inflow[..., None]
    )
    grad_keys = jnp.einsum(
        "bhts,tbhd->sbhd", grad_scores, queries, preferred_element_type=jnp.float32
    )
    grad_values = jnp.einsum(
        "bhts,tbhd->sbhd", weights_low, grad_attended, preferred_element_type=jnp.float32
    )
    weighted_queries = queries.astype(jnp.float32) * inflow[..., None]
    grad_prior_local = jnp.einsum(
        "tbhd,tbhe->bhde", weighted_queries, grad_attended.astype(jnp.float32), precision=lax.Precision.HIGHEST
    )
    link_decay = jnp.where((first_seg == prior_last)[:, None], span_decay, 0.0)
    back_identity = (
        jnp.ones((seq_count, head_count), jnp.float32),
        jnp.zeros((seq_count, head_count, DH, DH), jnp.float32),
    )
    grad_update = entering_2((link_decay, grad_prior_local), "ctx", chain_backward, back_identity)[
        1
    ]
    grad_values = grad_values + jnp.einsum(
        "tbhd,bhde->tbhe", keys_end.astype(jnp.float32), grad_update, precision=lax.Precision.HIGHEST
    )
    grad_keys = (
        grad_keys
        + jnp.einsum(
            "tbhe,bhde->tbhd", values_low.astype(jnp.float32), grad_update, precision=lax.Precision.HIGHEST
        )
        * end_weight[..., None]
    )
    grad_query_proj = (
        (grad_queries * silu_grad(proj_query).reshape(head_shape))
        .astype(jnp.bfloat16)
        .reshape(total_rows, local_width)
    )
    grad_key_proj = (
        (grad_keys * silu_grad(proj_key).reshape(head_shape))
        .astype(jnp.bfloat16)
        .reshape(total_rows, local_width)
    )
    grad_value_proj = grad_values.astype(jnp.bfloat16).reshape(total_rows, local_width)
    grad_wquery = jnp.dot(normed_flat.T, grad_query_proj, preferred_element_type=jnp.float32)
    grad_wkey = jnp.dot(normed_flat.T, grad_key_proj, preferred_element_type=jnp.float32)
    grad_wvalue = jnp.dot(normed_flat.T, grad_value_proj, preferred_element_type=jnp.float32)
    grad_wgate = jnp.dot(normed_flat.T, grad_gate_proj, preferred_element_type=jnp.float32)
    query_blocks = grad_query_proj.reshape(block_len, seq_count, local_width)
    key_blocks = grad_key_proj.reshape(block_len, seq_count, local_width)
    value_blocks = grad_value_proj.reshape(block_len, seq_count, local_width)
    gate_blocks = grad_gate_proj.reshape(block_len, seq_count, local_width)
    row_count = shard_len * lax.axis_size("tp")
    summed = jnp.zeros((row_count * seq_count, model_width), jnp.float32)
    for grad_blocks, weight_full in (
        (query_blocks, full_query),
        (key_blocks, full_key),
        (value_blocks, full_value),
        (gate_blocks, full_gate),
    ):
        piece_rows = grad_blocks.reshape(row_count * seq_count, local_width)
        summed = summed + jnp.dot(piece_rows, weight_full.T, preferred_element_type=jnp.float32)
    grad_normed = lax.psum_scatter(
        summed.reshape(row_count, seq_count, model_width).astype(jnp.bfloat16),
        "tp",
        scatter_dimension=0,
        tiled=True,
    ).astype(jnp.float32)
    grad_tokens = grad_residual + norm_backward(tok_float, grad_normed)
    every_grad = (
        lax.psum_scatter(grad_wquery, ("fsdp", "ctx"), scatter_dimension=0, tiled=True),
        lax.psum_scatter(grad_wkey, ("fsdp", "ctx"), scatter_dimension=0, tiled=True),
        lax.psum_scatter(grad_wvalue, ("fsdp", "ctx"), scatter_dimension=0, tiled=True),
        lax.psum_scatter(grad_wgate, ("fsdp", "ctx"), scatter_dimension=0, tiled=True),
        lax.psum_scatter(grad_wout, ("fsdp", "ctx"), scatter_dimension=1, tiled=True),
        lax.psum_scatter(grad_left, ("fsdp", "ctx"), scatter_dimension=0, tiled=True),
        lax.psum_scatter(grad_right, ("fsdp", "ctx"), scatter_dimension=0, tiled=True),
        lax.psum_scatter(grad_down, ("fsdp", "ctx"), scatter_dimension=1, tiled=True),
    )
    return (
        output,
        grad_tokens,
        every_grad[0],
        every_grad[1],
        every_grad[2],
        every_grad[3],
        every_grad[4],
        every_grad[5],
        every_grad[6],
        every_grad[7],
    )


def paired(
    tokens, segment_ids, decay_rate, w_query, w_key, w_value, w_gate, w_out,
    glu_left, glu_right, glu_down, cotangent,
):
    tok, cot = tokens.transpose(1, 0, 2), cotangent.transpose(1, 0, 2)
    (
        n1, n2, pkq, pg, qkv, pm, att, mix, sb, wb, wo, ids, rate,
        dr, dx1, fs, fo, dpr, dnear, dsz, left_acc,
    ) = call_forward(
        decay_rate, tok, cot, segment_ids, (w_query, w_key, w_value, w_gate), w_out,
        glu_left.T, glu_right.T, glu_down,
    )
    out, g_tok, g_q, g_k, g_v, g_g, g_o, g_left, g_right, g_down = call_backward(
        ids, rate, fs, left_acc, dr, wo, att, pg, qkv, n2, dpr, pm, sb, pkq, dsz, mix, n1, wb, fo, dx1, tok,
        dnear,
    )
    return (
        out.transpose(1, 0, 2), g_tok.transpose(1, 0, 2),
        g_q, g_k, g_v, g_g, g_o, g_left.T, g_right.T, g_down,
    )


def solution(mesh):
    in_specs = (
        P(("ctx", "tp"), "fsdp", None),
        P("fsdp", "ctx"),
        P("tp"),
        P(("fsdp", "ctx"), "tp"),
        P(("fsdp", "ctx"), "tp"),
        P(("fsdp", "ctx"), "tp"),
        P(("fsdp", "ctx"), "tp"),
        P("tp", ("fsdp", "ctx")),
        P(("fsdp", "ctx"), "tp"),
        P(("fsdp", "ctx"), "tp"),
        P("tp", ("fsdp", "ctx")),
        P(("ctx", "tp"), "fsdp", None),
    )
    out_specs = (
        P(("ctx", "tp"), "fsdp", None),
        P(("ctx", "tp"), "fsdp", None),
        P(("fsdp", "ctx"), "tp"),
        P(("fsdp", "ctx"), "tp"),
        P(("fsdp", "ctx"), "tp"),
        P(("fsdp", "ctx"), "tp"),
        P("tp", ("fsdp", "ctx")),
        P(("fsdp", "ctx"), "tp"),
        P(("fsdp", "ctx"), "tp"),
        P("tp", ("fsdp", "ctx")),
    )
    sizes = tuple(mesh.shape[a] for a in ("fsdp", "ctx", "tp"))
    body = paired if sizes == (2, 4, 4) else shards
    return jax.shard_map(body, mesh=mesh, in_specs=in_specs, out_specs=out_specs, check_vma=False)
```

```python
import functools

import jax
import jax.numpy as jnp
from jax import lax
from jax.experimental import pallas as pl
from jax.experimental.pallas import tpu as pltpu
from jax.sharding import PartitionSpec as P

DH = 128
CH = 256
EPSILON = 1e-06
HEAD_FLOOR = 1.0
BF = jnp.bfloat16
F32 = jnp.float32
MESH = pl.DeviceIdType.MESH
MIB = 1 << 20


def dg(a, b, ca, cb):
    return lax.dot_general(a, b, (((ca,), (cb,)), ((), ())), preferred_element_type=F32)


def rows128(i):
    return pl.ds(pl.multiple_of(i * 128, 128), 128)


def cols256(i):
    return pl.ds(pl.multiple_of(i * 256, 256), 256)


def inverse_norm(v, floor_value):
    return lax.rsqrt(jnp.mean(v * v, axis=-1, keepdims=True) + floor_value)


def norm_slope(v, d, floor_value):
    inv = inverse_norm(v, floor_value)
    inner = jnp.mean(d * v, axis=-1, keepdims=True)
    return inv * (d - v * (inner * inv * inv))


class Place:
    def __init__(self):
        x, k, z = lax.axis_index("fsdp"), lax.axis_index("ctx"), lax.axis_index("tp")
        self.x, self.k, self.z = x, k, z
        self.y, self.c = k // 2, k % 2
        self.t, self.zh = z % 2, z // 2
        self.r = x * 4 + k
        self.peer = {
            "X": (1 - x, k, z),
            "Y": (x, (k + 2) % 4, z),
            "C": (x, k + 1 - 2 * self.c, z),
            "P": (x, k, z + 1 - 2 * self.t),
            "Q": (x, k, (z + 2) % 4),
        }

    def flip(self, r, axis):
        if axis == "X":
            return (r + 4) % 8
        if axis == "Y":
            return r + 2 - 4 * ((r // 2) % 2)
        return r + 1 - 2 * (r % 2)

    def greet(self):
        bar = pltpu.get_barrier_semaphore()
        for peer in self.peer.values():
            pl.semaphore_signal(bar, inc=1, device_id=peer, device_id_type=MESH)

    def meet(self):
        pl.semaphore_wait(pltpu.get_barrier_semaphore(), len(self.peer))


class Links:
    def __init__(self, place, send, recv, local):
        self.place, self.send, self.recv, self.local = place, send, recv, local
        self.n = self.m = 0
        self.sent, self.kept = [], []

    def remote(self, src, dst, peer):
        cp = pltpu.make_async_remote_copy(
            src_ref=src,
            dst_ref=dst,
            send_sem=self.send.at[self.n],
            recv_sem=self.recv.at[self.n],
            device_id=self.place.peer[peer],
            device_id_type=MESH,
        )
        self.n += 1
        return cp

    def go(self, src, dst, peer):
        cp = self.remote(src, dst, peer)
        cp.start()
        self.sent.append(cp)
        return cp

    def keep(self, src, dst):
        cp = pltpu.make_async_copy(src, dst, self.local.at[self.m])
        self.m += 1
        cp.start()
        self.kept.append(cp)
        return cp

    def fetch(self, src, dst):
        cp = pltpu.make_async_copy(src, dst, self.local.at[self.m])
        self.m += 1
        cp.start()
        return cp

    def gone(self, cp):
        cp.wait_send()
        self.sent = [other for other in self.sent if other is not cp]

    def written(self, cp):
        cp.wait()
        self.kept = [other for other in self.kept if other is not cp]

    def drain(self):
        for cp in self.sent:
            cp.wait_send()
        for cp in self.kept:
            cp.wait()


class Gather:
    def __init__(self, links, order, view, own=None):
        self.links, self.view = links, view
        pc = links.place
        self.pc, self.own = pc, own
        self.first, self.second = ("X", "Y") if order == "A" else ("Y", "X")
        self.rf = pc.flip(pc.r, self.first)
        self.rs = pc.flip(pc.r, self.second)
        self.rfs = pc.flip(self.rf, self.second)
        self.cps = [{}, {}]

    def put(self, slot, name, r, peer, src=None):
        b = self.pc.zh if slot == 0 else 1 - self.pc.zh
        src = self.view(b, r) if src is None else src
        self.cps[slot][name] = self.links.go(src, self.view(b, r), peer)

    def launch(self, slot, src=None):
        r = self.pc.r
        self.put(slot, "f", r, self.first, src)
        self.put(slot, "sa", r, self.second, src)
        self.put(slot, "c0", r, "C", src)

    def cross(self):
        self.put(0, "z", self.pc.r, "Q", self.own)

    def start(self):
        self.launch(0, self.own)
        self.cross()

    def other(self):
        self.cps[0]["z"].wait_recv()
        self.launch(1)

    def step1(self, slot):
        self.cps[slot]["f"].wait_recv()
        self.put(slot, "sb", self.rf, self.second)
        self.put(slot, "c1", self.rf, "C")

    def step2(self, slot):
        self.cps[slot]["sa"].wait_recv()
        self.put(slot, "c2", self.rs, "C")
        self.cps[slot]["sb"].wait_recv()
        self.put(slot, "c3", self.rfs, "C")

    def step3(self, slot):
        for name in ("c0", "c1", "c2", "c3"):
            self.cps[slot][name].wait_recv()


def last_id(ids, kk, half, s):
    at = 255 + 256 * half
    return ids[kk, s : s + 1, at : at + 1]


def prior_id(pc, ids, s):
    before = jnp.where(pc.zh == 1, last_id(ids, pc.k, 0, s), last_id(ids, (pc.k + 3) % 4, 1, s))
    return jnp.where((pc.zh == 1) | (pc.k > 0), before, -1.0)


def same(a, b):
    return jnp.where(a == b, 1.0, 0.0)


def fill_decay(rate, grid, wend, gin):
    ti = lax.broadcasted_iota(jnp.int32, (CH, CH), 0).astype(F32)
    si = lax.broadcasted_iota(jnp.int32, (CH, CH), 1).astype(F32)
    dist = ti - si
    pos = lax.broadcasted_iota(jnp.int32, (CH, DH), 0).astype(F32)

    def head(h, _):
        lane = rate[h, 0:1, :]
        both = jnp.concatenate([lane, lane], axis=1)
        grid[h] = jnp.where(dist >= 0.0, jnp.exp(-both * jnp.maximum(dist, 0.0)), 0.0)
        wend[h] = jnp.exp(-lane * (CH - 1.0 - pos))
        gin[h] = jnp.exp(-lane * (pos + 1.0))
        return 0

    lax.fori_loop(0, 4, head, 0)


def fill_masks(pc, ids, mask, endf, inf):
    for s in range(2):
        row = ids[pc.k, s : s + 1, pl.ds(pl.multiple_of(pc.zh * CH, CH), CH)]
        along = jnp.broadcast_to(row, (CH, CH))
        down = along.T
        mask[s] = same(along, down)
        col = down[:, :DH]
        endf[s] = same(col, jnp.broadcast_to(row[:, CH - 1 : CH], (CH, DH)))
        inf[s] = same(col, jnp.broadcast_to(prior_id(pc, ids, s), (CH, DH)))


def forward_factors(pc, ids, rate, fac):
    for s in range(2):
        prior = prior_id(pc, ids, s)
        low = last_id(ids, pc.y * 2, 1, s)
        f1 = same(last_id(ids, pc.k, 0, s), last_id(ids, pc.k, 1, s))
        f2 = same(low, last_id(ids, pc.y * 2 + 1, 1, s))
        p2 = same(low, prior) * jnp.where(pc.c == 1, 1.0, 0.0)
        p3 = same(last_id(ids, 1, 1, s), prior) * jnp.where(pc.y == 1, 1.0, 0.0)
        d2 = pc.zh.astype(F32) * CH
        d3 = (2 * pc.c + pc.zh).astype(F32) * CH
        for h in range(4):
            one = rate[h, 0:1, :]
            unit = jnp.ones_like(one)
            l1, l2 = jnp.exp(-CH * one) * f1, jnp.exp(-2.0 * CH * one) * f2
            fac[s, h, 0:1, :] = jnp.where(pc.zh == 1, unit, l1)
            fac[s, h, 1:2, :] = jnp.where(pc.zh == 1, l1, unit)
            fac[s, h, 2:3, :] = jnp.where(pc.zh == 1, unit, 0.0 * unit)
            fac[s, h, 3:4, :] = jnp.where(pc.c == 1, unit, l2)
            fac[s, h, 4:5, :] = jnp.where(pc.c == 1, l2, unit)
            fac[s, h, 5:6, :] = jnp.exp(-d2 * one) * p2
            fac[s, h, 6:7, :] = jnp.exp(-d3 * one) * p3


def backward_factors(pc, ids, rate, fac):
    for s in range(2):
        low = last_id(ids, pc.y * 2, 1, s)
        prev_k = jnp.where(pc.k > 0, last_id(ids, (pc.k + 3) % 4, 1, s), -1.0)
        prev_y = jnp.where(pc.y > 0, last_id(ids, (pc.y * 2 + 3) % 4, 1, s), -1.0)
        here = jnp.where(pc.zh == 1, last_id(ids, pc.k, 1, s), last_id(ids, pc.k, 0, s))
        f1, f2 = same(prev_k, last_id(ids, pc.k, 0, s)), same(prev_y, low)
        p2 = same(here, low) * jnp.where(pc.c == 0, 1.0, 0.0)
        p3 = same(here, last_id(ids, 1, 1, s)) * jnp.where(pc.y == 0, 1.0, 0.0)
        d2 = (1 - pc.zh).astype(F32) * CH
        d3 = (2 * (1 - pc.c) + (1 - pc.zh)).astype(F32) * CH
        for h in range(4):
            one = rate[h, 0:1, :]
            unit = jnp.ones_like(one)
            l1, l2 = jnp.exp(-CH * one) * f1, jnp.exp(-2.0 * CH * one) * f2
            fac[s, h, 0:1, :] = jnp.where(pc.zh == 0, unit, l1)
            fac[s, h, 1:2, :] = jnp.where(pc.zh == 0, l1, unit)
            fac[s, h, 2:3, :] = jnp.where(pc.zh == 0, unit, 0.0 * unit)
            fac[s, h, 3:4, :] = jnp.where(pc.c == 0, unit, l2)
            fac[s, h, 4:5, :] = jnp.where(pc.c == 0, l2, unit)
            fac[s, h, 5:6, :] = jnp.exp(-d2 * one) * p2
            fac[s, h, 6:7, :] = jnp.exp(-d3 * one) * p3


def pair_sum(fac, s, own, got, total, prefix):
    for h in range(4):
        g = got[s, h].astype(F32)
        tot = fac[s, h, 0:1, :] * own[s, h] + fac[s, h, 1:2, :] * g
        prefix[s, h] = fac[s, h, 2:3, :] * g
        own[s, h] = tot
        total[s, h] = tot.astype(BF)


def quad_sum(fac, s, own, got, total, prefix):
    for h in range(4):
        g = got[s, h].astype(F32)
        total[s, h] = (fac[s, h, 3:4, :] * own[s, h] + fac[s, h, 4:5, :] * g).astype(BF)
        prefix[s, h] = prefix[s, h] + fac[s, h, 5:6, :] * g


class Scatter:
    def __init__(self, links, kind, bufs):
        self.links, self.kind = links, kind
        pc = links.place
        self.pc = pc
        self.acc, self.sc, self.rc, self.sf, self.rf, self.ss, self.rs, self.sz, self.rz = bufs
        self.c_cp, self.f_cp, self.s_cp = {}, {}, {}
        self.last = 2 * pc.x + pc.y

    def way(self, b):
        x, y = self.pc.x, self.pc.y
        if b == 0:
            return "X", "Y", x, y, lambda f, m: 2 * f + m
        return "Y", "X", y, x, lambda f, m: 2 * m + f

    def core_stage(self, b, product, after=None):
        if after is not None:
            self.links.gone(after.c_cp[b])

        def pair(i, _):
            p = product(b, i)
            lo, hi = (p[:128], p[128:]) if self.kind == "rows" else (p[:, :128], p[:, 128:])
            self.sc[b, i] = jnp.where(self.pc.c == 0, hi, lo).astype(BF)
            self.acc[b, i] = jnp.where(self.pc.c == 0, lo, hi).astype(self.acc.dtype)
            return 0

        lax.fori_loop(0, 4, pair, 0)
        self.c_cp[b] = self.links.go(self.sc.at[b], self.rc.at[b], "C")

    def add(self, b, i, got):
        return self.acc[b, i].astype(F32) + got.astype(F32)

    def first_stage(self, b, joined=False):
        first, _, fv, _, at = self.way(b)
        if not joined:
            self.c_cp[b].wait_recv()
        for m in range(2):
            i = at(1 - fv, m)
            self.sf[b, m] = (self.acc[b, i] if joined else self.add(b, i, self.rc[b, i])).astype(BF)
        self.f_cp[b] = self.links.go(self.sf.at[b], self.rf.at[b], first)
        if not joined:
            for m in range(2):
                i = at(fv, m)
                self.acc[b, i] = self.add(b, i, self.rc[b, i]).astype(self.acc.dtype)

    def join(self, b):
        self.c_cp[b].wait_recv()
        for i in range(4):
            self.acc[b, i] = self.add(b, i, self.rc[b, i]).astype(self.acc.dtype)

    def second_stage(self, b):
        _, second, fv, sv, at = self.way(b)
        self.f_cp[b].wait_recv()
        self.ss[b] = self.add(b, at(fv, 1 - sv), self.rf[b, 1 - sv]).astype(BF)
        self.s_cp[b] = self.links.go(self.ss.at[b], self.rs.at[b], second)
        self.acc[b, self.last] = self.add(b, self.last, self.rf[b, sv]).astype(self.acc.dtype)

    def plane_stage(self):
        zh = self.pc.zh
        for b in range(2):
            self.s_cp[b].wait_recv()
        self.sz[...] = self.add(1 - zh, self.last, self.rs[1 - zh]).astype(BF)
        if self.rz is not None:
            self.z_cp = self.links.go(self.sz, self.rz, "Q")

    def near(self):
        zh = self.pc.zh
        return self.add(zh, self.last, self.rs[zh])

    def total(self):
        self.z_cp.wait_recv()
        return self.near() + self.rz[...].astype(F32)


def scatter_bufs(slab, acc=F32, core=2):
    vm = pltpu.VMEM
    return [vm((2, 4) + slab, acc)] + [vm((2, 4) + slab, BF)] * core + [
        vm((2, 2) + slab, BF), vm((2, 2) + slab, BF), vm((2,) + slab, BF), vm((2,) + slab, BF),
        vm(slab, BF), vm(slab, BF),
    ]


def forward_and_glu(
    rate_in, tok, cot, seg, wq, wk, wv, wg, wo_in, gl_in, gr_in, gd_in,
    xm_o, n1_o, n2_o, pkq_o, pg_o, qkv_o, p_o, att_o, mix_o, sb_o, w_o, wo_o, ids_o, rate_o,
    dr_o, dx1_o, fs_o, fo_o, dpr_o, gdown_o, dsz_o, left_o,
    xb, n1, ct, n2, x1, pg, qkv, pm, att, mix, sb, wb, wo, gl, gr, gd,
    ids, rate, fac, grid, wend, gin, mask, endf, inf, uf, us, ur, ts, tr, vs, vr, pf,
    br_s, br_r, dn_r, dn, hid, dpl, dpr, tmp, dr, fs, fo, gdown, left_acc,
    *rest,
):
    down_b, left_b = rest[:8] + (None,), (left_acc, rest[1], rest[8]) + (None,) * 6
    send, recv, local = rest[9:]
    pc = Place()
    pc.greet()
    ln = Links(pc, send, recv, local)
    own, r = pc.zh, pc.r
    far_b = 1 - own

    def mine(s):
        return pl.ds(pl.multiple_of(s * CH + pc.t * 128, 128), 128)

    def theirs(s):
        return pl.ds(pl.multiple_of(s * CH + (1 - pc.t) * 128, 128), 128)

    def wview(i):
        return lambda b, rr: wb.at[i, b, rows128(rr), :]

    def gview(w):
        return lambda b, rr: w.at[b, rows128(rr), :]

    for hh in range(2):
        rate[own * 2 + hh] = jnp.full((8, DH), rate_in[hh], F32)
    for s in range(2):
        xb[mine(s), :] = tok[:, s, :]
        ct[mine(s), :] = cot[:, s, :]
    for i, w in enumerate((wk, wv, wq, wg)):
        wb[i, own, rows128(r), :] = w[...].astype(BF)
    wo[own, rows128(r), :] = wo_in[...].T.astype(BF)
    ids[pc.k] = jnp.zeros((8, 512), F32)
    ids[pc.k, 0:2, :] = seg[...].astype(F32)
    pc.meet()

    g_o = Gather(ln, "A", gview(wo))
    qkvgo = [Gather(ln, "AB"[i % 2], wview(i)) for i in range(4)] + [g_o]
    g_l, g_r, g_d = Gather(ln, "A", gview(gl)), Gather(ln, "B", gview(gr)), Gather(ln, "A", gview(gd))
    rate_cp = ln.go(rate.at[pl.ds(own * 2, 2)], rate.at[pl.ds(own * 2, 2)], "Q")
    ids_y = ln.go(ids.at[pc.k], ids.at[pc.k], "Y")
    ids_c = ln.go(ids.at[pc.k], ids.at[pc.k], "C")
    for g in qkvgo[:2]:
        g.cross()
        g.launch(0)
    x_cp = [ln.go(xb.at[mine(s)], xb.at[mine(s)], "P") for s in range(2)]
    for g in qkvgo[2:]:
        g.launch(0)
    for g in qkvgo[2:]:
        g.cross()
    for s in range(2):
        xf = xb[mine(s), :].astype(F32)
        n1[mine(s), :] = (xf * inverse_norm(xf, EPSILON)).astype(BF)
    for w, w_in in ((gl, gl_in), (gr, gr_in), (gd, gd_in)):
        w[own, rows128(r), :] = w_in[...].T.astype(BF)
    kf = (pc.k + 2) % 4
    ids_y.wait_recv()
    ids_f = ln.go(ids.at[kf], ids.at[kf], "C")
    for g in qkvgo:
        g.step1(0)
    rate_cp.wait_recv()
    fill_decay(rate, grid, wend, gin)
    for g in qkvgo[:2]:
        g.other()
    for g in qkvgo:
        g.step2(0)
    ids_c.wait_recv()
    ids_f.wait_recv()
    fill_masks(pc, ids, mask, endf, inf)
    forward_factors(pc, ids, rate, fac)
    for g in qkvgo[:2]:
        g.step1(1)
    g_l.launch(0)
    g_r.launch(0)
    for g in qkvgo[:2]:
        g.step2(1)
    for s in range(2):
        x_cp[s].wait_recv()
        xf = xb[theirs(s), :].astype(F32)
        n1[theirs(s), :] = (xf * inverse_norm(xf, EPSILON)).astype(BF)

    def project(i):
        for slot in range(2):
            qkvgo[i].step3(slot)

        def block(b, _):
            p = dg(n1[...], wb[i, b], 1, 0)
            if i == 0:
                x1[:, cols256(b)] = p
            elif i == 2:
                x1[:, cols256(2 + b)] = p
            elif i == 3:
                pg[:, cols256(b)] = p
            if i < 3:
                a = (p if i == 1 else p * jax.nn.sigmoid(p)).astype(BF)
                qkv[i, b * 2] = a[:, :DH]
                qkv[i, b * 2 + 1] = a[:, DH:]
            return 0

        lax.fori_loop(0, 2, block, 0)

    project(0)
    project(1)
    u_cp = []
    for s in range(2):
        rs_ = pl.ds(s * CH, CH)

        def state(h, _):
            kw = (qkv[0, h, rs_, :].astype(F32) * (wend[h] * endf[s])).astype(BF)
            u = dg(kw, qkv[1, h, rs_, :], 0, 0)
            uf[s, h] = u
            us[s, h] = u.astype(BF)
            return 0

        lax.fori_loop(0, 4, state, 0)
        u_cp.append(ln.go(us.at[s], ur.at[s], "Q"))
    ct_cp = [ln.go(ct.at[mine(0)], ct.at[mine(0)], "P")]
    for g in qkvgo[2:]:
        g.other()
    g_l.cross()
    g_r.cross()
    g_l.step1(0)
    g_r.step1(0)
    for g in qkvgo[2:]:
        g.step1(1)
    for g in qkvgo[2:]:
        g.step2(1)
    project(2)
    for s in range(2):
        rs_ = pl.ds(s * CH, CH)

        def inside(h, _):
            sc = dg(qkv[2, h, rs_, :], qkv[0, h, rs_, :], 1, 1)
            p = (sc * grid[h] * mask[s]).astype(BF)
            pm[s, h] = p
            att[h, rs_, :] = dg(p, qkv[1, h, rs_, :], 1, 0)
            return 0

        lax.fori_loop(0, 4, inside, 0)
    project(3)
    g_o.step3(0)
    g_o.step3(1)
    pkq_cp = ln.keep(x1, pkq_o)
    for s in range(2):
        ln.keep(xb.at[mine(s)], xm_o.at[s])
    for i in range(4):
        ln.keep(wb.at[i], w_o.at[i])
    ln.keep(n1, n1_o)
    ln.keep(pg, pg_o)
    ln.keep(qkv, qkv_o)
    ln.keep(ids, ids_o)
    ln.keep(rate, rate_o)
    ln.keep(pm, p_o)
    ln.keep(wo, wo_o)
    g_l.step2(0)
    g_r.step2(0)
    g_d.launch(0)

    v_cp = []
    for s in range(2):
        u_cp[s].wait_recv()
        pair_sum(fac, s, uf, ur, ts, pf)
        t_cp = ln.go(ts.at[s], tr.at[s], "C")
        t_cp.wait_recv()
        quad_sum(fac, s, uf, tr, vs, pf)
        v_cp.append(ln.go(vs.at[s], vr.at[s], "Y"))
    ln.written(pkq_cp)
    b_cp = []
    for s in range(2):
        v_cp[s].wait_recv()
        rs_ = pl.ds(s * CH, CH)

        def enter(h, _):
            low_st = (pf[s, h] + fac[s, h, 6:7, :] * vr[s, h].astype(F32)).astype(BF)
            sb[s, h] = low_st
            o = att[h, rs_, :] + (gin[h] * inf[s]) * dg(qkv[2, h, rs_, :], low_st, 1, 0)
            att[h, rs_, :] = o
            on = o * inverse_norm(o, HEAD_FLOOR)
            mix[rs_, rows128(h)] = (on * jax.nn.sigmoid(pg[rs_, rows128(h)])).astype(BF)
            return 0

        lax.fori_loop(0, 4, enter, 0)
        part = dg(mix[rs_, :256], wo[0], 1, 1) + dg(mix[rs_, 256:], wo[1], 1, 1)
        br_s[rs_, :] = part.astype(BF)
        b_cp.append(ln.go(br_s.at[rs_], br_r.at[rs_], "P"))
        x1[rs_, :] = xb[rs_, :].astype(F32) + part
        if s == 0:
            g_d.cross()
            g_d.step1(0)
            g_l.other()
    ln.keep(att, att_o)
    ln.keep(mix, mix_o)
    ln.keep(sb, sb_o)
    ct_cp.append(ln.go(ct.at[mine(1)], ct.at[mine(1)], "P"))
    g_r.other()
    g_d.step2(0)
    g_l.step1(1)
    g_r.step1(1)
    for g in (g_l, g_r, g_d):
        g.step3(0)
    g_l.step2(1)
    g_r.step2(1)
    d_cp = []

    def units(s, b):
        rs_ = pl.ds(s * CH, CH)
        a = dg(n2[rs_, :], gl[b], 1, 0)
        c = dg(n2[rs_, :], gr[b], 1, 0)
        hid[b, rs_, :] = (a * c).astype(BF)
        dh = dg(ct[rs_, :], gd[b], 1, 0)
        dpl[b, rs_, :] = (dh * c).astype(BF)
        dpr[b, rs_, :] = (dh * a).astype(BF)

    for s in range(2):
        rs_ = pl.ds(s * CH, CH)
        b_cp[s].wait_recv()
        v = x1[rs_, :] + br_r[rs_, :].astype(F32)
        x1[rs_, :] = v
        n2[rs_, :] = (v * inverse_norm(v, EPSILON)).astype(BF)
        if s == 0:
            g_d.other()
        ct_cp[s].wait_recv()
        units(s, own)
        if s == 0:
            g_d.step1(1)
            g_l.step3(1)
            g_r.step3(1)
            g_d.step2(1)
            g_d.step3(1)
        units(s, far_b)
        part = (
            dg(dpl[0, rs_, :], gl[0], 1, 1) + dg(dpr[0, rs_, :], gr[0], 1, 1)
            + dg(dpl[1, rs_, :], gl[1], 1, 1) + dg(dpr[1, rs_, :], gr[1], 1, 1)
        )
        dn[rs_, :] = part
        ln.gone(b_cp[s])
        br_s[rs_, :] = part.astype(BF)
        d_cp.append(ln.go(br_s.at[rs_], dn_r.at[rs_], "P"))
    ln.keep(n2, n2_o)
    ln.keep(dpr, dpr_o)

    down = Scatter(ln, "cols", down_b)
    left = Scatter(ln, "cols", left_b)
    for b in range(2):
        down.core_stage(b, lambda b, i: dg(hid[b], ct[:, cols256(i)], 0, 0))

    def turn(s):
        rs_ = pl.ds(s * CH, CH)
        d_cp[s].wait_recv()
        g = ct[rs_, :].astype(F32) + norm_slope(x1[rs_, :], dn[rs_, :] + dn_r[rs_, :].astype(F32), EPSILON)
        dn[rs_, :] = g
        dr[rs_, :] = g.astype(BF)
        ln.keep(dr.at[rs_], dr_o.at[rs_])
        ln.keep(dn.at[mine(s)], dx1_o.at[s])

    def feed(s):
        rs_ = pl.ds(s * CH, CH)
        tmp[...] = dg(hid[0, rs_, :], gd[0], 1, 1) + dg(hid[1, rs_, :], gd[1], 1, 1)
        fs[s] = tmp[rows128(1 - pc.t), :].astype(BF)
        fo[s] = x1[mine(s), :] + tmp[rows128(pc.t), :]

    feed(0)
    for b in range(2):
        down.first_stage(b)
    for b in range(2):
        left.core_stage(b, lambda b, i: dg(dpl[b], n2[:, cols256(i)], 0, 0), down)
    turn(0)
    for b in range(2):
        down.second_stage(b)
    feed(1)
    ln.keep(fs, fs_o)
    ln.keep(fo, fo_o)
    for b in range(2):
        left.join(b)
    ln.keep(left.acc, left_o)
    down.plane_stage()
    ln.keep(down.sz, dsz_o)
    gdown[...] = down.near()
    ln.keep(gdown, gdown_o)
    turn(1)
    ln.drain()


def call_forward(rate, tok, cot, seg, ws, wo, gl, gr, gd):
    sd, vm = jax.ShapeDtypeStruct, pltpu.VMEM
    ff = gl.shape[0]
    act = (512, 1024)
    st = (2, 4, DH, DH)
    outs = [
        sd((2, 128, 1024), BF), sd(act, BF), sd(act, BF), sd(act, F32), sd((512, 512), F32), sd((3, 4, 512, DH), BF),
        sd((2, 4, CH, CH), BF), sd((4, 512, DH), F32), sd((512, 512), BF), sd(st, BF),
        sd((4, 2, 1024, 256), BF), sd((2, 1024, 256), BF), sd((4, 8, 512), F32), sd((4, 8, DH), F32),
        sd(act, BF), sd((2, 128, 1024), F32), sd((2, 128, 1024), BF), sd((2, 128, 1024), F32),
        sd((2, 512, ff), BF), sd((ff, 128), F32), sd((ff, 128), BF), sd((2, 4, ff, 128), BF),
    ]
    scratch = [
        vm(act, BF), vm(act, BF), vm(act, BF), vm(act, BF), vm(act, F32), vm((512, 512), F32),
        vm((3, 4, 512, DH), BF), vm((2, 4, CH, CH), BF), vm((4, 512, DH), F32), vm((512, 512), BF),
        vm(st, BF), vm((4, 2, 1024, 256), BF), vm((2, 1024, 256), BF),
        vm((2, 1024, ff), BF), vm((2, 1024, ff), BF), vm((2, 1024, ff), BF),
        vm((4, 8, 512), F32), vm((4, 8, DH), F32), vm((2, 4, 8, DH), F32),
        vm((4, CH, CH), F32), vm((4, CH, DH), F32), vm((4, CH, DH), F32),
        vm((2, CH, CH), F32), vm((2, CH, DH), F32), vm((2, CH, DH), F32),
        vm(st, F32), vm(st, BF), vm(st, BF), vm(st, BF), vm(st, BF), vm(st, BF), vm(st, BF), vm(st, F32),
        vm(act, BF), vm(act, BF), vm(act, BF), vm(act, F32),
        vm((2, 512, ff), BF), vm((2, 512, ff), BF), vm((2, 512, ff), BF),
        vm((CH, 1024), F32), vm(act, BF), vm((2, 128, 1024), BF), vm((2, 128, 1024), F32), vm((ff, 128), F32), vm((2, 4, ff, 128), BF),
        *scatter_bufs((ff, 128), BF)[:-1], vm((2, 4, ff, 128), BF),
        pltpu.SemaphoreType.DMA((160,)), pltpu.SemaphoreType.DMA((160,)), pltpu.SemaphoreType.DMA((40,)),
    ]
    vin = pl.BlockSpec(memory_space=pltpu.VMEM)
    return pl.pallas_call(
        forward_and_glu,
        out_shape=outs,
        in_specs=[pl.BlockSpec(memory_space=pltpu.SMEM)] + [vin] * 11,
        out_specs=[pl.BlockSpec(memory_space=pl.ANY)] * len(outs),
        scratch_shapes=scratch,
        compiler_params=pltpu.CompilerParams(
            collective_id=0, has_side_effects=True, vmem_limit_bytes=63 * MIB
        ),
        name="forward_and_glu",
    )(rate, tok, cot, seg, *ws, wo, gl, gr, gd)


def silu_slope(v):
    g = jax.nn.sigmoid(v)
    return g * (1.0 + v * (1.0 - g))


N_BACK_IN = 22


def cut_bufs(refs):
    sets = []
    for n in (6, 9, 9, 9, 9, 9, 9):
        sets.append(tuple(refs[:n]))
        refs = refs[n:]
    return sets, refs


def attn_backward(*refs):
    ins, refs = refs[:N_BACK_IN], refs[N_BACK_IN:]
    outs, refs = refs[:10], refs[10:]
    bufs, refs = refs[:N_BACK_IN], refs[N_BACK_IN:]
    out_o, gtok_o, gq_o, gk_o, gv_o, gg_o, go_o, gl_o, gr_o, gd_o = outs
    (
        ids, rate, fs, left_acc, dr, wo, att, pg, qkv, n2, dpr, pm, sb, pkq, dsz, mix, n1, wb, fo, dx1, x, dnear
    ) = bufs
    (
        fac, grid, wend, gin, mask, endf, inf, dm, dob, dp, vf, vs, vr, ts, tr, ws, wr, rf, du,
        tmp, nsend, nrecv, frecv, drz, gtok, gw, gout, gleft, gright,
    ) = refs[:29]
    refs = refs[29:]
    sc_bufs, refs = cut_bufs(refs)
    send, recv, local = refs
    pc = Place()
    pc.greet()
    ln = Links(pc, send, recv, local)
    got = [ln.fetch(a, b) for a, b in zip(ins, bufs)]

    def ready(n):
        while len(got) > N_BACK_IN - n:
            got.pop(0).wait()

    pc.meet()
    left = Scatter(ln, "cols", (left_acc, None, None) + sc_bufs[0])
    right = Scatter(ln, "cols", sc_bufs[1])
    s_out = Scatter(ln, "cols", sc_bufs[2])
    s_w = [Scatter(ln, "rows", sc_bufs[3 + i]) for i in range(4)]
    ready(3)
    f_cp = ln.go(fs, frecv, "P")
    fill_decay(rate, grid, wend, gin)
    fill_masks(pc, ids, mask, endf, inf)
    backward_factors(pc, ids, rate, fac)
    ready(4)
    for b in range(2):
        left.first_stage(b, True)
    ready(6)

    def mine(s):
        return pl.ds(pl.multiple_of(s * CH + pc.t * 128, 128), 128)

    def through(b, _):
        dm[:, cols256(b)] = dg(dr[...], wo[b], 1, 0)
        return 0

    lax.fori_loop(0, 2, through, 0)
    ready(9)
    v_cp = []
    for s in range(2):
        rs_ = pl.ds(s * CH, CH)

        def outer(h, _):
            d, o = dm[rs_, rows128(h)], att[h, rs_, :]
            g = jax.nn.sigmoid(pg[rs_, rows128(h)])
            inv = inverse_norm(o, HEAD_FLOOR)
            dp[3, rs_, rows128(h)] = (d * (o * inv) * g * (1.0 - g)).astype(BF)
            e = d * g
            inner = jnp.mean(e * o, axis=-1, keepdims=True)
            do = (inv * (e - o * (inner * inv * inv))).astype(BF)
            dob[h, rs_, :] = do
            gq = (qkv[2, h, rs_, :].astype(F32) * (gin[h] * inf[s])).astype(BF)
            v = dg(gq, do, 0, 0)
            vf[s, h] = v
            vs[s, h] = v.astype(BF)
            return 0

        lax.fori_loop(0, 4, outer, 0)
        v_cp.append(ln.go(vs.at[s], vr.at[s], "Q"))

    def product(i):
        return lambda b, j: dg(n1[:, cols256(j)], dp[i, :, cols256(b)], 0, 0)

    ready(11)
    for b in range(2):
        right.core_stage(b, lambda b, i: dg(dpr[b], n2[:, cols256(i)], 0, 0))
    for b in range(2):
        left.second_stage(b)
    ready(15)
    z_cp = ln.go(dsz, drz, "Q")
    for b in range(2):
        right.first_stage(b)

    def inner(s):
        rs_ = pl.ds(s * CH, CH)

        def inside(h, _):
            do, q, k = dob[h, rs_, :], qkv[2, h, rs_, :], qkv[0, h, rs_, :]
            dsc = (dg(do, qkv[1, h, rs_, :], 1, 1) * grid[h] * mask[s]).astype(BF)
            dq = dg(dsc, k, 1, 0) + (gin[h] * inf[s]) * dg(do, sb[s, h], 1, 1)
            dp[2, rs_, rows128(h)] = (dq * silu_slope(pkq[rs_, rows128(4 + h)])).astype(BF)
            dm[rs_, rows128(h)] = dg(dsc, q, 0, 0)
            att[h, rs_, :] = dg(pm[s, h], do, 0, 0)
            return 0

        lax.fori_loop(0, 4, inside, 0)

    def pair_up(s):
        v_cp[s].wait_recv()
        pair_sum(fac, s, vf, vr, ts, rf)
        return ln.go(ts.at[s], tr.at[s], "C")

    def quad_up(s):
        t_cp[s].wait_recv()
        quad_sum(fac, s, vf, tr, ws, rf)
        return ln.go(ws.at[s], wr.at[s], "Y")

    def close_up(s):
        w_cp[s].wait_recv()
        rs_ = pl.ds(s * CH, CH)

        def close(h, _):
            d = (rf[s, h] + fac[s, h, 6:7, :] * wr[s, h].astype(F32)).astype(BF)
            k, v = qkv[0, h, rs_, :], qkv[1, h, rs_, :]
            w = wend[h] * endf[s]
            kw = (k.astype(F32) * w).astype(BF)
            dp[1, rs_, rows128(h)] = (att[h, rs_, :] + dg(kw, d, 1, 0)).astype(BF)
            dk = dm[rs_, rows128(h)] + w * dg(v, d, 1, 1)
            dp[0, rs_, rows128(h)] = (dk * silu_slope(pkq[rs_, rows128(h)])).astype(BF)
            return 0

        lax.fori_loop(0, 4, close, 0)

    def through_weights(s):
        rs_ = pl.ds(s * CH, CH)
        acc = None
        for i in range(4):
            for b in range(2):
                p = dg(dp[i, rs_, b * 256 : (b + 1) * 256], wb[i, b], 1, 1)
                acc = p if acc is None else acc + p
        tmp[...] = acc
        nsend[s] = tmp[rows128(1 - pc.t), :].astype(BF)
        gtok[s] = tmp[rows128(pc.t), :]
        return ln.go(nsend.at[s], nrecv.at[s], "P")

    def out_core(b):
        s_out.core_stage(b, lambda b, i: dg(mix[:, cols256(b)], dr[:, cols256(i)], 0, 0))

    inner(0)
    t_cp = [pair_up(0)]
    t_cp.append(pair_up(1))
    ready(17)
    for b in range(2):
        out_core(b)
    w_cp = [quad_up(0), quad_up(1)]
    inner(1)
    for b in range(2):
        right.second_stage(b)
    for b in range(2):
        s_out.first_stage(b)
    left.plane_stage()
    for b in range(2):
        s_w[3].core_stage(b, product(3))
    ready(22)
    close_up(0)
    close_up(1)
    for b in range(2):
        s_w[3].first_stage(b)
    for i in (0, 1):
        for b in range(2):
            s_w[i].core_stage(b, product(i))
    for b in range(2):
        s_out.second_stage(b)
    right.plane_stage()
    n_cp = [through_weights(0)]
    for i in (0, 1):
        for b in range(2):
            s_w[i].first_stage(b)
    for b in range(2):
        s_w[3].second_stage(b)
    n_cp.append(through_weights(1))
    for b in range(2):
        s_w[2].core_stage(b, product(2))
    for i in (0, 1):
        for b in range(2):
            s_w[i].second_stage(b)
    s_out.plane_stage()
    s_w[3].plane_stage()
    for b in range(2):
        s_w[2].first_stage(b)
    for i in (0, 1):
        s_w[i].plane_stage()
    for b in range(2):
        s_w[2].second_stage(b)
    s_w[2].plane_stage()
    f_cp.wait_recv()
    frecv[...] = (fo[...] + frecv[...].astype(F32)).astype(BF)
    ln.keep(frecv, out_o)
    for s in range(2):
        n_cp[s].wait_recv()
        dn = gtok[s] + nrecv[s].astype(F32)
        gtok[s] = dx1[s] + norm_slope(x[s].astype(F32), dn, EPSILON)
    ln.keep(gtok, gtok_o)
    z_cp.wait_recv()
    dnear[...] = dnear[...] + drz[...].astype(F32)
    ln.keep(dnear, gd_o)
    gleft[...] = left.total()
    ln.keep(gleft, gl_o)
    gright[...] = right.total()
    ln.keep(gright, gr_o)
    gout[...] = s_out.total()
    ln.keep(gout, go_o)
    for i, o in ((3, gg_o), (2, gq_o), (0, gk_o), (1, gv_o)):
        gw[i] = s_w[i].total()
        ln.keep(gw.at[i], o)
    ln.drain()


def call_backward(*args):
    sd, vm = jax.ShapeDtypeStruct, pltpu.VMEM
    ff = args[10].shape[2]
    outs = [
        sd((2, 128, 1024), BF), sd((2, 128, 1024), F32),
        sd((128, 256), F32), sd((128, 256), F32), sd((128, 256), F32), sd((128, 256), F32),
        sd((256, 128), F32), sd((ff, 128), F32), sd((ff, 128), F32), sd((ff, 128), F32),
    ]
    st = (2, 4, DH, DH)
    scratch = [vm(a.shape, a.dtype) for a in args] + [
        vm((2, 4, 8, DH), F32), vm((4, CH, CH), F32), vm((4, CH, DH), F32), vm((4, CH, DH), F32),
        vm((2, CH, CH), F32), vm((2, CH, DH), F32), vm((2, CH, DH), F32),
        vm((512, 512), F32), vm((4, 512, DH), BF), vm((4, 512, 512), BF),
        vm(st, F32), vm(st, BF), vm(st, BF), vm(st, BF), vm(st, BF), vm(st, BF), vm(st, BF),
        vm(st, F32), vm((8, 128), BF),
        vm((CH, 1024), F32), vm((2, 128, 1024), BF), vm((2, 128, 1024), BF), vm((2, 128, 1024), BF),
        vm((ff, 128), BF), vm((2, 128, 1024), F32), vm((4, 128, 256), F32),
        vm((256, 128), F32), vm((ff, 128), F32), vm((ff, 128), F32),
        *scatter_bufs((ff, 128), BF, 0)[1:], *scatter_bufs((ff, 128), BF),
        *scatter_bufs((256, 128)), *scatter_bufs((128, 256)), *scatter_bufs((128, 256)),
        *scatter_bufs((128, 256)), *scatter_bufs((128, 256)),
        pltpu.SemaphoreType.DMA((64,)), pltpu.SemaphoreType.DMA((64,)), pltpu.SemaphoreType.DMA((40,)),
    ]
    return pl.pallas_call(
        attn_backward,
        out_shape=outs,
        in_specs=[pl.BlockSpec(memory_space=pl.ANY)] * len(args),
        out_specs=[pl.BlockSpec(memory_space=pl.ANY)] * len(outs),
        scratch_shapes=scratch,
        compiler_params=pltpu.CompilerParams(
            collective_id=2, has_side_effects=True, vmem_limit_bytes=63 * MIB
        ),
        name="attention_backward",
    )(*args)


def entering(x, axis, join, neutral):
    place = lax.axis_index(axis)
    gathered = jax.tree.map(
        lambda a, kind: lax.all_gather(a.astype(kind), axis),
        x,
        (jnp.bfloat16, jnp.bfloat16, jnp.bfloat16, jnp.bfloat16),
    )
    state = jax.tree.map(lambda a, e: jnp.zeros_like(a) + jnp.asarray(e, a.dtype), x, neutral)

    def one(lap, state):
        return join(
            state,
            jax.tree.map(
                lambda a, own: lax.dynamic_index_in_dim(a, lap, 0, False).astype(own.dtype),
                gathered,
                x,
            ),
        )

    return lax.fori_loop(0, place, one, state)


def entering_2(x, axis, join, neutral):
    count = lax.axis_size(axis)
    place = lax.axis_index(axis)
    ahead = count - 1 - place
    gathered = jax.tree.map(
        lambda a, kind: lax.all_gather(a.astype(kind), axis), x, (jnp.bfloat16, jnp.bfloat16)
    )
    state = jax.tree.map(lambda a, e: jnp.zeros_like(a) + jnp.asarray(e, a.dtype), x, neutral)

    def one(lap, state):
        source = count - 1 - lap
        return join(
            state,
            jax.tree.map(
                lambda a, own: lax.dynamic_index_in_dim(a, source, 0, False).astype(own.dtype),
                gathered,
                x,
            ),
        )

    return lax.fori_loop(0, ahead, one, state)


def normalize(values, floor_value=EPSILON):
    return values * lax.rsqrt(jnp.mean(values * values, axis=-1, keepdims=True) + floor_value)


def norm_backward(values, upstream, floor_value=EPSILON):
    inverse = lax.rsqrt(jnp.mean(values * values, axis=-1, keepdims=True) + floor_value)
    inner_mean = jnp.mean(upstream * values, axis=-1, keepdims=True)
    return inverse * (upstream - values * inner_mean * inverse * inverse)


def silu_grad(values):
    sigmoid_value = jax.nn.sigmoid(values)
    return sigmoid_value * (1.0 + values * (1.0 - sigmoid_value))


def chain_forward(earlier, later):
    early_first, early_last, early_decay, early_state = earlier
    late_first, late_last, late_decay, late_state = later
    linked = (late_first == early_last) | (early_last < 0.0) | (late_first < 0.0)
    carried = jnp.where(linked[:, None], late_decay, 0.0)
    first_seg = jnp.where(early_first < 0.0, late_first, early_first)
    last_seg = jnp.where(late_last < 0.0, early_last, late_last)
    return (
        first_seg,
        last_seg,
        early_decay * carried,
        late_state + carried[:, :, None, None] * early_state,
    )


def chain_backward(earlier, later):
    return (earlier[0] * later[0], later[1] + later[0][:, :, None, None] * earlier[1])


def shards(
    tokens,
    segment_ids,
    decay_rate,
    w_query,
    w_key,
    w_value,
    w_gate,
    w_out,
    glu_left,
    glu_right,
    glu_down,
    cotangent,
):
    shard_len, seq_count, model_width = tokens.shape
    tok_float = tokens.astype(jnp.float32)
    normed_part = normalize(tok_float).astype(jnp.bfloat16)
    gathered = (
        lax.all_gather(w_query.astype(jnp.bfloat16), ("fsdp", "ctx"), axis=0, tiled=True),
        lax.all_gather(w_key.astype(jnp.bfloat16), ("fsdp", "ctx"), axis=0, tiled=True),
        lax.all_gather(w_value.astype(jnp.bfloat16), ("fsdp", "ctx"), axis=0, tiled=True),
        lax.all_gather(w_gate.astype(jnp.bfloat16), ("fsdp", "ctx"), axis=0, tiled=True),
        lax.all_gather(w_out.astype(jnp.bfloat16), ("fsdp", "ctx"), axis=1, tiled=True),
        lax.all_gather(glu_left.astype(jnp.bfloat16), ("fsdp", "ctx"), axis=0, tiled=True),
        lax.all_gather(glu_right.astype(jnp.bfloat16), ("fsdp", "ctx"), axis=0, tiled=True),
        lax.all_gather(glu_down.astype(jnp.bfloat16), ("fsdp", "ctx"), axis=1, tiled=True),
    )
    full_query, full_key, full_value, full_gate, full_out, full_left, full_right, full_down = (
        gathered
    )
    normed = lax.all_gather(normed_part, "tp", axis=0, tiled=True)
    block_len = normed.shape[0]
    total_rows = block_len * seq_count
    normed_flat = normed.reshape(total_rows, model_width)
    local_width = full_query.shape[1]
    head_count = local_width // DH
    head_shape = (block_len, seq_count, head_count, DH)
    proj_query = jnp.dot(normed_flat, full_query, preferred_element_type=jnp.float32)
    proj_key = jnp.dot(normed_flat, full_key, preferred_element_type=jnp.float32)
    proj_value = jnp.dot(normed_flat, full_value, preferred_element_type=jnp.float32)
    proj_gate = jnp.dot(normed_flat, full_gate, preferred_element_type=jnp.float32)
    queries = jax.nn.silu(proj_query).astype(jnp.bfloat16).reshape(head_shape)
    keys_low = jax.nn.silu(proj_key).astype(jnp.bfloat16).reshape(head_shape)
    values_low = proj_value.astype(jnp.bfloat16).reshape(head_shape)
    seg_pos = segment_ids.T
    seg_float = seg_pos.astype(jnp.float32)
    position = jnp.arange(block_len).astype(jnp.float32)
    distance = position[:, None] - position[None, :]
    same_doc = (segment_ids[:, :, None] == segment_ids[:, None, :]) & (distance >= 0.0)[None]
    decay_grid = jnp.where(
        same_doc[:, None],
        jnp.exp(-decay_rate[None, :, None, None] * jnp.maximum(distance, 0.0)[None, None]),
        0.0,
    )
    end_weight = jnp.where(
        (seg_pos == seg_pos[-1:])[:, :, None],
        jnp.exp(-(block_len - 1.0 - position)[:, None, None] * decay_rate[None, None, :]),
        0.0,
    )
    keys_end = (keys_low.astype(jnp.float32) * end_weight[..., None]).astype(jnp.bfloat16)
    update = jnp.einsum("tbhd,tbhe->bhde", keys_end, values_low, preferred_element_type=jnp.float32)
    first_seg = seg_float[0]
    last_seg = seg_float[-1]
    span_decay = jnp.where(
        (first_seg == last_seg)[:, None], jnp.exp(-block_len * decay_rate)[None, :], 0.0
    )
    identity = (
        -jnp.ones((seq_count,), jnp.float32),
        -jnp.ones((seq_count,), jnp.float32),
        jnp.ones((seq_count, head_count), jnp.float32),
        jnp.zeros((seq_count, head_count, DH, DH), jnp.float32),
    )
    scanned = entering((first_seg, last_seg, span_decay, update), "ctx", chain_forward, identity)
    prior_last = scanned[1]
    state_low = scanned[3].astype(jnp.bfloat16)
    inflow = jnp.where(
        (seg_pos == prior_last[None, :])[:, :, None],
        jnp.exp(-(position + 1.0)[:, None, None] * decay_rate[None, None, :]),
        0.0,
    )
    scores = jnp.einsum("tbhd,sbhd->bhts", queries, keys_low, preferred_element_type=jnp.float32)
    weights_low = (scores * decay_grid).astype(jnp.bfloat16)
    intra = jnp.einsum(
        "bhts,sbhd->tbhd", weights_low, values_low, preferred_element_type=jnp.float32
    )
    inter = (
        jnp.einsum("tbhd,bhde->tbhe", queries, state_low, preferred_element_type=jnp.float32)
        * inflow[..., None]
    )
    attended = intra + inter
    attended_norm = normalize(attended, HEAD_FLOOR)
    gate_value = jax.nn.sigmoid(proj_gate).reshape(head_shape)
    mixed_heads = (
        (attended_norm * gate_value).astype(jnp.bfloat16).reshape(block_len, seq_count, local_width)
    )
    row_count = shard_len * lax.axis_size("tp")
    piece_rows = mixed_heads.reshape(row_count * seq_count, local_width)
    branch = lax.psum_scatter(
        jnp.dot(piece_rows, full_out, preferred_element_type=jnp.float32).reshape(
            row_count, seq_count, model_width
        ),
        "tp",
        scatter_dimension=0,
        tiled=True,
    )
    residual = tok_float + branch
    second_part = normalize(residual).astype(jnp.bfloat16)
    second = lax.all_gather(second_part, "tp", axis=0, tiled=True)
    second_flat = second.reshape(total_rows, model_width)
    left_proj = jnp.dot(second_flat, full_left, preferred_element_type=jnp.float32)
    right_proj = jnp.dot(second_flat, full_right, preferred_element_type=jnp.float32)
    hidden = (left_proj * right_proj).astype(jnp.bfloat16)
    ffn_width = hidden.shape[1]
    hidden_blocks = hidden.reshape(block_len, seq_count, ffn_width)
    row_count = shard_len * lax.axis_size("tp")
    piece_rows = hidden_blocks.reshape(row_count * seq_count, ffn_width)
    ffn_branch = lax.psum_scatter(
        jnp.dot(piece_rows, full_down, preferred_element_type=jnp.float32)
        .reshape(row_count, seq_count, model_width)
        .astype(jnp.bfloat16),
        "tp",
        scatter_dimension=0,
        tiled=True,
    ).astype(jnp.float32)
    output = (residual + ffn_branch).astype(jnp.bfloat16)
    upstream = lax.all_gather(cotangent, "tp", axis=0, tiled=True).reshape(total_rows, model_width)
    grad_down = jnp.dot(hidden.T, upstream, preferred_element_type=jnp.float32)
    grad_hidden = jnp.dot(upstream, full_down.T, preferred_element_type=jnp.float32)
    grad_left_proj = (grad_hidden * right_proj).astype(jnp.bfloat16)
    grad_right_proj = (grad_hidden * left_proj).astype(jnp.bfloat16)
    grad_left = jnp.dot(second_flat.T, grad_left_proj, preferred_element_type=jnp.float32)
    grad_right = jnp.dot(second_flat.T, grad_right_proj, preferred_element_type=jnp.float32)
    left_blocks = grad_left_proj.reshape(block_len, seq_count, ffn_width)
    right_blocks = grad_right_proj.reshape(block_len, seq_count, ffn_width)
    row_count = shard_len * lax.axis_size("tp")
    left_rows = left_blocks.reshape(row_count * seq_count, ffn_width)
    right_rows = right_blocks.reshape(row_count * seq_count, ffn_width)
    summed = jnp.dot(left_rows, full_left.T, preferred_element_type=jnp.float32) + jnp.dot(
        right_rows, full_right.T, preferred_element_type=jnp.float32
    )
    grad_second = lax.psum_scatter(
        summed.reshape(row_count, seq_count, model_width), "tp", scatter_dimension=0, tiled=True
    )
    grad_residual = cotangent.astype(jnp.float32) + norm_backward(residual, grad_second)
    branch_low = grad_residual.astype(jnp.bfloat16)
    grad_branch = lax.all_gather(branch_low, "tp", axis=0, tiled=True).reshape(
        total_rows, model_width
    )
    grad_wout = jnp.dot(
        mixed_heads.reshape(total_rows, local_width).T,
        grad_branch,
        preferred_element_type=jnp.float32,
    )
    grad_mixed = jnp.dot(grad_branch, full_out.T, preferred_element_type=jnp.float32).reshape(
        head_shape
    )
    grad_gate_proj = (
        (grad_mixed * attended_norm * gate_value * (1.0 - gate_value))
        .astype(jnp.bfloat16)
        .reshape(total_rows, local_width)
    )
    grad_attended = norm_backward(attended, grad_mixed * gate_value, HEAD_FLOOR).astype(
        jnp.bfloat16
    )
    grad_weights = jnp.einsum(
        "tbhd,sbhd->bhts", grad_attended, values_low, preferred_element_type=jnp.float32
    )
    grad_scores = (grad_weights * decay_grid).astype(jnp.bfloat16)
    grad_queries = jnp.einsum(
        "bhts,sbhd->tbhd", grad_scores, keys_low, preferred_element_type=jnp.float32
    )
    grad_queries = (
        grad_queries
        + jnp.einsum(
            "tbhe,bhde->tbhd", grad_attended, state_low, preferred_element_type=jnp.float32
        )
        * inflow[..., None]
    )
    grad_keys = jnp.einsum(
        "bhts,tbhd->sbhd", grad_scores, queries, preferred_element_type=jnp.float32
    )
    grad_values = jnp.einsum(
        "bhts,tbhd->sbhd", weights_low, grad_attended, preferred_element_type=jnp.float32
    )
    weighted_queries = queries.astype(jnp.float32) * inflow[..., None]
    grad_prior_local = jnp.einsum(
        "tbhd,tbhe->bhde", weighted_queries, grad_attended.astype(jnp.float32), precision=lax.Precision.HIGHEST
    )
    link_decay = jnp.where((first_seg == prior_last)[:, None], span_decay, 0.0)
    back_identity = (
        jnp.ones((seq_count, head_count), jnp.float32),
        jnp.zeros((seq_count, head_count, DH, DH), jnp.float32),
    )
    grad_update = entering_2((link_decay, grad_prior_local), "ctx", chain_backward, back_identity)[
        1
    ]
    grad_values = grad_values + jnp.einsum(
        "tbhd,bhde->tbhe", keys_end.astype(jnp.float32), grad_update, precision=lax.Precision.HIGHEST
    )
    grad_keys = (
        grad_keys
        + jnp.einsum(
            "tbhe,bhde->tbhd", values_low.astype(jnp.float32), grad_update, precision=lax.Precision.HIGHEST
        )
        * end_weight[..., None]
    )
    grad_query_proj = (
        (grad_queries * silu_grad(proj_query).reshape(head_shape))
        .astype(jnp.bfloat16)
        .reshape(total_rows, local_width)
    )
    grad_key_proj = (
        (grad_keys * silu_grad(proj_key).reshape(head_shape))
        .astype(jnp.bfloat16)
        .reshape(total_rows, local_width)
    )
    grad_value_proj = grad_values.astype(jnp.bfloat16).reshape(total_rows, local_width)
    grad_wquery = jnp.dot(normed_flat.T, grad_query_proj, preferred_element_type=jnp.float32)
    grad_wkey = jnp.dot(normed_flat.T, grad_key_proj, preferred_element_type=jnp.float32)
    grad_wvalue = jnp.dot(normed_flat.T, grad_value_proj, preferred_element_type=jnp.float32)
    grad_wgate = jnp.dot(normed_flat.T, grad_gate_proj, preferred_element_type=jnp.float32)
    query_blocks = grad_query_proj.reshape(block_len, seq_count, local_width)
    key_blocks = grad_key_proj.reshape(block_len, seq_count, local_width)
    value_blocks = grad_value_proj.reshape(block_len, seq_count, local_width)
    gate_blocks = grad_gate_proj.reshape(block_len, seq_count, local_width)
    row_count = shard_len * lax.axis_size("tp")
    summed = jnp.zeros((row_count * seq_count, model_width), jnp.float32)
    for grad_blocks, weight_full in (
        (query_blocks, full_query),
        (key_blocks, full_key),
        (value_blocks, full_value),
        (gate_blocks, full_gate),
    ):
        piece_rows = grad_blocks.reshape(row_count * seq_count, local_width)
        summed = summed + jnp.dot(piece_rows, weight_full.T, preferred_element_type=jnp.float32)
    grad_normed = lax.psum_scatter(
        summed.reshape(row_count, seq_count, model_width).astype(jnp.bfloat16),
        "tp",
        scatter_dimension=0,
        tiled=True,
    ).astype(jnp.float32)
    grad_tokens = grad_residual + norm_backward(tok_float, grad_normed)
    every_grad = (
        lax.psum_scatter(grad_wquery, ("fsdp", "ctx"), scatter_dimension=0, tiled=True),
        lax.psum_scatter(grad_wkey, ("fsdp", "ctx"), scatter_dimension=0, tiled=True),
        lax.psum_scatter(grad_wvalue, ("fsdp", "ctx"), scatter_dimension=0, tiled=True),
        lax.psum_scatter(grad_wgate, ("fsdp", "ctx"), scatter_dimension=0, tiled=True),
        lax.psum_scatter(grad_wout, ("fsdp", "ctx"), scatter_dimension=1, tiled=True),
        lax.psum_scatter(grad_left, ("fsdp", "ctx"), scatter_dimension=0, tiled=True),
        lax.psum_scatter(grad_right, ("fsdp", "ctx"), scatter_dimension=0, tiled=True),
        lax.psum_scatter(grad_down, ("fsdp", "ctx"), scatter_dimension=1, tiled=True),
    )
    return (
        output,
        grad_tokens,
        every_grad[0],
        every_grad[1],
        every_grad[2],
        every_grad[3],
        every_grad[4],
        every_grad[5],
        every_grad[6],
        every_grad[7],
    )


def paired(
    tokens, segment_ids, decay_rate, w_query, w_key, w_value, w_gate, w_out,
    glu_left, glu_right, glu_down, cotangent,
):
    (
        own_rows, n1, n2, pkq, pg, qkv, pm, att, mix, sb, wb, wo, ids, rate,
        dr, dx1, fs, fo, dpr, dnear, dsz, left_acc,
    ) = call_forward(
        decay_rate, tokens, cotangent, segment_ids, (w_query, w_key, w_value, w_gate), w_out,
        glu_left.T, glu_right.T, glu_down,
    )
    out, g_tok, g_q, g_k, g_v, g_g, g_o, g_left, g_right, g_down = call_backward(
        ids, rate, fs, left_acc, dr, wo, att, pg, qkv, n2, dpr, pm, sb, pkq, dsz, mix, n1, wb, fo, dx1, own_rows,
        dnear,
    )
    return (
        out.transpose(1, 0, 2), g_tok.transpose(1, 0, 2),
        g_q, g_k, g_v, g_g, g_o, g_left.T, g_right.T, g_down,
    )


def solution(mesh):
    in_specs = (
        P(("ctx", "tp"), "fsdp", None),
        P("fsdp", "ctx"),
        P("tp"),
        P(("fsdp", "ctx"), "tp"),
        P(("fsdp", "ctx"), "tp"),
        P(("fsdp", "ctx"), "tp"),
        P(("fsdp", "ctx"), "tp"),
        P("tp", ("fsdp", "ctx")),
        P(("fsdp", "ctx"), "tp"),
        P(("fsdp", "ctx"), "tp"),
        P("tp", ("fsdp", "ctx")),
        P(("ctx", "tp"), "fsdp", None),
    )
    out_specs = (
        P(("ctx", "tp"), "fsdp", None),
        P(("ctx", "tp"), "fsdp", None),
        P(("fsdp", "ctx"), "tp"),
        P(("fsdp", "ctx"), "tp"),
        P(("fsdp", "ctx"), "tp"),
        P(("fsdp", "ctx"), "tp"),
        P("tp", ("fsdp", "ctx")),
        P(("fsdp", "ctx"), "tp"),
        P(("fsdp", "ctx"), "tp"),
        P("tp", ("fsdp", "ctx")),
    )
    sizes = tuple(mesh.shape[a] for a in ("fsdp", "ctx", "tp"))
    body = paired if sizes == (2, 4, 4) else shards
    return jax.shard_map(body, mesh=mesh, in_specs=in_specs, out_specs=out_specs, check_vma=False)
```
